32 devices in a mesh: wide: 16 (over z, x, core), narrow: 2 (over y).
Axes of the slice: x: 2, y: 2, z: 4, core: 2. Of those that a mesh axis runs over, the one named last changes fastest.
Arguments:
- object_field: float32 [2, 4096, 1024], P(None, 'wide', 'narrow'), may hold values from -1 to 1
- probe: float32 [2, 256, 256], replicated, may hold values from -6 to 6
- intensity: float32 [16, 2, 8, 256, 256], P('wide', 'narrow'), may hold values from 0.05 to 4
- row_offsets: int32 [16, 2, 8], P('wide', 'narrow'), may hold values from 0 to 255
- col_offsets: int32 [16, 2, 8], P('wide', 'narrow'), may hold values from 0 to 511
- counts: int32 [16, 2], P('wide', 'narrow'), may hold values from 2 to 8, as said below
Outputs:
- new_object: float32 [2, 4096, 1024], P(None, 'wide', 'narrow')
- new_probe: float32 [2, 256, 256], replicated
The draws below stay inside these ranges and needn't reach their ends.
Inputs may be any that keep to these rules, and one draw needn't show every extreme that they name: `counts`: the number of live slots of each tile; slots at or beyond it hold offsets and intensities that are not used; some tile has exactly 8, some exactly 2.
All inputs are finite; a program needn't handle non-finite values.
Results may differ from the reference program's by a relative error of at most 0.0003.
Values sent between devices are 32-bit elements; how exact they have to be, the bound alone decides.
No kernel may reach another device: no remote copies, remote signals or barrier semaphores. Data moves between devices by JAX's collectives and lax.ppermute only.
A program may use at most 64 MiB of HBM per device.

```python
import math
import jax
import jax.numpy as jnp
from jax import lax

PR = 256
H = 128
TR = 256
TC = 512
CAP = 8
NY = 4096
NX = 1024
N_WIDE = 16
N_NARROW = 2


def draw_counts(key, part):
    key_values, key_pick = jax.random.split(key)
    tiles = N_WIDE * N_NARROW
    spread_counts = jax.random.randint(key_values, (tiles,), 2, CAP + 1)
    busiest = jax.random.randint(key_pick, (), 0, tiles)
    positions = lax.iota(jnp.int32, tiles)
    spread_counts = jnp.where(positions == busiest, CAP, spread_counts)
    spread_counts = jnp.where(positions == (busiest + 1) % tiles, 2, spread_counts)
    return spread_counts.reshape(N_WIDE, N_NARROW).astype(jnp.int32)


def place_ends(entries, rng, smallest, high):
    longest = entries.shape.index(max(entries.shape))
    spots = []
    for shift in (0, 1):
        where = [jax.random.randint(jax.random.fold_in(rng, axis), (), 0, length) for axis, length in enumerate(entries.shape)]
        where[longest] = (where[longest] + shift) % entries.shape[longest]
        spots.append(tuple(where))
    return entries.at[spots[0]].set(smallest).at[spots[1]].set(high)


def block_levels(stream_key, dims, cuts, least, high):
    def one(dim, blocks):
        heights = jax.random.uniform(jax.random.fold_in(jax.random.fold_in(stream_key, 6), dim), (blocks,), jnp.float32, least / len(cuts), high / len(cuts))
        return jnp.repeat(jnp.exp(heights), dims[dim] // blocks).reshape((-1,) + (1,) * (len(dims) - dim - 1))

    loudness = one(*cuts[0])
    for cut in cuts[1:]:
        loudness = loudness * one(*cut)
    return loudness


def bell_draw(own_key, shape, scale, limit, dtype=jnp.bfloat16):
    values = jax.random.normal(own_key, shape, jnp.float32) * scale
    return jnp.minimum(jnp.maximum(values, -limit), limit).astype(dtype)


def setup_inputs(seed: int = 0) -> dict:
    keys = jax.random.split(jax.random.key(seed), 7)
    object_field = jnp.clip(jax.random.uniform(keys[0], (2, NY, NX), jnp.float32, -1.0, 1.0) * block_levels(keys[0], (2, NY, NX), ((1, 16), (2, 2)), -0.4, 0.0), -1.0, 1.0)
    probe = bell_draw(keys[1], (2, PR, PR), 1.0, 6.0, jnp.float32)
    intensity = jnp.clip(jnp.exp(math.log(4.0) - 4.3820266 * jax.random.uniform(keys[2], (N_WIDE, N_NARROW, CAP, PR, PR), jnp.float32) ** block_levels(keys[2], (N_WIDE, N_NARROW, CAP, PR, PR), ((0, 16), (1, 2)), -0.2, 0.2)), 0.05, 4.0)
    row_offsets = place_ends(jax.random.randint(keys[3], (N_WIDE, N_NARROW, CAP), 0, TR), jax.random.fold_in(keys[3], 1), 0, TR - 1).astype(jnp.int32)
    col_offsets = place_ends(jax.random.randint(keys[4], (N_WIDE, N_NARROW, CAP), 0, TC), jax.random.fold_in(keys[4], 1), 0, TC - 1).astype(jnp.int32)
    counts = draw_counts(jax.random.fold_in(keys[6], 71), 0)
    return {"object_field": object_field, "probe": probe, "intensity": intensity, "row_offsets": row_offsets, "col_offsets": col_offsets, "counts": counts}


mix_object = 0.5
mix_probe = 0.5

def dft_tables(length):
    indices = lax.iota(jnp.int32, length)
    product = indices[:, None] * indices[None, :] % length
    angles = product.astype(jnp.float32) * (2.0 * math.pi / length)
    norm_scale = 1.0 / math.sqrt(length)
    return (jnp.cos(angles) * norm_scale, -jnp.sin(angles) * norm_scale)

def dot_high(left_matrix, right_matrix):
    return jnp.dot(left_matrix, right_matrix, preferred_element_type=jnp.float32, precision=lax.Precision.HIGHEST)

def complex_product(left_real, left_imag, right_real, right_imag):
    out_real = dot_high(left_real, right_real) - dot_high(left_imag, right_imag)
    out_imag = dot_high(left_real, right_imag) + dot_high(left_imag, right_real)
    return (out_real, out_imag)

def exit_difference(probe, patch, measured, cos_table, sin_table):
    exit_real = probe[0] * patch[0] - probe[1] * patch[1]
    exit_imag = probe[0] * patch[1] + probe[1] * patch[0]
    half_real, half_imag = complex_product(cos_table, sin_table, exit_real, exit_imag)
    far_real, far_imag = complex_product(half_real, half_imag, cos_table, sin_table)
    factor = jnp.sqrt(measured) / jnp.sqrt(far_real * far_real + far_imag * far_imag + 1.0)
    proj_real = far_real * factor
    proj_imag = far_imag * factor
    back_half_real, back_half_imag = complex_product(cos_table, -sin_table, proj_real, proj_imag)
    back_real, back_imag = complex_product(back_half_real, back_half_imag, cos_table, -sin_table)
    return (back_real - exit_real, back_imag - exit_imag)

def reference(object_field, probe, intensity, row_offsets, col_offsets, counts):
    padded = jnp.pad(object_field, ((0, 0), (H, H), (H, H)))
    cos_table, sin_table = dft_tables(PR)
    row_base = (lax.iota(jnp.int32, N_WIDE) * TR)[:, None, None]
    col_base = (lax.iota(jnp.int32, N_NARROW) * TC)[None, :, None]
    flat_rows = (row_offsets + row_base).reshape(-1).astype(jnp.int32)
    flat_cols = (col_offsets + col_base).reshape(-1).astype(jnp.int32)
    alive_slots = (lax.iota(jnp.int32, CAP)[None, None, :] < counts[:, :, None]).reshape(-1)
    measures = intensity.reshape(N_WIDE * N_NARROW * CAP, PR, PR)
    power = probe[0] * probe[0] + probe[1] * probe[1]

    def work(totals, row_start, col_start, measured):
        grad_pad, cover_pad, probe_grad, probe_weight = totals
        zero_index = row_start * 0
        patch = lax.dynamic_slice(padded, (zero_index, row_start, col_start), (2, PR, PR))
        diff_real, diff_imag = exit_difference(probe, patch, measured, cos_table, sin_table)
        object_real = probe[0] * diff_real + probe[1] * diff_imag
        object_imag = probe[0] * diff_imag - probe[1] * diff_real
        old_grad = lax.dynamic_slice(grad_pad, (zero_index, row_start, col_start), (2, PR, PR))
        grad_pad = lax.dynamic_update_slice(grad_pad, old_grad + jnp.stack([object_real, object_imag]), (zero_index, row_start, col_start))
        old_cover = lax.dynamic_slice(cover_pad, (row_start, col_start), (PR, PR))
        cover_pad = lax.dynamic_update_slice(cover_pad, old_cover + power, (row_start, col_start))
        grad_real = patch[0] * diff_real + patch[1] * diff_imag
        grad_imag = patch[0] * diff_imag - patch[1] * diff_real
        probe_grad = probe_grad + jnp.stack([grad_real, grad_imag])
        probe_weight = probe_weight + patch[0] * patch[0] + patch[1] * patch[1]
        return (grad_pad, cover_pad, probe_grad, probe_weight)

    def visit(totals, item):
        row_start, col_start, alive, measured = item

        def active(state):
            return work(state, row_start, col_start, measured)

        def passive(state):
            return state
        return (lax.cond(alive, active, passive, totals), None)
    initial = (jnp.zeros(padded.shape, jnp.float32), jnp.zeros(padded.shape[1:], jnp.float32), jnp.zeros((2, PR, PR), jnp.float32), jnp.zeros((PR, PR), jnp.float32))
    totals, unused = lax.scan(visit, initial, (flat_rows, flat_cols, alive_slots, measures))
    grad_pad, cover_pad, probe_grad, probe_weight = totals
    object_grad = grad_pad[:, H:H + NY, H:H + NX]
    coverage = cover_pad[H:H + NY, H:H + NX]
    object_denom = (1.0 - mix_object) * coverage + mix_object * jnp.max(coverage)
    new_object = object_field + object_grad / object_denom[None]
    probe_denom = (1.0 - mix_probe) * probe_weight + mix_probe * jnp.max(probe_weight)
    new_probe = probe + probe_grad / probe_denom[None]
    return (new_object, new_probe)
```

```python
import functools
import math

import jax
import jax.numpy as jnp
import ml_dtypes
import numpy as np
from jax import lax
from jax.experimental import pallas as pl
from jax.experimental.pallas import tpu as pltpu
from jax.sharding import PartitionSpec as P

H = 128
LANES = 128
CHUNK = 32
INFO = 8
BF = jnp.bfloat16
F32 = jnp.float32
MIX_OBJECT = 0.5
MIX_PROBE = 0.5
VMEM = pl.BlockSpec(memory_space=pltpu.VMEM)
SMEM = pl.BlockSpec(memory_space=pltpu.SMEM)


def rounded_pair(table):
    table = table.astype(np.float32)
    high = table.astype(ml_dtypes.bfloat16)
    low = (table - high.astype(np.float32)).astype(ml_dtypes.bfloat16)
    return high, low


def dft_tables(length):
    index = np.arange(length)
    angle = 2.0 * np.pi * ((index[:, None] * index[None, :]) % length) / length
    cos_high, cos_low = rounded_pair(np.cos(angle) / math.sqrt(length))
    sin_high, sin_low = rounded_pair(-np.sin(angle) / math.sqrt(length))
    left_high = np.block([[cos_high, -sin_high], [sin_high, cos_high]])
    left_low = np.block([[cos_low, -sin_low], [sin_low, cos_low]])
    right_high = np.block([[cos_high, sin_high], [-sin_high, cos_high]])
    right_low = np.block([[cos_low, sin_low], [-sin_low, cos_low]])
    left = np.concatenate([left_high, left_high, left_low], axis=1)
    right = np.concatenate([right_high, right_high, right_low], axis=0)
    return left, right


def split(x):
    high = x.astype(BF)
    return high, (x - high.astype(F32)).astype(BF)


def side_block(place, side, sides, blocks):
    if sides == 1:
        return jnp.where(place[1] == 0, blocks - 1, 0)
    return 0 if side == 0 else blocks - 1


def side_step(place, side, sides):
    if sides == 1:
        return jnp.where(place[1] == 0, 1, -1)
    return -1 if side == 0 else 1


def cover_kernel(tile_rows, tile_cols, sides, place, info, probe, cover, peak, total, power):
    pr = probe.shape[1]
    pieces = pr // LANES
    for j in range(pieces):
        cut = slice(j * LANES, (j + 1) * LANES)
        power[j] = probe[0, :, cut] * probe[0, :, cut] + probe[1, :, cut] * probe[1, :, cut]
    total[...] = jnp.zeros_like(total)
    lanes = lax.broadcasted_iota(jnp.int32, (CHUNK, LANES), 1)
    even = place[0] % 2 == 0
    steps_down = (0, jnp.where(even, 1, -1), jnp.where(even, -1, 1))
    steps_right = (0,) + tuple(side_step(place, s, sides) for s in range(sides))
    for v in range(3):
        for h in range(1 + sides):
            source = v * (1 + sides) + h
            down, right = steps_down[v], steps_right[h]

            def visit(k, carry):
                row = info[source, k] + pr - H + down * tile_rows
                col = info[source, 8 + k] + pr - H + right * tile_cols
                inside = (row > 0) & (row < pr + tile_rows) & (col > 0) & (col < pr + tile_cols)

                @pl.when(inside)
                def _():
                    shift = col & (LANES - 1)
                    block = col >> 7
                    low = lanes < shift
                    for q in range(pr // CHUNK):
                        turned = [
                            pltpu.roll(power[j, q * CHUNK : (q + 1) * CHUNK, :], shift, 1)
                            for j in range(pieces)
                        ]
                        here = pl.ds(row + q * CHUNK, CHUNK)
                        zero = jnp.zeros((CHUNK, LANES), F32)
                        total[block, here, :] += jnp.where(low, zero, turned[0])
                        for j in range(1, pieces):
                            total[block + j, here, :] += jnp.where(low, turned[j - 1], turned[j])
                        total[block + pieces, here, :] += jnp.where(low, turned[-1], zero)

                return carry

            lax.fori_loop(0, info[source, 16], visit, 0)
    first = pr // LANES
    best = jnp.zeros((8, LANES), F32)
    for b in range(tile_cols // LANES):
        own = total[first + b, pr : pr + tile_rows, :]
        cover[:, b * LANES : (b + 1) * LANES] = own
        best = jnp.maximum(best, jnp.max(own.reshape(tile_rows // 8, 8, LANES), axis=0))
    peak[...] = jnp.full((8, LANES), jnp.max(best), F32)


def cover_call(place, info, probe, tile_rows, tile_cols, sides):
    pr = probe.shape[1]
    blocks = (tile_cols + 2 * pr) // LANES + 1
    return pl.pallas_call(
        functools.partial(cover_kernel, tile_rows, tile_cols, sides),
        out_shape=(
            jax.ShapeDtypeStruct((tile_rows, tile_cols), F32),
            jax.ShapeDtypeStruct((8, LANES), F32),
        ),
        in_specs=[SMEM, SMEM, VMEM],
        out_specs=(VMEM, VMEM),
        scratch_shapes=[
            pltpu.VMEM((blocks, tile_rows + 2 * pr, LANES), F32),
            pltpu.VMEM((pr // LANES, pr, LANES), F32),
        ],
        compiler_params=pltpu.CompilerParams(vmem_limit_bytes=24 << 20),
        cost_estimate=pl.CostEstimate(flops=4_000_000, bytes_accessed=8_000_000, transcendentals=0),
        name="cover",
    )(place, info, probe)


def positions_kernel(sides, *refs):
    place, rows, cols, count = refs[:4]
    tile, near, far_side = refs[4:7]
    side_in = refs[7 : 7 + sides]
    probe, measured, left, right = refs[7 + sides : 11 + sides]
    outs = refs[11 + sides :]
    middle, near_rim, far_rim = outs[:3]
    side_out = outs[3 : 3 + sides]
    probe_sums = outs[3 + sides]
    ext, grad, patch, exits, data, wide_data, half = outs[4 + sides :]

    pr = probe.shape[1]
    pieces = pr // LANES
    tile_rows, tile_cols = tile.shape[1:]
    ext_rows = tile_rows + 2 * H
    blocks = (tile_cols + 2 * H) // LANES
    own_blocks = tile_cols // LANES
    even = place[0] % 2 == 0
    near_row = pl.multiple_of(jnp.where(even, tile_rows + H, 0), 8)
    far_row = pl.multiple_of(jnp.where(even, 0, tile_rows + H), 8)
    side_blocks = [side_block(place, s, sides, blocks) for s in range(sides)]
    own = pl.ds(H, tile_rows)
    for ch in range(2):
        if sides == 1:
            ext[ch * blocks + blocks - 1 - side_blocks[0]] = jnp.zeros((ext_rows, LANES), F32)
        for b in range(own_blocks):
            at, cut = ch * blocks + 1 + b, slice(b * LANES, (b + 1) * LANES)
            ext[at, own, :] = tile[ch, :, cut]
            ext[at, pl.ds(near_row, H), :] = near[ch, 0:H, cut]
            ext[at, pl.ds(far_row, H), :] = far_side[ch, 0:H, cut]
        for s in range(sides):
            at = ch * blocks + side_blocks[s]
            cut = slice(tile_cols + s * LANES, tile_cols + (s + 1) * LANES)
            ext[at, own, :] = side_in[s][ch, 0:tile_rows, :]
            ext[at, pl.ds(near_row, H), :] = near[ch, 0:H, cut]
            ext[at, pl.ds(far_row, H), :] = far_side[ch, 0:H, cut]
    grad[...] = jnp.zeros_like(grad)
    probe_sums[...] = jnp.zeros_like(probe_sums)
    lanes = lax.broadcasted_iota(jnp.int32, (CHUNK, LANES), 1)

    def times_left():
        stack = jnp.concatenate([data[...], data[0 : 2 * pr]], axis=0)
        return jnp.dot(left[...], stack, preferred_element_type=F32)

    def times_right():
        for q in range(pr // CHUNK):
            cut = slice(q * CHUNK, (q + 1) * CHUNK)
            high, low = split(half[cut, :])
            wide_data[cut, 0:pr] = high
            wide_data[cut, 2 * pr : 3 * pr] = low
            high, low = split(half[pr + q * CHUNK : pr + (q + 1) * CHUNK, :])
            wide_data[cut, pr : 2 * pr] = high
            wide_data[cut, 3 * pr : 4 * pr] = low
        stack = jnp.concatenate([wide_data[...], wide_data[:, 0 : 2 * pr]], axis=1)
        return jnp.dot(stack, right[...], preferred_element_type=F32)

    def put(value, part, q, cut):
        high, low = split(value)
        data[part * pr + q * CHUNK : part * pr + (q + 1) * CHUNK, cut] = high
        data[(2 + part) * pr + q * CHUNK : (2 + part) * pr + (q + 1) * CHUNK, cut] = low

    def visit(k, carry):
        row, col = rows[0, 0, k], cols[0, 0, k]
        shift, block = col & (LANES - 1), col >> 7
        back = (LANES - shift) & (LANES - 1)
        keep = lanes < LANES - shift
        for q in range(pr // CHUNK):
            cut = slice(q * CHUNK, (q + 1) * CHUNK)
            here = pl.ds(row + q * CHUNK, CHUNK)
            seen = []
            for ch in range(2):
                turned = [
                    pltpu.roll(ext[ch * blocks + block + j, here, :], back, 1)
                    for j in range(pieces + 1)
                ]
                seen.append([jnp.where(keep, turned[j], turned[j + 1]) for j in range(pieces)])
            for j in range(pieces):
                part = slice(j * LANES, (j + 1) * LANES)
                probe_real, probe_imag = probe[0, cut, part], probe[1, cut, part]
                real, imag = seen[0][j], seen[1][j]
                patch[0, cut, part], patch[1, cut, part] = real, imag
                exit_real = probe_real * real - probe_imag * imag
                exit_imag = probe_real * imag + probe_imag * real
                exits[0, cut, part], exits[1, cut, part] = exit_real, exit_imag
                put(exit_real, 0, q, part)
                put(exit_imag, 1, q, part)
        half[...] = times_left()
        far = times_right()
        for q in range(pr // CHUNK):
            cut = slice(q * CHUNK, (q + 1) * CHUNK)
            real, imag = far[cut, 0:pr], far[cut, pr : 2 * pr]
            factor = jnp.sqrt(measured[0, 0, k, cut, :]) * lax.rsqrt(real * real + imag * imag + 1.0)
            put(real * factor, 0, q, slice(0, pr))
            put(-(imag * factor), 1, q, slice(0, pr))
        half[...] = times_left()
        conj_back = times_right()
        low = lanes < shift
        zero = jnp.zeros((CHUNK, LANES), F32)
        for q in range(pr // CHUNK):
            cut = slice(q * CHUNK, (q + 1) * CHUNK)
            here = pl.ds(row + q * CHUNK, CHUNK)
            turned = [[], []]
            for j in range(pieces):
                part = slice(j * LANES, (j + 1) * LANES)
                other = slice(pr + j * LANES, pr + (j + 1) * LANES)
                diff_real = conj_back[cut, part] - exits[0, cut, part]
                diff_imag = -conj_back[cut, other] - exits[1, cut, part]
                probe_real, probe_imag = probe[0, cut, part], probe[1, cut, part]
                turned[0].append(pltpu.roll(probe_real * diff_real + probe_imag * diff_imag, shift, 1))
                turned[1].append(pltpu.roll(probe_real * diff_imag - probe_imag * diff_real, shift, 1))
                real, imag = patch[0, cut, part], patch[1, cut, part]
                probe_sums[0, j, cut, :] += real * diff_real + imag * diff_imag
                probe_sums[1, j, cut, :] += real * diff_imag - imag * diff_real
                probe_sums[2, j, cut, :] += real * real + imag * imag
            for ch in range(2):
                at = ch * blocks + block
                grad[at, here, :] += jnp.where(low, zero, turned[ch][0])
                for j in range(1, pieces):
                    grad[at + j, here, :] += jnp.where(low, turned[ch][j - 1], turned[ch][j])
                grad[at + pieces, here, :] += jnp.where(low, turned[ch][-1], zero)
        return carry

    lax.fori_loop(0, count[0, 0], visit, 0)
    for ch in range(2):
        for b in range(own_blocks):
            at, cut = ch * blocks + 1 + b, slice(b * LANES, (b + 1) * LANES)
            middle[ch, :, cut] = grad[at, own, :]
            near_rim[ch, :, cut] = grad[at, pl.ds(near_row, H), :]
            far_rim[ch, :, cut] = grad[at, pl.ds(far_row, H), :]
        for s in range(sides):
            at = ch * blocks + side_blocks[s]
            side_out[s][ch, 0:H, :] = grad[at, pl.ds(near_row, H), :]
            side_out[s][ch, H : H + tile_rows, :] = grad[at, own, :]
            side_out[s][ch, H + tile_rows :, :] = grad[at, pl.ds(far_row, H), :]


def positions_call(place, rows, cols, count, tile, near, far_side, side_in, probe, measured):
    pr = probe.shape[1]
    sides = len(side_in)
    tile_rows, tile_cols = tile.shape[1:]
    ext_rows = tile_rows + 2 * H
    blocks = (tile_cols + 2 * H) // LANES
    left, right = dft_tables(pr)
    shape = lambda *dims: jax.ShapeDtypeStruct(dims, F32)
    slots = measured.shape[2]
    return pl.pallas_call(
        functools.partial(positions_kernel, sides),
        out_shape=(
            shape(2, tile_rows, tile_cols),
            shape(2, H, tile_cols),
            shape(2, H, tile_cols),
            *[shape(2, ext_rows, LANES)] * sides,
            shape(3, pr // LANES, pr, LANES),
        ),
        in_specs=[SMEM] * 4 + [VMEM] * (7 + sides),
        out_specs=(VMEM,) * (4 + sides),
        scratch_shapes=[
            pltpu.VMEM((2 * blocks, ext_rows, LANES), F32),
            pltpu.VMEM((2 * blocks, ext_rows, LANES), F32),
            pltpu.VMEM((2, pr, pr), F32),
            pltpu.VMEM((2, pr, pr), F32),
            pltpu.VMEM((4 * pr, pr), BF),
            pltpu.VMEM((pr, 4 * pr), BF),
            pltpu.VMEM((2 * pr, pr), F32),
        ],
        compiler_params=pltpu.CompilerParams(vmem_limit_bytes=52 << 20),
        cost_estimate=pl.CostEstimate(
            flops=slots * 96 * pr * pr * pr, bytes_accessed=16_000_000, transcendentals=slots * 2 * pr * pr
        ),
        name="positions",
    )(place, rows, cols, count, tile, near, far_side, *side_in, probe, measured, jnp.asarray(left), jnp.asarray(right))


def object_kernel(sides, *refs):
    place, tile, middle, cover, peak, near, far_side = refs[:7]
    side_in = refs[7 : 7 + sides]
    out = refs[7 + sides]
    tile_rows, tile_cols = tile.shape[1:]
    own_blocks = tile_cols // LANES
    even = place[0] % 2 == 0
    sums = refs[8 + sides]
    sums[...] = middle[...]
    near_row = pl.multiple_of(jnp.where(even, tile_rows - H, 0), 8)
    far_row = pl.multiple_of(jnp.where(even, 0, tile_rows - H), 8)
    sums[:, pl.ds(near_row, H), :] += near[...]
    sums[:, pl.ds(far_row, H), :] += far_side[...]
    for s in range(sides):
        received = side_in[s][:, H : H + tile_rows, :]
        if sides == 1:
            for edge, where in ((0, own_blocks - 1), (1, 0)):

                @pl.when((place[1] == 0) == (edge == 0))
                def _():
                    sums[:, :, where * LANES : (where + 1) * LANES] += received
        else:
            where = 0 if s == 0 else own_blocks - 1
            sums[:, :, where * LANES : (where + 1) * LANES] += received
    top = MIX_OBJECT * peak[0:1, 0:1]
    inverse = 1.0 / ((1.0 - MIX_OBJECT) * cover[...] + top)
    for ch in range(2):
        out[ch] = tile[ch] + sums[ch] * inverse


def object_call(place, tile, middle, cover, peak, near, far_side, side_in):
    sides = len(side_in)
    return pl.pallas_call(
        functools.partial(object_kernel, sides),
        out_shape=jax.ShapeDtypeStruct(tile.shape, F32),
        in_specs=[SMEM] + [VMEM] * (6 + sides),
        out_specs=VMEM,
        scratch_shapes=[pltpu.VMEM(tile.shape, F32)],
        compiler_params=pltpu.CompilerParams(vmem_limit_bytes=24 << 20),
        name="object_update",
    )(place, tile, middle, cover, peak, near, far_side, *side_in)


def probe_kernel(sums, probe, out):
    pr = probe.shape[1]
    pieces = pr // LANES
    weights = sums[2 * pieces * pr : 3 * pieces * pr, :]
    best = jnp.max(jnp.max(weights.reshape(-1, 8, LANES), axis=0), keepdims=True)
    for j in range(pieces):
        cut = slice(j * LANES, (j + 1) * LANES)
        weight = sums[(2 * pieces + j) * pr : (2 * pieces + j + 1) * pr, :]
        inverse = 1.0 / ((1.0 - MIX_PROBE) * weight + MIX_PROBE * best)
        for ch in range(2):
            at = (ch * pieces + j) * pr
            out[ch, :, cut] = probe[ch, :, cut] + sums[at : at + pr, :] * inverse


def probe_call(sums, probe):
    return pl.pallas_call(
        probe_kernel,
        out_shape=jax.ShapeDtypeStruct(probe.shape, F32),
        in_specs=[VMEM, VMEM],
        out_specs=VMEM,
        name="probe_update",
    )(sums, probe)


def swap(x, axis, first):
    size = lax.axis_size(axis)
    pairs = []
    for i in range(first, size - 1, 2):
        pairs += [(i, i + 1), (i + 1, i)]
    return lax.ppermute(x, axis, pairs)


def shifted(x, axis, by):
    size = lax.axis_size(axis)
    return lax.ppermute(x, axis, [(i, i + by) for i in range(size) if 0 <= i + by < size])


def to_sides(pieces):
    if len(pieces) == 1:
        return [swap(pieces[0], "narrow", 0)]
    return [shifted(pieces[1], "narrow", 1), shifted(pieces[0], "narrow", -1)]


def bits_of(axis):
    size = lax.axis_size(axis)
    return [1 << b for b in range(size.bit_length() - 1)]


def partner(x, axis, bit):
    size = lax.axis_size(axis)
    return lax.ppermute(x, axis, [(i, i ^ bit) for i in range(size)])


def half_of(x, which):
    rows = x.shape[0] // 2
    return lax.dynamic_slice_in_dim(x, which * rows, rows, axis=0)


def sum_everywhere(terms, peak):
    wide, narrow = bits_of("wide"), bits_of("narrow")
    halving = [("wide", b) for b in wide[:2]] + [("narrow", b) for b in narrow]
    doubling = [("wide", b) for b in wide[2:]]
    state = lambda axis, bit: (lax.axis_index(axis) // bit) % 2
    for axis, bit in halving:
        mine = state(axis, bit)
        got = partner(jnp.concatenate([half_of(terms, 1 - mine), peak], axis=0), axis, bit)
        rows = terms.shape[0] // 2
        terms = half_of(terms, mine) + got[:rows]
        peak = jnp.maximum(peak, got[rows:])
    for axis, bit in doubling:
        got = partner(jnp.concatenate([terms, peak], axis=0), axis, bit)
        rows = terms.shape[0]
        terms = terms + got[:rows]
        peak = jnp.maximum(peak, got[rows:])
    for axis, bit in halving[::-1]:
        first = state(axis, bit) == 0
        got = partner(terms, axis, bit)
        terms = jnp.concatenate([jnp.where(first, terms, got), jnp.where(first, got, terms)], axis=0)
    return terms, peak


def body(tile, probe, measured, rows, cols, counts):
    wide, narrow = lax.axis_index("wide"), lax.axis_index("narrow")
    sides = 1 if lax.axis_size("narrow") == 2 else 2
    tile_rows, tile_cols = tile.shape[1:]
    even = wide % 2 == 0
    place = jnp.stack([wide, narrow]).astype(jnp.int32)

    own_info = jnp.concatenate(
        [rows.reshape(-1), cols.reshape(-1), counts.reshape(-1), jnp.zeros((LANES - 17,), jnp.int32)]
    ).astype(F32)
    info_rows = jnp.broadcast_to(own_info, (2, INFO, LANES))

    def with_info(x):
        return jnp.concatenate([x, info_rows], axis=1)

    if sides == 1:
        edge = jnp.where(narrow == 0, tile_cols - H, 0)
        edges = [with_info(lax.dynamic_slice_in_dim(tile, edge, H, axis=2))]
    else:
        edges = [with_info(tile[:, :, :H]), with_info(tile[:, :, tile_cols - H :])]
    side_in = to_sides(edges)

    def band(at_end):
        start = jnp.where(at_end, tile_rows - H, 0)
        mine = lax.dynamic_slice_in_dim(tile, start, H, axis=1)
        mine = jnp.concatenate([mine, jnp.pad(info_rows, ((0, 0), (0, 0), (0, tile_cols - LANES)))], axis=1)
        others = [
            jnp.concatenate([lax.dynamic_slice_in_dim(s, start, H, axis=1), s[:, tile_rows:]], axis=1)
            for s in side_in
        ]
        return jnp.concatenate([mine] + others, axis=2)

    near = swap(band(even), "wide", 0)
    far_side = swap(band(~even), "wide", 1)

    def infos(x, row):
        return [x[0, row, 0:32]] + [
            x[0, row, tile_cols + s * LANES : tile_cols + s * LANES + 32] for s in range(sides)
        ]

    info = jnp.stack(
        [own_info[:32]] + [s[0, tile_rows, :32] for s in side_in] + infos(near, H) + infos(far_side, H)
    ).astype(jnp.int32)
    cover, peak = cover_call(place, info, probe, tile_rows, tile_cols, sides)

    out = positions_call(place, rows, cols, counts, tile, near, far_side, side_in, probe, measured)
    middle, near_rim, far_rim = out[:3]
    side_rims, probe_sums = list(out[3 : 3 + sides]), out[3 + sides]

    summed, peak = sum_everywhere(probe_sums.reshape(-1, LANES), peak)
    new_probe = probe_call(summed, probe)

    side_got = to_sides(side_rims)

    def with_sides(rim, part):
        for s, got in enumerate(side_got):
            if sides == 1:
                start = jnp.where(narrow == 0, tile_cols - H, 0)
            else:
                start = 0 if s == 0 else tile_cols - H
            old = lax.dynamic_slice_in_dim(rim, start, H, axis=2)
            rim = lax.dynamic_update_slice_in_dim(rim, old + got[:, part], start, axis=2)
        return rim

    near_got = swap(with_sides(near_rim, slice(0, H)), "wide", 0)
    far_got = swap(with_sides(far_rim, slice(H + tile_rows, None)), "wide", 1)
    new_object = object_call(place, tile, middle, cover, peak, near_got, far_got, side_got)
    return new_object, new_probe


def solution(mesh):
    placed = (
        P(None, "wide", "narrow"),
        P(),
        P("wide", "narrow", None, None, None),
        P("wide", "narrow", None),
        P("wide", "narrow", None),
        P("wide", "narrow"),
    )
    return jax.shard_map(
        body,
        mesh=mesh,
        in_specs=placed,
        out_specs=(P(None, "wide", "narrow"), P()),
        check_vma=False,
    )
```

```python
import functools
import math

import jax
import jax.numpy as jnp
import ml_dtypes
import numpy as np
from jax import lax
from jax.experimental import pallas as pl
from jax.experimental.pallas import tpu as pltpu
from jax.sharding import PartitionSpec as P

H = 128
LANES = 128
CHUNK = 32
WAYS = 2
INFO = 8
BF = jnp.bfloat16
F32 = jnp.float32
MIX_OBJECT = 0.5
MIX_PROBE = 0.5
VMEM = pl.BlockSpec(memory_space=pltpu.VMEM)
SMEM = pl.BlockSpec(memory_space=pltpu.SMEM)


def rounded_pair(table):
    table = table.astype(np.float32)
    high = table.astype(ml_dtypes.bfloat16)
    low = (table - high.astype(np.float32)).astype(ml_dtypes.bfloat16)
    return high, low


def dft_tables(length):
    index = np.arange(length)
    angle = 2.0 * np.pi * ((index[:, None] * index[None, :]) % length) / length
    cos_high, cos_low = rounded_pair(np.cos(angle) / math.sqrt(length))
    sin_high, sin_low = rounded_pair(-np.sin(angle) / math.sqrt(length))
    left = np.concatenate([cos_high, sin_high, cos_high, sin_high, cos_low, sin_low], axis=1)
    right_high = np.block([[cos_high, sin_high], [-sin_high, cos_high]])
    right_low = np.block([[cos_low, sin_low], [-sin_low, cos_low]])
    right = np.concatenate([right_high, right_high, right_low], axis=0)
    return left, right


def split(x):
    high = x.astype(BF)
    return high, (x - high.astype(F32)).astype(BF)


def side_block(place, side, sides, blocks):
    if sides == 1:
        return jnp.where(place[1] == 0, blocks - 1, 0)
    return 0 if side == 0 else blocks - 1


def side_step(place, side, sides):
    if sides == 1:
        return jnp.where(place[1] == 0, 1, -1)
    return -1 if side == 0 else 1


def cover_kernel(tile_rows, tile_cols, sides, place, info, probe, cover, peak, total, power):
    pr = probe.shape[1]
    pieces = pr // LANES
    for j in range(pieces):
        cut = slice(j * LANES, (j + 1) * LANES)
        power[j] = probe[0, :, cut] * probe[0, :, cut] + probe[1, :, cut] * probe[1, :, cut]
    total[...] = jnp.zeros_like(total)
    lanes = lax.broadcasted_iota(jnp.int32, (CHUNK, LANES), 1)
    even = place[0] % 2 == 0
    steps_down = (0, jnp.where(even, 1, -1), jnp.where(even, -1, 1))
    steps_right = (0,) + tuple(side_step(place, s, sides) for s in range(sides))
    for v in range(3):
        for h in range(1 + sides):
            source = v * (1 + sides) + h
            down, right = steps_down[v], steps_right[h]

            def visit(k, carry):
                row = info[source, k] + pr - H + down * tile_rows
                col = info[source, 8 + k] + pr - H + right * tile_cols
                inside = (row > 0) & (row < pr + tile_rows) & (col > 0) & (col < pr + tile_cols)

                @pl.when(inside)
                def _():
                    shift = col & (LANES - 1)
                    block = col >> 7
                    low = lanes < shift
                    for q in range(pr // CHUNK):
                        turned = [
                            pltpu.roll(power[j, q * CHUNK : (q + 1) * CHUNK, :], shift, 1)
                            for j in range(pieces)
                        ]
                        here = pl.ds(row + q * CHUNK, CHUNK)
                        zero = jnp.zeros((CHUNK, LANES), F32)
                        total[block, here, :] += jnp.where(low, zero, turned[0])
                        for j in range(1, pieces):
                            total[block + j, here, :] += jnp.where(low, turned[j - 1], turned[j])
                        total[block + pieces, here, :] += jnp.where(low, turned[-1], zero)

                return carry

            lax.fori_loop(0, info[source, 16], visit, 0)
    first = pr // LANES
    best = jnp.zeros((8, LANES), F32)
    for b in range(tile_cols // LANES):
        own = total[first + b, pr : pr + tile_rows, :]
        cover[:, b * LANES : (b + 1) * LANES] = own
        best = jnp.maximum(best, jnp.max(own.reshape(tile_rows // 8, 8, LANES), axis=0))
    peak[...] = jnp.full((8, LANES), jnp.max(best), F32)


def cover_call(place, info, probe, tile_rows, tile_cols, sides):
    pr = probe.shape[1]
    blocks = (tile_cols + 2 * pr) // LANES + 1
    return pl.pallas_call(
        functools.partial(cover_kernel, tile_rows, tile_cols, sides),
        out_shape=(
            jax.ShapeDtypeStruct((tile_rows, tile_cols), F32),
            jax.ShapeDtypeStruct((8, LANES), F32),
        ),
        in_specs=[SMEM, SMEM, VMEM],
        out_specs=(VMEM, VMEM),
        scratch_shapes=[
            pltpu.VMEM((blocks, tile_rows + 2 * pr, LANES), F32),
            pltpu.VMEM((pr // LANES, pr, LANES), F32),
        ],
        compiler_params=pltpu.CompilerParams(vmem_limit_bytes=24 << 20),
        cost_estimate=pl.CostEstimate(flops=4_000_000, bytes_accessed=8_000_000, transcendentals=0),
        name="cover",
    )(place, info, probe)


def positions_kernel(sides, *refs):
    place, rows, cols, count = refs[:4]
    tile, near, far_side = refs[4:7]
    side_in, corners = refs[7 : 7 + sides], refs[7 + sides : 7 + 2 * sides]
    probe, measured, left, right = refs[7 + 2 * sides : 11 + 2 * sides]
    outs = refs[11 + 2 * sides :]
    middle, near_rim, far_rim = outs[:3]
    side_out = outs[3 : 3 + sides]
    probe_sums = outs[3 + sides]
    ext, grad = outs[4 + sides : 6 + sides]
    scratch = outs[6 + sides :]
    patches, exits, stacks, wides, fields = [scratch[i * WAYS : (i + 1) * WAYS] for i in range(5)]

    pr = probe.shape[1]
    pieces = pr // LANES
    tile_rows, tile_cols = tile.shape[1:]
    ext_rows = tile_rows + 2 * H
    blocks = (tile_cols + 2 * H) // LANES
    own_blocks = tile_cols // LANES
    even = place[0] % 2 == 0
    near_row = pl.multiple_of(jnp.where(even, tile_rows + H, 0), 8)
    far_row = pl.multiple_of(jnp.where(even, 0, tile_rows + H), 8)
    side_blocks = [side_block(place, s, sides, blocks) for s in range(sides)]
    own, near_rows, far_rows = pl.ds(H, tile_rows), pl.ds(near_row, H), pl.ds(far_row, H)
    for ch in range(2):
        if sides == 1:
            ext[ch * blocks + blocks - 1 - side_blocks[0]] = jnp.zeros((ext_rows, LANES), F32)
        for b in range(own_blocks):
            at, cut = ch * blocks + 1 + b, slice(b * LANES, (b + 1) * LANES)
            ext[at, own, :] = tile[ch, :, cut]
            ext[at, near_rows, :] = near[ch, 0:H, cut]
            ext[at, far_rows, :] = far_side[ch, :, cut]
        for s in range(sides):
            at = ch * blocks + side_blocks[s]
            cut = slice(tile_cols + s * LANES, tile_cols + (s + 1) * LANES)
            ext[at, own, :] = side_in[s][ch, 0:tile_rows, :]
            ext[at, near_rows, :] = near[ch, 0:H, cut]
            ext[at, far_rows, :] = corners[s][ch]
    grad[...] = jnp.zeros_like(grad)
    probe_sums[...] = jnp.zeros_like(probe_sums)
    lanes = lax.broadcasted_iota(jnp.int32, (CHUNK, LANES), 1)

    def put(stack, value, part, q, first):
        width = value.shape[1]
        high, low = split(value)
        rows_at = lambda block: slice(block * pr + q * CHUNK, block * pr + (q + 1) * CHUNK)
        here, there = slice(first, first + width), slice(pr + first, pr + first + width)
        if part == 0:
            stack[rows_at(0), here], stack[rows_at(1), there] = high, high
            stack[rows_at(2), here], stack[rows_at(3), there] = low, low
        else:
            stack[rows_at(0), there], stack[rows_at(1), here] = high, -high
            stack[rows_at(2), there], stack[rows_at(3), here] = low, -low

    def times_left(w):
        stack = jnp.concatenate([stacks[w][...], stacks[w][0 : 2 * pr]], axis=0)
        fields[w][...] = jnp.dot(left[...], stack, preferred_element_type=F32)

    def times_right(w):
        for q in range(pr // CHUNK):
            cut = slice(q * CHUNK, (q + 1) * CHUNK)
            high, low = split(fields[w][cut, :])
            wides[w][cut, 0 : 2 * pr] = high
            wides[w][cut, 2 * pr : 4 * pr] = low
        stack = jnp.concatenate([wides[w][...], wides[w][:, 0 : 2 * pr]], axis=1)
        fields[w][...] = jnp.dot(stack, right[...], preferred_element_type=F32)

    def load(w, k):
        row, col = rows[0, 0, k], cols[0, 0, k]
        shift, block = col & (LANES - 1), col >> 7
        back = (LANES - shift) & (LANES - 1)
        keep = lanes < LANES - shift
        for q in range(pr // CHUNK):
            cut = slice(q * CHUNK, (q + 1) * CHUNK)
            here = pl.ds(row + q * CHUNK, CHUNK)
            seen = []
            for ch in range(2):
                turned = [
                    pltpu.roll(ext[ch * blocks + block + j, here, :], back, 1)
                    for j in range(pieces + 1)
                ]
                seen.append([jnp.where(keep, turned[j], turned[j + 1]) for j in range(pieces)])
            for j in range(pieces):
                part = slice(j * LANES, (j + 1) * LANES)
                probe_real, probe_imag = probe[0, cut, part], probe[1, cut, part]
                real, imag = seen[0][j], seen[1][j]
                patches[w][0, cut, part], patches[w][1, cut, part] = real, imag
                exit_real = probe_real * real - probe_imag * imag
                exit_imag = probe_real * imag + probe_imag * real
                exits[w][0, cut, part], exits[w][1, cut, part] = exit_real, exit_imag
                put(stacks[w], exit_real, 0, q, j * LANES)
                put(stacks[w], exit_imag, 1, q, j * LANES)

    def project(w, k):
        for q in range(pr // CHUNK):
            cut = slice(q * CHUNK, (q + 1) * CHUNK)
            real, imag = fields[w][cut, 0:pr], fields[w][cut, pr : 2 * pr]
            factor = jnp.sqrt(measured[0, 0, k, cut, :]) * lax.rsqrt(real * real + imag * imag + 1.0)
            put(stacks[w], real * factor, 0, q, 0)
            put(stacks[w], -(imag * factor), 1, q, 0)

    def finish(w, k, live):
        row, col = rows[0, 0, k], cols[0, 0, k]
        shift, block = col & (LANES - 1), col >> 7
        low = lanes < shift
        zero = jnp.zeros((CHUNK, LANES), F32)
        for q in range(pr // CHUNK):
            cut = slice(q * CHUNK, (q + 1) * CHUNK)
            here = pl.ds(row + q * CHUNK, CHUNK)
            turned = [[], []]
            for j in range(pieces):
                part = slice(j * LANES, (j + 1) * LANES)
                other = slice(pr + j * LANES, pr + (j + 1) * LANES)
                diff_real = fields[w][cut, part] - exits[w][0, cut, part]
                diff_imag = -fields[w][cut, other] - exits[w][1, cut, part]
                real, imag = patches[w][0, cut, part], patches[w][1, cut, part]
                weight = real * real + imag * imag
                if live is not None:
                    diff_real, diff_imag = diff_real * live, diff_imag * live
                    weight = weight * live
                probe_real, probe_imag = probe[0, cut, part], probe[1, cut, part]
                turned[0].append(pltpu.roll(probe_real * diff_real + probe_imag * diff_imag, shift, 1))
                turned[1].append(pltpu.roll(probe_real * diff_imag - probe_imag * diff_real, shift, 1))
                probe_sums[j, 0, cut, :] += real * diff_real + imag * diff_imag
                probe_sums[j, 1, cut, :] += real * diff_imag - imag * diff_real
                probe_sums[j, 2, cut, :] += weight
            for ch in range(2):
                at = ch * blocks + block
                grad[at, here, :] += jnp.where(low, zero, turned[ch][0])
                for j in range(1, pieces):
                    grad[at + j, here, :] += jnp.where(low, turned[ch][j - 1], turned[ch][j])
                grad[at + pieces, here, :] += jnp.where(low, turned[ch][-1], zero)

    live_slots = count[0, 0]

    def visit(i, carry):
        slots = [jnp.minimum(i * WAYS + w, live_slots - 1) for w in range(WAYS)]
        lives = [None] + [jnp.where(i * WAYS + w < live_slots, 1.0, 0.0) for w in range(1, WAYS)]
        for w in range(WAYS):
            load(w, slots[w])
            times_left(w)
        for w in range(WAYS):
            times_right(w)
        for w in range(WAYS):
            project(w, slots[w])
            times_left(w)
        for w in range(WAYS):
            times_right(w)
        for w in range(WAYS):
            finish(w, slots[w], lives[w])
        return carry

    lax.fori_loop(0, (live_slots + WAYS - 1) // WAYS, visit, 0)
    for ch in range(2):
        for b in range(own_blocks):
            at, cut = ch * blocks + 1 + b, slice(b * LANES, (b + 1) * LANES)
            middle[ch, :, cut] = grad[at, own, :]
            near_rim[ch, :, cut] = grad[at, near_rows, :]
            far_rim[ch, :, cut] = grad[at, far_rows, :]
        for s in range(sides):
            at = ch * blocks + side_blocks[s]
            cut = slice(tile_cols + s * LANES, tile_cols + (s + 1) * LANES)
            side_out[s][ch] = grad[at, own, :]
            near_rim[ch, :, cut] = grad[at, near_rows, :]
            far_rim[ch, :, cut] = grad[at, far_rows, :]


def positions_call(place, rows, cols, count, tile, near, far_side, side_in, corners, probe, measured):
    pr = probe.shape[1]
    sides = len(side_in)
    tile_rows, tile_cols = tile.shape[1:]
    ext_rows = tile_rows + 2 * H
    blocks = (tile_cols + 2 * H) // LANES
    left, right = dft_tables(pr)
    shape = lambda *dims: jax.ShapeDtypeStruct(dims, F32)
    slots = measured.shape[2]
    return pl.pallas_call(
        functools.partial(positions_kernel, sides),
        out_shape=(
            shape(2, tile_rows, tile_cols),
            shape(2, H, tile_cols + sides * LANES),
            shape(2, H, tile_cols + sides * LANES),
            *[shape(2, tile_rows, LANES)] * sides,
            shape(pr // LANES, 3, pr, LANES),
        ),
        in_specs=[SMEM] * 4 + [VMEM] * (7 + 2 * sides),
        out_specs=(VMEM,) * (4 + sides),
        scratch_shapes=[
            pltpu.VMEM((2 * blocks, ext_rows, LANES), F32),
            pltpu.VMEM((2 * blocks, ext_rows, LANES), F32),
            *[pltpu.VMEM((2, pr, pr), F32)] * (2 * WAYS),
            *[pltpu.VMEM((4 * pr, 2 * pr), BF)] * WAYS,
            *[pltpu.VMEM((pr, 4 * pr), BF)] * WAYS,
            *[pltpu.VMEM((pr, 2 * pr), F32)] * WAYS,
        ],
        compiler_params=pltpu.CompilerParams(vmem_limit_bytes=44 << 20),
        cost_estimate=pl.CostEstimate(
            flops=slots * 96 * pr * pr * pr, bytes_accessed=16_000_000, transcendentals=slots * 2 * pr * pr
        ),
        name="positions",
    )(place, rows, cols, count, tile, near, far_side, *side_in, *corners, probe, measured,
      jnp.asarray(left), jnp.asarray(right))


def update_kernel(sides, *refs):
    place, tile, middle, cover, peak, near, far_side = refs[:7]
    side_in = refs[7 : 7 + sides]
    own_terms, other_terms, probe, out, new_probe, sums = refs[7 + sides :]
    tile_rows, tile_cols = tile.shape[1:]
    own_blocks = tile_cols // LANES
    even = place[0] % 2 == 0
    sums[...] = middle[...]
    near_row = pl.multiple_of(jnp.where(even, tile_rows - H, 0), 8)
    far_row = pl.multiple_of(jnp.where(even, 0, tile_rows - H), 8)
    sums[:, pl.ds(near_row, H), :] += near[:, :, 0:tile_cols]
    sums[:, pl.ds(far_row, H), :] += far_side[:, :, 0:tile_cols]
    for s in range(sides):
        if sides == 1:
            for edge, where in ((0, own_blocks - 1), (1, 0)):

                @pl.when((place[1] == 0) == (edge == 0))
                def _():
                    sums[:, :, where * LANES : (where + 1) * LANES] += side_in[s][...]
        else:
            where = 0 if s == 0 else own_blocks - 1
            sums[:, :, where * LANES : (where + 1) * LANES] += side_in[s][...]
    top = MIX_OBJECT * peak[0:1, 0:1]
    inverse = 1.0 / ((1.0 - MIX_OBJECT) * cover[...] + top)
    for ch in range(2):
        out[ch] = tile[ch] + sums[ch] * inverse

    pr = probe.shape[1]
    pieces = pr // LANES
    both = (own_terms, other_terms)

    def update(parts):
        flat = [parts[j * len(parts) // pieces] for j in range(pieces)]
        span = flat[0].shape[0] // (pieces // len(parts))
        term = lambda j, ch: flat[j][(j % (pieces // len(parts))) * span + ch * pr :][:pr]
        weights = [term(j, 2) for j in range(pieces)]
        best = functools.reduce(jnp.maximum, weights)
        best = jnp.max(jnp.max(best.reshape(-1, 8, LANES), axis=0), keepdims=True)
        for j in range(pieces):
            cut = slice(j * LANES, (j + 1) * LANES)
            scale = 1.0 / ((1.0 - MIX_PROBE) * weights[j] + MIX_PROBE * best)
            for ch in range(2):
                new_probe[ch, :, cut] = probe[ch, :, cut] + term(j, ch) * scale

    for first in (0, 1):

        @pl.when(place[0] % 2 == first)
        def _():
            update([both[first][...], both[1 - first][...]])


def update_call(place, tile, middle, cover, peak, near, far_side, side_in, own_terms, other_terms, probe):
    sides = len(side_in)
    return pl.pallas_call(
        functools.partial(update_kernel, sides),
        out_shape=(jax.ShapeDtypeStruct(tile.shape, F32), jax.ShapeDtypeStruct(probe.shape, F32)),
        in_specs=[SMEM] + [VMEM] * (9 + sides),
        out_specs=(VMEM, VMEM),
        scratch_shapes=[pltpu.VMEM(tile.shape, F32)],
        compiler_params=pltpu.CompilerParams(vmem_limit_bytes=32 << 20),
        name="update",
    )(place, tile, middle, cover, peak, near, far_side, *side_in, own_terms, other_terms, probe)


def swap(x, axis, first):
    size = lax.axis_size(axis)
    pairs = []
    for i in range(first, size - 1, 2):
        pairs += [(i, i + 1), (i + 1, i)]
    return lax.ppermute(x, axis, pairs)


def shifted(x, axis, by):
    size = lax.axis_size(axis)
    return lax.ppermute(x, axis, [(i, i + by) for i in range(size) if 0 <= i + by < size])


def to_sides(pieces):
    if len(pieces) == 1:
        return [swap(pieces[0], "narrow", 0)]
    return [shifted(pieces[1], "narrow", 1), shifted(pieces[0], "narrow", -1)]


def bits_of(axis):
    size = lax.axis_size(axis)
    return [1 << b for b in range(size.bit_length() - 1)]


def partner(x, axis, bit):
    size = lax.axis_size(axis)
    return lax.ppermute(x, axis, [(i, i ^ bit) for i in range(size)])


def half_of(x, which):
    rows = x.shape[0] // 2
    return lax.dynamic_slice_in_dim(x, which * rows, rows, axis=0)


def bit_state(axis, bit):
    return (lax.axis_index(axis) // bit) % 2


def halve(terms, peak, axis, bit):
    mine = bit_state(axis, bit)
    got = partner(jnp.concatenate([half_of(terms, 1 - mine), peak], axis=0), axis, bit)
    rows = terms.shape[0] // 2
    return half_of(terms, mine) + got[:rows], jnp.maximum(peak, got[rows:])


def double(terms, peak, axis, bit):
    got = partner(jnp.concatenate([terms, peak], axis=0), axis, bit)
    rows = terms.shape[0]
    return terms + got[:rows], jnp.maximum(peak, got[rows:])


def gather(terms, axis, bit):
    first = bit_state(axis, bit) == 0
    got = partner(terms, axis, bit)
    return jnp.concatenate([jnp.where(first, terms, got), jnp.where(first, got, terms)], axis=0)


def to_corners(bands):
    wide, narrow = lax.axis_size("wide"), lax.axis_size("narrow")
    steps = [0] if len(bands) == 1 else [-1, 1]
    got = []
    for s, step in enumerate(steps):
        pairs = []
        for i in range(1, wide - 1, 2):
            for n in range(narrow):
                m = 1 - n if step == 0 else n - step
                if 0 <= m < narrow:
                    pairs += [(i * narrow + n, (i + 1) * narrow + m), ((i + 1) * narrow + n, i * narrow + m)]
        band = bands[0] if step == 0 else bands[1 - s]
        got.append(lax.ppermute(band, ("wide", "narrow"), pairs))
    return got


def after(x, *others):
    return lax.optimization_barrier((x, *others))[0]


def body(tile, probe, measured, rows, cols, counts):
    wide, narrow = lax.axis_index("wide"), lax.axis_index("narrow")
    sides = 1 if lax.axis_size("narrow") == 2 else 2
    tile_rows, tile_cols = tile.shape[1:]
    even = wide % 2 == 0
    place = jnp.stack([wide, narrow]).astype(jnp.int32)

    own_info = jnp.concatenate(
        [rows.reshape(-1), cols.reshape(-1), counts.reshape(-1), jnp.zeros((LANES - 17,), jnp.int32)]
    ).astype(F32)
    info_rows = jnp.broadcast_to(own_info, (2, INFO, LANES))

    near_start = jnp.where(even, tile_rows - H, 0)
    far_start = jnp.where(even, 0, tile_rows - H)
    side_start = jnp.where(narrow == 0, tile_cols - H, 0)
    side_starts = [side_start] if sides == 1 else [0, tile_cols - H]
    edges = [lax.dynamic_slice_in_dim(tile, start, H, axis=2) for start in side_starts]

    side_in = to_sides([jnp.concatenate([e, info_rows], axis=1) for e in edges])
    far_side = swap(lax.dynamic_slice_in_dim(tile, far_start, H, axis=1), "wide", 1)
    corners = to_corners([lax.dynamic_slice_in_dim(e, far_start, H, axis=1) for e in edges])

    mine = lax.dynamic_slice_in_dim(tile, near_start, H, axis=1)
    mine = jnp.concatenate([mine, jnp.pad(info_rows, ((0, 0), (0, 0), (0, tile_cols - LANES)))], axis=1)
    others = [
        jnp.concatenate([lax.dynamic_slice_in_dim(s, near_start, H, axis=1), s[:, tile_rows:]], axis=1)
        for s in side_in
    ]
    near = swap(jnp.concatenate([mine] + others, axis=2), "wide", 0)
    own_infos = jnp.concatenate([info_rows[:1]] + [s[:1, tile_rows:] for s in side_in], axis=0)
    far_infos = swap(own_infos, "wide", 1)
    near_infos = jnp.stack(
        [near[0, H:, :LANES]] + [near[0, H:, tile_cols + s * LANES : tile_cols + (s + 1) * LANES] for s in range(sides)]
    )
    info = jnp.concatenate([own_infos, near_infos, far_infos], axis=0)[:, 0, :32].astype(jnp.int32)
    cover, peak = cover_call(place, info, probe, tile_rows, tile_cols, sides)

    out = positions_call(place, rows, cols, counts, tile, near, far_side, side_in, corners, probe, measured)
    middle, near_rim, far_rim = out[:3]
    side_rims, probe_sums = list(out[3 : 3 + sides]), out[3 + sides]

    terms = probe_sums.reshape(-1, LANES)
    wide_bits, narrow_bits = bits_of("wide"), bits_of("narrow")
    terms, peak = halve(terms, peak, "wide", wide_bits[0])
    near_got = swap(after(near_rim, terms), "wide", 0)
    terms, peak = halve(terms, peak, "wide", wide_bits[1])
    far_got = swap(after(far_rim, terms), "wide", 1)
    for bit in narrow_bits:
        terms, peak = halve(terms, peak, "narrow", bit)
    for bit in wide_bits[2:]:
        terms, peak = double(terms, peak, "wide", bit)
    for bit in narrow_bits[::-1]:
        terms = gather(terms, "narrow", bit)

    def with_rims(piece, s):
        cut = slice(tile_cols + s * LANES, tile_cols + (s + 1) * LANES)
        below = jnp.where(even, near_got[:, :, cut], far_got[:, :, cut])
        above = jnp.where(even, far_got[:, :, cut], near_got[:, :, cut])
        return piece + jnp.concatenate([above, below], axis=1)

    side_got = to_sides([with_rims(piece, s) for s, piece in enumerate(side_rims)])
    terms = gather(terms, "wide", wide_bits[1])
    other_terms = partner(terms, "wide", wide_bits[0])
    return update_call(
        place, tile, middle, cover, peak, near_got, far_got, side_got, terms, other_terms, probe
    )


def solution(mesh):
    placed = (
        P(None, "wide", "narrow"),
        P(),
        P("wide", "narrow", None, None, None),
        P("wide", "narrow", None),
        P("wide", "narrow", None),
        P("wide", "narrow"),
    )
    return jax.shard_map(
        body,
        mesh=mesh,
        in_specs=placed,
        out_specs=(P(None, "wide", "narrow"), P()),
        check_vma=False,
    )
```

```python
import functools
import math

import jax
import jax.numpy as jnp
import ml_dtypes
import numpy as np
from jax import lax
from jax.experimental import pallas as pl
from jax.experimental.pallas import tpu as pltpu
from jax.sharding import PartitionSpec as P

H = 128
LANES = 128
CHUNK = 32
WAYS = 2
INFO = 8
BF = jnp.bfloat16
F32 = jnp.float32
MIX_OBJECT = 0.5
MIX_PROBE = 0.5
VMEM = pl.BlockSpec(memory_space=pltpu.VMEM)
SMEM = pl.BlockSpec(memory_space=pltpu.SMEM)


def rounded_pair(table):
    table = table.astype(np.float32)
    high = table.astype(ml_dtypes.bfloat16)
    low = (table - high.astype(np.float32)).astype(ml_dtypes.bfloat16)
    return high, low


def dft_tables(length):
    index = np.arange(length)
    angle = 2.0 * np.pi * ((index[:, None] * index[None, :]) % length) / length
    cos_high, cos_low = rounded_pair(np.cos(angle) / math.sqrt(length))
    sin_high, sin_low = rounded_pair(-np.sin(angle) / math.sqrt(length))
    left = np.concatenate([cos_high, sin_high, cos_high, sin_high, cos_low, sin_low], axis=1)
    right_high = np.block([[cos_high, sin_high], [-sin_high, cos_high]])
    right_low = np.block([[cos_low, sin_low], [-sin_low, cos_low]])
    right = np.concatenate([right_high, right_high, right_low], axis=0)
    return left, right


def split(x):
    high = x.astype(BF)
    return high, (x - high.astype(F32)).astype(BF)


def side_block(place, side, sides, blocks):
    if sides == 1:
        return jnp.where(place[1] == 0, blocks - 1, 0)
    return 0 if side == 0 else blocks - 1


def side_step(place, side, sides):
    if sides == 1:
        return jnp.where(place[1] == 0, 1, -1)
    return -1 if side == 0 else 1


def cover_kernel(tile_rows, tile_cols, sides, place, info, probe, cover, peak, total, power):
    pr = probe.shape[1]
    pieces = pr // LANES
    for j in range(pieces):
        cut = slice(j * LANES, (j + 1) * LANES)
        power[j] = probe[0, :, cut] * probe[0, :, cut] + probe[1, :, cut] * probe[1, :, cut]
    total[...] = jnp.zeros_like(total)
    lanes = lax.broadcasted_iota(jnp.int32, (CHUNK, LANES), 1)
    even = place[0] % 2 == 0
    steps_down = (0, jnp.where(even, 1, -1), jnp.where(even, -1, 1))
    steps_right = (0,) + tuple(side_step(place, s, sides) for s in range(sides))
    for v in range(3):
        for h in range(1 + sides):
            source = v * (1 + sides) + h
            down, right = steps_down[v], steps_right[h]

            def visit(k, carry):
                row = info[source, k] + pr - H + down * tile_rows
                col = info[source, 8 + k] + pr - H + right * tile_cols
                inside = (row > 0) & (row < pr + tile_rows) & (col > 0) & (col < pr + tile_cols)

                @pl.when(inside)
                def _():
                    shift = col & (LANES - 1)
                    block = col >> 7
                    low = lanes < shift
                    for q in range(pr // CHUNK):
                        turned = [
                            pltpu.roll(power[j, q * CHUNK : (q + 1) * CHUNK, :], shift, 1)
                            for j in range(pieces)
                        ]
                        here = pl.ds(row + q * CHUNK, CHUNK)
                        zero = jnp.zeros((CHUNK, LANES), F32)
                        total[block, here, :] += jnp.where(low, zero, turned[0])
                        for j in range(1, pieces):
                            total[block + j, here, :] += jnp.where(low, turned[j - 1], turned[j])
                        total[block + pieces, here, :] += jnp.where(low, turned[-1], zero)

                return carry

            lax.fori_loop(0, info[source, 16], visit, 0)
    first = pr // LANES
    best = jnp.zeros((8, LANES), F32)
    for b in range(tile_cols // LANES):
        own = total[first + b, pr : pr + tile_rows, :]
        cover[:, b * LANES : (b + 1) * LANES] = own
        best = jnp.maximum(best, jnp.max(own.reshape(tile_rows // 8, 8, LANES), axis=0))
    peak[...] = jnp.full((8, LANES), jnp.max(best), F32)


def cover_call(place, info, probe, tile_rows, tile_cols, sides):
    pr = probe.shape[1]
    blocks = (tile_cols + 2 * pr) // LANES + 1
    return pl.pallas_call(
        functools.partial(cover_kernel, tile_rows, tile_cols, sides),
        out_shape=(
            jax.ShapeDtypeStruct((tile_rows, tile_cols), F32),
            jax.ShapeDtypeStruct((8, LANES), F32),
        ),
        in_specs=[SMEM, SMEM, VMEM],
        out_specs=(VMEM, VMEM),
        scratch_shapes=[
            pltpu.VMEM((blocks, tile_rows + 2 * pr, LANES), F32),
            pltpu.VMEM((pr // LANES, pr, LANES), F32),
        ],
        compiler_params=pltpu.CompilerParams(vmem_limit_bytes=24 << 20),
        cost_estimate=pl.CostEstimate(flops=4_000_000, bytes_accessed=8_000_000, transcendentals=0),
        name="cover",
    )(place, info, probe)


def positions_kernel(sides, *refs):
    place, rows, cols, count = refs[:4]
    tile, near, far_side = refs[4:7]
    side_in, near_corners, far_corners = [refs[7 + i * sides : 7 + (i + 1) * sides] for i in range(3)]
    probe, measured, left, right = refs[7 + 3 * sides : 11 + 3 * sides]
    outs = refs[11 + 3 * sides :]
    middle, near_rim, far_rim = outs[:3]
    side_out = outs[3 : 3 + sides]
    probe_sums = outs[3 + sides]
    ext, grad = outs[4 + sides : 6 + sides]
    scratch = outs[6 + sides :]
    patches, exits, stacks, wides, fields = [scratch[i * WAYS : (i + 1) * WAYS] for i in range(5)]

    pr = probe.shape[1]
    pieces = pr // LANES
    tile_rows, tile_cols = tile.shape[1:]
    ext_rows = tile_rows + 2 * H
    blocks = (tile_cols + 2 * H) // LANES
    own_blocks = tile_cols // LANES
    even = place[0] % 2 == 0
    near_row = pl.multiple_of(jnp.where(even, tile_rows + H, 0), 8)
    far_row = pl.multiple_of(jnp.where(even, 0, tile_rows + H), 8)
    side_blocks = [side_block(place, s, sides, blocks) for s in range(sides)]
    own, near_rows, far_rows = pl.ds(H, tile_rows), pl.ds(near_row, H), pl.ds(far_row, H)
    for ch in range(2):
        if sides == 1:
            ext[ch * blocks + blocks - 1 - side_blocks[0]] = jnp.zeros((ext_rows, LANES), F32)
        for b in range(own_blocks):
            at, cut = ch * blocks + 1 + b, slice(b * LANES, (b + 1) * LANES)
            ext[at, own, :] = tile[ch, :, cut]
            ext[at, near_rows, :] = near[ch, 0:H, cut]
            ext[at, far_rows, :] = far_side[ch, 0:H, cut]
        for s in range(sides):
            at = ch * blocks + side_blocks[s]
            ext[at, own, :] = side_in[s][ch, 0:tile_rows, :]
            ext[at, near_rows, :] = near_corners[s][ch, 0:H, :]
            ext[at, far_rows, :] = far_corners[s][ch, 0:H, :]
    grad[...] = jnp.zeros_like(grad)
    probe_sums[...] = jnp.zeros_like(probe_sums)
    lanes = lax.broadcasted_iota(jnp.int32, (CHUNK, LANES), 1)

    def put(stack, value, part, q, first):
        width = value.shape[1]
        high, low = split(value)
        rows_at = lambda block: slice(block * pr + q * CHUNK, block * pr + (q + 1) * CHUNK)
        here, there = slice(first, first + width), slice(pr + first, pr + first + width)
        if part == 0:
            stack[rows_at(0), here], stack[rows_at(1), there] = high, high
            stack[rows_at(2), here], stack[rows_at(3), there] = low, low
        else:
            stack[rows_at(0), there], stack[rows_at(1), here] = high, -high
            stack[rows_at(2), there], stack[rows_at(3), here] = low, -low

    def times_left(w):
        stack = jnp.concatenate([stacks[w][...], stacks[w][0 : 2 * pr]], axis=0)
        fields[w][...] = jnp.dot(left[...], stack, preferred_element_type=F32)

    def times_right(w):
        for q in range(pr // CHUNK):
            cut = slice(q * CHUNK, (q + 1) * CHUNK)
            high, low = split(fields[w][cut, :])
            wides[w][cut, 0 : 2 * pr] = high
            wides[w][cut, 2 * pr : 4 * pr] = low
        stack = jnp.concatenate([wides[w][...], wides[w][:, 0 : 2 * pr]], axis=1)
        fields[w][...] = jnp.dot(stack, right[...], preferred_element_type=F32)

    def load(w, k):
        row, col = rows[0, 0, k], cols[0, 0, k]
        shift, block = col & (LANES - 1), col >> 7
        back = (LANES - shift) & (LANES - 1)
        keep = lanes < LANES - shift
        for q in range(pr // CHUNK):
            cut = slice(q * CHUNK, (q + 1) * CHUNK)
            here = pl.ds(row + q * CHUNK, CHUNK)
            seen = []
            for ch in range(2):
                turned = [
                    pltpu.roll(ext[ch * blocks + block + j, here, :], back, 1)
                    for j in range(pieces + 1)
                ]
                seen.append([jnp.where(keep, turned[j], turned[j + 1]) for j in range(pieces)])
            for j in range(pieces):
                part = slice(j * LANES, (j + 1) * LANES)
                probe_real, probe_imag = probe[0, cut, part], probe[1, cut, part]
                real, imag = seen[0][j], seen[1][j]
                patches[w][0, cut, part], patches[w][1, cut, part] = real, imag
                exit_real = probe_real * real - probe_imag * imag
                exit_imag = probe_real * imag + probe_imag * real
                exits[w][0, cut, part], exits[w][1, cut, part] = exit_real, exit_imag
                put(stacks[w], exit_real, 0, q, j * LANES)
                put(stacks[w], exit_imag, 1, q, j * LANES)

    def project(w, k):
        for q in range(pr // CHUNK):
            cut = slice(q * CHUNK, (q + 1) * CHUNK)
            real, imag = fields[w][cut, 0:pr], fields[w][cut, pr : 2 * pr]
            factor = jnp.sqrt(measured[0, 0, k, cut, :]) * lax.rsqrt(real * real + imag * imag + 1.0)
            put(stacks[w], real * factor, 0, q, 0)
            put(stacks[w], -(imag * factor), 1, q, 0)

    def finish(w, k, live):
        row, col = rows[0, 0, k], cols[0, 0, k]
        shift, block = col & (LANES - 1), col >> 7
        low = lanes < shift
        zero = jnp.zeros((CHUNK, LANES), F32)
        for q in range(pr // CHUNK):
            cut = slice(q * CHUNK, (q + 1) * CHUNK)
            here = pl.ds(row + q * CHUNK, CHUNK)
            turned = [[], []]
            for j in range(pieces):
                part = slice(j * LANES, (j + 1) * LANES)
                other = slice(pr + j * LANES, pr + (j + 1) * LANES)
                diff_real = fields[w][cut, part] - exits[w][0, cut, part]
                diff_imag = -fields[w][cut, other] - exits[w][1, cut, part]
                real, imag = patches[w][0, cut, part], patches[w][1, cut, part]
                weight = real * real + imag * imag
                if live is not None:
                    diff_real, diff_imag = diff_real * live, diff_imag * live
                    weight = weight * live
                probe_real, probe_imag = probe[0, cut, part], probe[1, cut, part]
                turned[0].append(pltpu.roll(probe_real * diff_real + probe_imag * diff_imag, shift, 1))
                turned[1].append(pltpu.roll(probe_real * diff_imag - probe_imag * diff_real, shift, 1))
                probe_sums[j, 0, cut, :] += real * diff_real + imag * diff_imag
                probe_sums[j, 1, cut, :] += real * diff_imag - imag * diff_real
                probe_sums[j, 2, cut, :] += weight
            for ch in range(2):
                at = ch * blocks + block
                grad[at, here, :] += jnp.where(low, zero, turned[ch][0])
                for j in range(1, pieces):
                    grad[at + j, here, :] += jnp.where(low, turned[ch][j - 1], turned[ch][j])
                grad[at + pieces, here, :] += jnp.where(low, turned[ch][-1], zero)

    live_slots = count[0, 0]

    def visit(i, carry):
        slots = [jnp.minimum(i * WAYS + w, live_slots - 1) for w in range(WAYS)]
        lives = [None] + [jnp.where(i * WAYS + w < live_slots, 1.0, 0.0) for w in range(1, WAYS)]
        for w in range(WAYS):
            load(w, slots[w])
            times_left(w)
        for w in range(WAYS):
            times_right(w)
        for w in range(WAYS):
            project(w, slots[w])
            times_left(w)
        for w in range(WAYS):
            times_right(w)
        for w in range(WAYS):
            finish(w, slots[w], lives[w])
        return carry

    lax.fori_loop(0, (live_slots + WAYS - 1) // WAYS, visit, 0)
    for ch in range(2):
        for b in range(own_blocks):
            at, cut = ch * blocks + 1 + b, slice(b * LANES, (b + 1) * LANES)
            middle[ch, :, cut] = grad[at, own, :]
            near_rim[ch, :, cut] = grad[at, near_rows, :]
            far_rim[ch, :, cut] = grad[at, far_rows, :]
        for s in range(sides):
            at = ch * blocks + side_blocks[s]
            cut = slice(tile_cols + s * LANES, tile_cols + (s + 1) * LANES)
            side_out[s][ch] = grad[at, own, :]
            near_rim[ch, :, cut] = grad[at, near_rows, :]
            far_rim[ch, :, cut] = grad[at, far_rows, :]


def positions_call(
    place, rows, cols, count, tile, near, far_side, side_in, near_corners, far_corners, probe, measured
):
    pr = probe.shape[1]
    sides = len(side_in)
    tile_rows, tile_cols = tile.shape[1:]
    ext_rows = tile_rows + 2 * H
    blocks = (tile_cols + 2 * H) // LANES
    left, right = dft_tables(pr)
    shape = lambda *dims: jax.ShapeDtypeStruct(dims, F32)
    slots = measured.shape[2]
    return pl.pallas_call(
        functools.partial(positions_kernel, sides),
        out_shape=(
            shape(2, tile_rows, tile_cols),
            shape(2, H, tile_cols + sides * LANES),
            shape(2, H, tile_cols + sides * LANES),
            *[shape(2, tile_rows, LANES)] * sides,
            shape(pr // LANES, 3, pr, LANES),
        ),
        in_specs=[SMEM] * 4 + [VMEM] * (7 + 3 * sides),
        out_specs=(VMEM,) * (4 + sides),
        scratch_shapes=[
            pltpu.VMEM((2 * blocks, ext_rows, LANES), F32),
            pltpu.VMEM((2 * blocks, ext_rows, LANES), F32),
            *[pltpu.VMEM((2, pr, pr), F32)] * (2 * WAYS),
            *[pltpu.VMEM((4 * pr, 2 * pr), BF)] * WAYS,
            *[pltpu.VMEM((pr, 4 * pr), BF)] * WAYS,
            *[pltpu.VMEM((pr, 2 * pr), F32)] * WAYS,
        ],
        compiler_params=pltpu.CompilerParams(vmem_limit_bytes=28 << 20),
        cost_estimate=pl.CostEstimate(
            flops=slots * 96 * pr * pr * pr, bytes_accessed=16_000_000, transcendentals=slots * 2 * pr * pr
        ),
        name="positions",
    )(place, rows, cols, count, tile, near, far_side, *side_in, *near_corners, *far_corners, probe, measured,
      jnp.asarray(left), jnp.asarray(right))


def update_kernel(sides, *refs):
    place, tile, middle, cover, peak, near, far_side = refs[:7]
    side_in = refs[7 : 7 + sides]
    own_terms, other_terms, probe, out, new_probe, sums = refs[7 + sides :]
    tile_rows, tile_cols = tile.shape[1:]
    own_blocks = tile_cols // LANES
    even = place[0] % 2 == 0
    sums[...] = middle[...]
    near_row = pl.multiple_of(jnp.where(even, tile_rows - H, 0), 8)
    far_row = pl.multiple_of(jnp.where(even, 0, tile_rows - H), 8)
    sums[:, pl.ds(near_row, H), :] += near[:, :, 0:tile_cols]
    sums[:, pl.ds(far_row, H), :] += far_side[:, :, 0:tile_cols]
    for s in range(sides):
        if sides == 1:
            for edge, where in ((0, own_blocks - 1), (1, 0)):

                @pl.when((place[1] == 0) == (edge == 0))
                def _():
                    sums[:, :, where * LANES : (where + 1) * LANES] += side_in[s][...]
        else:
            where = 0 if s == 0 else own_blocks - 1
            sums[:, :, where * LANES : (where + 1) * LANES] += side_in[s][...]
    rows = own_terms.shape[0]
    top = MIX_OBJECT * jnp.maximum(peak[0:1, 0:1], other_terms[rows : rows + 1, 0:1])
    inverse = 1.0 / ((1.0 - MIX_OBJECT) * cover[...] + top)
    for ch in range(2):
        out[ch] = tile[ch] + sums[ch] * inverse

    pr = probe.shape[1]
    pieces = pr // LANES
    both = (own_terms, other_terms)

    def update(parts):
        flat = [parts[j * len(parts) // pieces] for j in range(pieces)]
        span = flat[0].shape[0] // (pieces // len(parts))
        term = lambda j, ch: flat[j][(j % (pieces // len(parts))) * span + ch * pr :][:pr]
        weights = [term(j, 2) for j in range(pieces)]
        best = functools.reduce(jnp.maximum, weights)
        best = jnp.max(jnp.max(best.reshape(-1, 8, LANES), axis=0), keepdims=True)
        for j in range(pieces):
            cut = slice(j * LANES, (j + 1) * LANES)
            scale = 1.0 / ((1.0 - MIX_PROBE) * weights[j] + MIX_PROBE * best)
            for ch in range(2):
                new_probe[ch, :, cut] = probe[ch, :, cut] + term(j, ch) * scale

    for first in (0, 1):

        @pl.when(place[0] % 2 == first)
        def _():
            update([both[first][0:rows, :], both[1 - first][0:rows, :]])


def update_call(place, tile, middle, cover, peak, near, far_side, side_in, own_terms, other_terms, probe):
    sides = len(side_in)
    return pl.pallas_call(
        functools.partial(update_kernel, sides),
        out_shape=(jax.ShapeDtypeStruct(tile.shape, F32), jax.ShapeDtypeStruct(probe.shape, F32)),
        in_specs=[SMEM] + [VMEM] * (9 + sides),
        out_specs=(VMEM, VMEM),
        scratch_shapes=[pltpu.VMEM(tile.shape, F32)],
        compiler_params=pltpu.CompilerParams(vmem_limit_bytes=32 << 20),
        name="update",
    )(place, tile, middle, cover, peak, near, far_side, *side_in, own_terms, other_terms, probe)


def swap(x, axis, first):
    size = lax.axis_size(axis)
    pairs = []
    for i in range(first, size - 1, 2):
        pairs += [(i, i + 1), (i + 1, i)]
    return lax.ppermute(x, axis, pairs)


def shifted(x, axis, by):
    size = lax.axis_size(axis)
    return lax.ppermute(x, axis, [(i, i + by) for i in range(size) if 0 <= i + by < size])


def to_sides(pieces):
    if len(pieces) == 1:
        return [swap(pieces[0], "narrow", 0)]
    return [shifted(pieces[1], "narrow", 1), shifted(pieces[0], "narrow", -1)]


def bits_of(axis):
    size = lax.axis_size(axis)
    return [1 << b for b in range(size.bit_length() - 1)]


def partner(x, axis, bit):
    size = lax.axis_size(axis)
    return lax.ppermute(x, axis, [(i, i ^ bit) for i in range(size)])


def half_of(x, which):
    rows = x.shape[0] // 2
    return lax.dynamic_slice_in_dim(x, which * rows, rows, axis=0)


def bit_state(axis, bit):
    return (lax.axis_index(axis) // bit) % 2


def halve(terms, axis, bit):
    mine = bit_state(axis, bit)
    return half_of(terms, mine) + partner(half_of(terms, 1 - mine), axis, bit)


def double(terms, peak, axis, bit):
    got = partner(jnp.concatenate([terms, peak], axis=0), axis, bit)
    rows = terms.shape[0]
    return terms + got[:rows], jnp.maximum(peak, got[rows:])


def gather(terms, peak, axis, bit):
    first = bit_state(axis, bit) == 0
    got = partner(jnp.concatenate([terms, peak], axis=0), axis, bit)
    rows = terms.shape[0]
    other, peak = got[:rows], jnp.maximum(peak, got[rows:])
    return jnp.concatenate([jnp.where(first, terms, other), jnp.where(first, other, terms)], axis=0), peak


def to_corners(bands, first):
    wide, narrow = lax.axis_size("wide"), lax.axis_size("narrow")
    steps = [0] if len(bands) == 1 else [-1, 1]
    got = []
    for s, step in enumerate(steps):
        pairs = []
        for i in range(first, wide - 1, 2):
            for n in range(narrow):
                m = 1 - n if step == 0 else n - step
                if 0 <= m < narrow:
                    pairs += [(i * narrow + n, (i + 1) * narrow + m), ((i + 1) * narrow + n, i * narrow + m)]
        band = bands[0] if step == 0 else bands[1 - s]
        got.append(lax.ppermute(band, ("wide", "narrow"), pairs))
    return got


def after(x, *others):
    return lax.optimization_barrier((x, *others))[0]


def body(tile, probe, measured, rows, cols, counts):
    wide, narrow = lax.axis_index("wide"), lax.axis_index("narrow")
    sides = 1 if lax.axis_size("narrow") == 2 else 2
    tile_rows, tile_cols = tile.shape[1:]
    even = wide % 2 == 0
    place = jnp.stack([wide, narrow]).astype(jnp.int32)

    own_info = jnp.concatenate(
        [rows.reshape(-1), cols.reshape(-1), counts.reshape(-1), jnp.zeros((LANES - 17,), jnp.int32)]
    ).astype(F32)
    info_rows = jnp.broadcast_to(own_info, (2, INFO, LANES))

    near_start = jnp.where(even, tile_rows - H, 0)
    far_start = jnp.where(even, 0, tile_rows - H)
    side_start = jnp.where(narrow == 0, tile_cols - H, 0)
    side_starts = [side_start] if sides == 1 else [0, tile_cols - H]

    def cut_out(row, height, col, width):
        piece = lax.dynamic_slice(tile, (0, row, col), (2, height, width))
        notes = jnp.pad(info_rows, ((0, 0), (0, 0), (0, width - LANES)))
        return jnp.concatenate([piece, notes], axis=1)

    far_band = cut_out(far_start, H, 0, tile_cols)
    near_band = cut_out(near_start, H, 0, tile_cols)
    edges = [cut_out(0, tile_rows, start, H) for start in side_starts]
    far_ends = [cut_out(far_start, H, start, H) for start in side_starts]
    near_ends = [cut_out(near_start, H, start, H) for start in side_starts]
    far_band, near_band, edges, far_ends, near_ends = lax.optimization_barrier(
        (far_band, near_band, edges, far_ends, near_ends)
    )
    far_side = swap(far_band, "wide", 1)
    far_corners = to_corners(far_ends, 1)
    side_in = to_sides(edges)
    near_corners = to_corners(near_ends, 0)
    near = swap(near_band, "wide", 0)

    out = positions_call(place, rows, cols, counts, tile, near, far_side, side_in, near_corners, far_corners, probe, measured)
    middle, near_rim, far_rim = out[:3]
    side_rims, probe_sums = list(out[3 : 3 + sides]), out[3 + sides]

    terms = probe_sums.reshape(-1, LANES)
    wide_bits, narrow_bits = bits_of("wide"), bits_of("narrow")
    terms = halve(terms, "wide", wide_bits[0])
    near_got = swap(after(near_rim, terms), "wide", 0)
    notes = [side_in[s][0, tile_rows:] for s in range(sides)]
    notes += [near[0, H:, :LANES]] + [c[0, H:] for c in near_corners]
    notes += [far_side[0, H:, :LANES]] + [c[0, H:] for c in far_corners]
    info = jnp.stack([own_info[:32]] + [x[0, :32] for x in notes]).astype(jnp.int32)
    cover, peak = cover_call(place, after(info, terms), probe, tile_rows, tile_cols, sides)
    terms = halve(terms, "wide", wide_bits[1])
    far_got = swap(after(far_rim, terms), "wide", 1)
    for bit in narrow_bits:
        terms = halve(terms, "narrow", bit)
    for bit in wide_bits[2:]:
        terms, peak = double(terms, peak, "wide", bit)
    for bit in narrow_bits[::-1]:
        terms, peak = gather(terms, peak, "narrow", bit)

    def with_rims(piece, s):
        cut = slice(tile_cols + s * LANES, tile_cols + (s + 1) * LANES)
        below = jnp.where(even, near_got[:, :, cut], far_got[:, :, cut])
        above = jnp.where(even, far_got[:, :, cut], near_got[:, :, cut])
        return piece + jnp.concatenate([above, below], axis=1)

    side_got = to_sides([with_rims(piece, s) for s, piece in enumerate(side_rims)])
    terms, peak = gather(terms, peak, "wide", wide_bits[1])
    other_terms = partner(jnp.concatenate([terms, peak], axis=0), "wide", wide_bits[0])
    return update_call(
        place, tile, middle, cover, peak, near_got, far_got, side_got, terms, other_terms, probe
    )


def solution(mesh):
    placed = (
        P(None, "wide", "narrow"),
        P(),
        P("wide", "narrow", None, None, None),
        P("wide", "narrow", None),
        P("wide", "narrow", None),
        P("wide", "narrow"),
    )
    return jax.shard_map(
        body,
        mesh=mesh,
        in_specs=placed,
        out_specs=(P(None, "wide", "narrow"), P()),
        check_vma=False,
    )
```

```python
import functools
import math

import jax
import jax.numpy as jnp
import ml_dtypes
import numpy as np
from jax import lax
from jax.experimental import pallas as pl
from jax.experimental.pallas import tpu as pltpu
from jax.sharding import PartitionSpec as P

H = 128
LANES = 128
CHUNK = 32
WAYS = 2
INFO = 8
BF = jnp.bfloat16
F32 = jnp.float32
MIX_OBJECT = 0.5
MIX_PROBE = 0.5
VMEM = pl.BlockSpec(memory_space=pltpu.VMEM)
SMEM = pl.BlockSpec(memory_space=pltpu.SMEM)
ANY = pl.BlockSpec(memory_space=pl.ANY)


def rounded_pair(table):
    table = table.astype(np.float32)
    high = table.astype(ml_dtypes.bfloat16)
    low = (table - high.astype(np.float32)).astype(ml_dtypes.bfloat16)
    return high, low


def dft_tables(length):
    index = np.arange(length)
    angle = 2.0 * np.pi * ((index[:, None] * index[None, :]) % length) / length
    cos_high, cos_low = rounded_pair(np.cos(angle) / math.sqrt(length))
    sin_high, sin_low = rounded_pair(-np.sin(angle) / math.sqrt(length))
    left = np.concatenate([cos_high, sin_high, cos_high, sin_high, cos_low, sin_low], axis=1)
    right_high = np.block([[cos_high, sin_high], [-sin_high, cos_high]])
    right_low = np.block([[cos_low, sin_low], [-sin_low, cos_low]])
    right = np.concatenate([right_high, right_high, right_low], axis=0)
    return left, right


def split(x):
    high = x.astype(BF)
    return high, (x - high.astype(F32)).astype(BF)


def side_block(place, side, sides, blocks):
    if sides == 1:
        return jnp.where(place[1] == 0, blocks - 1, 0)
    return 0 if side == 0 else blocks - 1


def side_step(place, side, sides):
    if sides == 1:
        return jnp.where(place[1] == 0, 1, -1)
    return -1 if side == 0 else 1


def cover_kernel(tile_rows, tile_cols, sides, place, info, probe, cover, peak, total, power):
    pr = probe.shape[1]
    pieces = pr // LANES
    for j in range(pieces):
        cut = slice(j * LANES, (j + 1) * LANES)
        power[j] = probe[0, :, cut] * probe[0, :, cut] + probe[1, :, cut] * probe[1, :, cut]
    total[...] = jnp.zeros_like(total)
    lanes = lax.broadcasted_iota(jnp.int32, (CHUNK, LANES), 1)
    even = place[0] % 2 == 0
    steps_down = (0, jnp.where(even, 1, -1), jnp.where(even, -1, 1))
    steps_right = (0,) + tuple(side_step(place, s, sides) for s in range(sides))
    for v in range(3):
        for h in range(1 + sides):
            source = v * (1 + sides) + h
            down, right = steps_down[v], steps_right[h]

            def visit(k, carry):
                row = info[source, k] + pr - H + down * tile_rows
                col = info[source, 8 + k] + pr - H + right * tile_cols
                inside = (row > 0) & (row < pr + tile_rows) & (col > 0) & (col < pr + tile_cols)

                @pl.when(inside)
                def _():
                    shift = col & (LANES - 1)
                    block = col >> 7
                    low = lanes < shift
                    for q in range(pr // CHUNK):
                        turned = [
                            pltpu.roll(power[j, q * CHUNK : (q + 1) * CHUNK, :], shift, 1)
                            for j in range(pieces)
                        ]
                        here = pl.ds(row + q * CHUNK, CHUNK)
                        zero = jnp.zeros((CHUNK, LANES), F32)
                        total[block, here, :] += jnp.where(low, zero, turned[0])
                        for j in range(1, pieces):
                            total[block + j, here, :] += jnp.where(low, turned[j - 1], turned[j])
                        total[block + pieces, here, :] += jnp.where(low, turned[-1], zero)

                return carry

            lax.fori_loop(0, info[source, 16], visit, 0)
    first = pr // LANES
    best = jnp.zeros((8, LANES), F32)
    for b in range(tile_cols // LANES):
        own = total[first + b, pr : pr + tile_rows, :]
        cover[:, b * LANES : (b + 1) * LANES] = own
        best = jnp.maximum(best, jnp.max(own.reshape(tile_rows // 8, 8, LANES), axis=0))
    peak[...] = jnp.full((8, LANES), jnp.max(best), F32)


def cover_call(place, info, probe, tile_rows, tile_cols, sides):
    pr = probe.shape[1]
    blocks = (tile_cols + 2 * pr) // LANES + 1
    return pl.pallas_call(
        functools.partial(cover_kernel, tile_rows, tile_cols, sides),
        out_shape=(
            jax.ShapeDtypeStruct((tile_rows, tile_cols), F32),
            jax.ShapeDtypeStruct((8, LANES), F32),
        ),
        in_specs=[SMEM, SMEM, VMEM],
        out_specs=(VMEM, VMEM),
        scratch_shapes=[
            pltpu.VMEM((blocks, tile_rows + 2 * pr, LANES), F32),
            pltpu.VMEM((pr // LANES, pr, LANES), F32),
        ],
        compiler_params=pltpu.CompilerParams(vmem_limit_bytes=24 << 20),
        cost_estimate=pl.CostEstimate(flops=4_000_000, bytes_accessed=8_000_000, transcendentals=0),
        name="cover",
    )(place, info, probe)


def pack_kernel(sides, place, rows, cols, count, tile, *refs):
    far_band, near_band = refs[:2]
    edges, far_ends, near_ends = [refs[2 + i * sides : 2 + (i + 1) * sides] for i in range(3)]
    sems = refs[2 + 3 * sides]
    tile_rows, tile_cols = tile.shape[1:]
    even = place[0] % 2 == 0
    near_start = pl.multiple_of(jnp.where(even, tile_rows - H, 0), 8)
    far_start = pl.multiple_of(jnp.where(even, 0, tile_rows - H), 8)
    if sides == 1:
        starts = [pl.multiple_of(jnp.where(place[1] == 0, tile_cols - H, 0), LANES)]
    else:
        starts = [0, tile_cols - H]
    bands = [(far_band, far_start, H, 0), (near_band, near_start, H, 0)]
    for s, start in enumerate(starts):
        bands += [(edges[s], 0, tile_rows, start), (far_ends[s], far_start, H, start)]
        bands += [(near_ends[s], near_start, H, start)]
    copies = []
    for i, (band, row, height, col) in enumerate(bands):
        copies.append(
            pltpu.make_async_copy(
                tile.at[:, pl.ds(row, height), pl.ds(col, band.shape[2])], band.at[:, pl.ds(0, height), :], sems.at[i]
            )
        )
        copies[-1].start()
    lanes = lax.broadcasted_iota(jnp.int32, (INFO, LANES), 1)
    notes = jnp.where(lanes == 16, count[0, 0], 0)
    for k in range(rows.shape[2]):
        notes = jnp.where(lanes == k, rows[0, 0, k], jnp.where(lanes == 8 + k, cols[0, 0, k], notes))
    notes = notes.astype(F32)
    for band, row, height, col in bands:
        for ch in range(2):
            band[ch, height : height + INFO, 0:LANES] = notes
            if band.shape[2] > LANES:
                band[ch, height : height + INFO, LANES:] = jnp.zeros((INFO, band.shape[2] - LANES), F32)
    for copy in copies:
        copy.wait()


def pack_call(place, rows, cols, count, tile, sides):
    tile_rows, tile_cols = tile.shape[1:]
    shape = lambda height, width: jax.ShapeDtypeStruct((2, height + INFO, width), F32)
    shapes = [shape(H, tile_cols)] * 2 + [shape(tile_rows, LANES)] * sides + [shape(H, LANES)] * (2 * sides)
    out = pl.pallas_call(
        functools.partial(pack_kernel, sides),
        out_shape=shapes,
        in_specs=[SMEM] * 4 + [ANY],
        out_specs=[VMEM] * len(shapes),
        scratch_shapes=[pltpu.SemaphoreType.DMA((len(shapes),))],
        compiler_params=pltpu.CompilerParams(vmem_limit_bytes=8 << 20),
        name="pack",
    )(place, rows, cols, count, tile)
    return out[0], out[1], *[list(out[2 + i * sides : 2 + (i + 1) * sides]) for i in range(3)]


def positions_kernel(sides, last, *refs):
    place, rows, cols, count = refs[:4]
    if last:
        ext, grad_in, sums_in, probe, measured, left_in, right_in = refs[4:11]
        outs = refs[11:]
        middle, near_rim = outs[:2]
        side_out = outs[2 : 2 + sides]
        probe_sums = outs[2 + sides]
        grad = outs[3 + sides]
        scratch = outs[4 + sides :]
    else:
        tile, near, far_side = refs[4:7]
        side_in, near_corners, far_corners = [refs[7 + i * sides : 7 + (i + 1) * sides] for i in range(3)]
        probe, measured, left_in, right_in = refs[7 + 3 * sides : 11 + 3 * sides]
        far_rim, info, ext, grad, probe_sums = refs[11 + 3 * sides : 16 + 3 * sides]
        scratch = refs[16 + 3 * sides :]
    left, right, levels, order = scratch[:4]
    table_sems, level_sems, ext_sems = scratch[4:7]
    scratch = scratch[7:]
    patches, exits, stacks, wides, fields = [scratch[i * WAYS : (i + 1) * WAYS] for i in range(5)]

    pr = probe.shape[1]
    pieces = pr // LANES
    ext_rows = ext.shape[1]
    blocks = ext.shape[0] // 2
    own_blocks = blocks - 2
    tile_rows, tile_cols = ext_rows - 2 * H, own_blocks * LANES
    even = place[0] % 2 == 0
    near_row = pl.multiple_of(jnp.where(even, tile_rows + H, 0), 8)
    far_row = pl.multiple_of(jnp.where(even, 0, tile_rows + H), 8)
    side_blocks = [side_block(place, s, sides, blocks) for s in range(sides)]
    own, near_rows, far_rows = pl.ds(H, tile_rows), pl.ds(near_row, H), pl.ds(far_row, H)

    copies = []

    def fetch(source, target):
        copies.append(pltpu.make_async_copy(source, target, ext_sems.at[len(copies)]))
        copies[-1].start()

    if not last:
        for ch in range(2):
            for b in range(own_blocks):
                at, cut = ch * blocks + 1 + b, pl.ds(b * LANES, LANES)
                fetch(tile.at[ch, :, cut], ext.at[at, own, :])
                fetch(near.at[ch, pl.ds(0, H), cut], ext.at[at, near_rows, :])
                fetch(far_side.at[ch, pl.ds(0, H), cut], ext.at[at, far_rows, :])
            for s in range(sides):
                at = ch * blocks + side_blocks[s]
                fetch(side_in[s].at[ch, pl.ds(0, tile_rows), :], ext.at[at, own, :])
                fetch(near_corners[s].at[ch, pl.ds(0, H), :], ext.at[at, near_rows, :])
                fetch(far_corners[s].at[ch, pl.ds(0, H), :], ext.at[at, far_rows, :])
        for s in range(sides):
            fetch(side_in[s].at[0, pl.ds(tile_rows, INFO), :], info.at[s])
            fetch(near_corners[s].at[0, pl.ds(H, INFO), :], info.at[sides + 1 + s])
            fetch(far_corners[s].at[0, pl.ds(H, INFO), :], info.at[2 * sides + 2 + s])
        fetch(near.at[0, pl.ds(H, INFO), pl.ds(0, LANES)], info.at[sides])
        fetch(far_side.at[0, pl.ds(H, INFO), pl.ds(0, LANES)], info.at[2 * sides + 1])
    tables = [
        pltpu.make_async_copy(left_in, left, table_sems.at[0]),
        pltpu.make_async_copy(right_in, right, table_sems.at[1]),
    ]
    for copy in tables:
        copy.start()

    live_slots = count[0, 0]

    def touches(k):
        return jnp.where(even, rows[0, 0, k] < H, rows[0, 0, k] > tile_rows - H)

    def pick(wanted):
        def step(k, n):
            @pl.when(touches(k) == wanted)
            def _():
                order[n] = k

            return n + jnp.where(touches(k) == wanted, 1, 0)

        return step

    far_slots = lax.fori_loop(0, live_slots, pick(True), 0)
    lax.fori_loop(0, live_slots, pick(False), far_slots)
    border = jnp.minimum((far_slots + WAYS - 1) // WAYS * WAYS, live_slots)
    begin, end = (border, live_slots) if last else (0, border)

    def level_copy(i):
        return pltpu.make_async_copy(measured.at[0, 0, order[i]], levels.at[i], level_sems.at[i])

    def start_level(i, carry):
        level_copy(i).start()
        return carry

    lax.fori_loop(begin, end, start_level, 0)
    if last:
        grad[...] = grad_in[...]
        probe_sums[...] = sums_in[...]
    else:
        if sides == 1:
            for ch in range(2):
                ext[ch * blocks + blocks - 1 - side_blocks[0]] = jnp.zeros((ext_rows, LANES), F32)
        grad[...] = jnp.zeros_like(grad)
        probe_sums[...] = jnp.zeros_like(probe_sums)
    for copy in copies + tables:
        copy.wait()
    lanes = lax.broadcasted_iota(jnp.int32, (CHUNK, LANES), 1)

    def put(stack, value, part, q, first):
        width = value.shape[1]
        high, low = split(value)
        rows_at = lambda block: slice(block * pr + q * CHUNK, block * pr + (q + 1) * CHUNK)
        here, there = slice(first, first + width), slice(pr + first, pr + first + width)
        if part == 0:
            stack[rows_at(0), here], stack[rows_at(1), there] = high, high
            stack[rows_at(2), here], stack[rows_at(3), there] = low, low
        else:
            stack[rows_at(0), there], stack[rows_at(1), here] = high, -high
            stack[rows_at(2), there], stack[rows_at(3), here] = low, -low

    def times_left(w):
        stack = jnp.concatenate([stacks[w][...], stacks[w][0 : 2 * pr]], axis=0)
        fields[w][...] = jnp.dot(left[...], stack, preferred_element_type=F32)

    def times_right(w):
        for q in range(pr // CHUNK):
            cut = slice(q * CHUNK, (q + 1) * CHUNK)
            high, low = split(fields[w][cut, :])
            wides[w][cut, 0 : 2 * pr] = high
            wides[w][cut, 2 * pr : 4 * pr] = low
        stack = jnp.concatenate([wides[w][...], wides[w][:, 0 : 2 * pr]], axis=1)
        fields[w][...] = jnp.dot(stack, right[...], preferred_element_type=F32)

    def load(w, k):
        row, col = rows[0, 0, order[k]], cols[0, 0, order[k]]
        shift, block = col & (LANES - 1), col >> 7
        back = (LANES - shift) & (LANES - 1)
        keep = lanes < LANES - shift
        for q in range(pr // CHUNK):
            cut = slice(q * CHUNK, (q + 1) * CHUNK)
            here = pl.ds(row + q * CHUNK, CHUNK)
            seen = []
            for ch in range(2):
                turned = [
                    pltpu.roll(ext[ch * blocks + block + j, here, :], back, 1)
                    for j in range(pieces + 1)
                ]
                seen.append([jnp.where(keep, turned[j], turned[j + 1]) for j in range(pieces)])
            for j in range(pieces):
                part = slice(j * LANES, (j + 1) * LANES)
                probe_real, probe_imag = probe[0, cut, part], probe[1, cut, part]
                real, imag = seen[0][j], seen[1][j]
                patches[w][0, cut, part], patches[w][1, cut, part] = real, imag
                exit_real = probe_real * real - probe_imag * imag
                exit_imag = probe_real * imag + probe_imag * real
                exits[w][0, cut, part], exits[w][1, cut, part] = exit_real, exit_imag
                put(stacks[w], exit_real, 0, q, j * LANES)
                put(stacks[w], exit_imag, 1, q, j * LANES)

    def project(w, k):
        for q in range(pr // CHUNK):
            cut = slice(q * CHUNK, (q + 1) * CHUNK)
            real, imag = fields[w][cut, 0:pr], fields[w][cut, pr : 2 * pr]
            factor = jnp.sqrt(levels[k, cut, :]) * lax.rsqrt(real * real + imag * imag + 1.0)
            put(stacks[w], real * factor, 0, q, 0)
            put(stacks[w], -(imag * factor), 1, q, 0)

    def finish(w, k, live):
        row, col = rows[0, 0, order[k]], cols[0, 0, order[k]]
        shift, block = col & (LANES - 1), col >> 7
        low = lanes < shift
        zero = jnp.zeros((CHUNK, LANES), F32)
        for q in range(pr // CHUNK):
            cut = slice(q * CHUNK, (q + 1) * CHUNK)
            here = pl.ds(row + q * CHUNK, CHUNK)
            turned = [[], []]
            for j in range(pieces):
                part = slice(j * LANES, (j + 1) * LANES)
                other = slice(pr + j * LANES, pr + (j + 1) * LANES)
                diff_real = fields[w][cut, part] - exits[w][0, cut, part]
                diff_imag = -fields[w][cut, other] - exits[w][1, cut, part]
                real, imag = patches[w][0, cut, part], patches[w][1, cut, part]
                weight = real * real + imag * imag
                if live is not None:
                    diff_real, diff_imag = diff_real * live, diff_imag * live
                    weight = weight * live
                probe_real, probe_imag = probe[0, cut, part], probe[1, cut, part]
                turned[0].append(pltpu.roll(probe_real * diff_real + probe_imag * diff_imag, shift, 1))
                turned[1].append(pltpu.roll(probe_real * diff_imag - probe_imag * diff_real, shift, 1))
                probe_sums[j, 0, cut, :] += real * diff_real + imag * diff_imag
                probe_sums[j, 1, cut, :] += real * diff_imag - imag * diff_real
                probe_sums[j, 2, cut, :] += weight
            for ch in range(2):
                at = ch * blocks + block
                grad[at, here, :] += jnp.where(low, zero, turned[ch][0])
                for j in range(1, pieces):
                    grad[at + j, here, :] += jnp.where(low, turned[ch][j - 1], turned[ch][j])
                grad[at + pieces, here, :] += jnp.where(low, turned[ch][-1], zero)

    def visit(i, carry):
        first = begin + i * WAYS
        slots = [jnp.minimum(first + w, end - 1) for w in range(WAYS)]
        lives = [None] + [jnp.where(first + w < end, 1.0, 0.0) for w in range(1, WAYS)]
        for w in range(WAYS):

            @pl.when(first + w < end)
            def _():
                level_copy(slots[w]).wait()

        for w in range(WAYS):
            load(w, slots[w])
            times_left(w)
        for w in range(WAYS):
            times_right(w)
        for w in range(WAYS):
            project(w, slots[w])
            times_left(w)
        for w in range(WAYS):
            times_right(w)
        for w in range(WAYS):
            finish(w, slots[w], lives[w])
        return carry

    lax.fori_loop(0, (end - begin + WAYS - 1) // WAYS, visit, 0)
    for ch in range(2):
        for b in range(own_blocks):
            at, cut = ch * blocks + 1 + b, slice(b * LANES, (b + 1) * LANES)
            if last:
                middle[ch, :, cut] = grad[at, own, :]
                near_rim[ch, :, cut] = grad[at, near_rows, :]
            else:
                far_rim[ch, :, cut] = grad[at, far_rows, :]
        for s in range(sides):
            at = ch * blocks + side_blocks[s]
            cut = slice(tile_cols + s * LANES, tile_cols + (s + 1) * LANES)
            if last:
                side_out[s][ch] = grad[at, own, :]
                near_rim[ch, :, cut] = grad[at, near_rows, :]
            else:
                far_rim[ch, :, cut] = grad[at, far_rows, :]


def positions_calls(
    place, rows, cols, count, tile, near, far_side, side_in, near_corners, far_corners, probe, measured
):
    pr = probe.shape[1]
    sides = len(side_in)
    tile_rows, tile_cols = tile.shape[1:]
    ext_rows = tile_rows + 2 * H
    blocks = (tile_cols + 2 * H) // LANES
    left, right = (jnp.asarray(table) for table in dft_tables(pr))
    shape = lambda *dims: jax.ShapeDtypeStruct(dims, F32)
    slots = measured.shape[2]
    sums = shape(pr // LANES, 3, pr, LANES)
    field = shape(2 * blocks, ext_rows, LANES)
    rim = shape(2, H, tile_cols + sides * LANES)
    options = dict(
        compiler_params=pltpu.CompilerParams(vmem_limit_bytes=34 << 20),
        cost_estimate=pl.CostEstimate(
            flops=slots * 48 * pr * pr * pr, bytes_accessed=16_000_000, transcendentals=slots * pr * pr
        ),
    )
    scratch = [
        pltpu.VMEM(left.shape, BF),
        pltpu.VMEM(right.shape, BF),
        pltpu.VMEM((slots, pr, pr), F32),
        pltpu.SMEM((slots,), jnp.int32),
        pltpu.SemaphoreType.DMA((2,)),
        pltpu.SemaphoreType.DMA((slots,)),
        pltpu.SemaphoreType.DMA((6 * blocks + 3 * sides + 2,)),
        *[pltpu.VMEM((2, pr, pr), F32)] * (2 * WAYS),
        *[pltpu.VMEM((4 * pr, 2 * pr), BF)] * WAYS,
        *[pltpu.VMEM((pr, 4 * pr), BF)] * WAYS,
        *[pltpu.VMEM((pr, 2 * pr), F32)] * WAYS,
    ]
    far_rim, info, ext, grad, probe_sums = pl.pallas_call(
        functools.partial(positions_kernel, sides, False),
        out_shape=(rim, shape(3 * sides + 2, INFO, LANES), field, field, sums),
        in_specs=[SMEM] * 4 + [ANY] * (3 + 3 * sides) + [VMEM, ANY, ANY, ANY],
        out_specs=(VMEM,) * 5,
        scratch_shapes=scratch,
        name="positions_far",
        **options,
    )(place, rows, cols, count, tile, near, far_side, *side_in, *near_corners, *far_corners, probe, measured, left, right)
    out = pl.pallas_call(
        functools.partial(positions_kernel, sides, True),
        out_shape=(shape(2, tile_rows, tile_cols), rim, *[shape(2, tile_rows, LANES)] * sides, sums),
        in_specs=[SMEM] * 4 + [VMEM] * 4 + [ANY] * 3,
        out_specs=(VMEM,) * (3 + sides),
        scratch_shapes=[pltpu.VMEM(field.shape, F32)] + scratch,
        name="positions_near",
        **options,
    )(place, rows, cols, count, ext, grad, probe_sums, probe, measured, left, right)
    return out[0], out[1], far_rim, list(out[2 : 2 + sides]), out[2 + sides], info


def update_kernel(sides, *refs):
    place, tile, middle, cover, peak, near, far_side = refs[:7]
    side_in = refs[7 : 7 + sides]
    own_terms, other_terms, probe, out, new_probe, sums = refs[7 + sides :]
    tile_rows, tile_cols = tile.shape[1:]
    own_blocks = tile_cols // LANES
    even = place[0] % 2 == 0
    sums[...] = middle[...]
    near_row = pl.multiple_of(jnp.where(even, tile_rows - H, 0), 8)
    far_row = pl.multiple_of(jnp.where(even, 0, tile_rows - H), 8)
    sums[:, pl.ds(near_row, H), :] += near[:, :, 0:tile_cols]
    sums[:, pl.ds(far_row, H), :] += far_side[:, :, 0:tile_cols]
    for s in range(sides):
        if sides == 1:
            for edge, where in ((0, own_blocks - 1), (1, 0)):

                @pl.when((place[1] == 0) == (edge == 0))
                def _():
                    sums[:, :, where * LANES : (where + 1) * LANES] += side_in[s][...]
        else:
            where = 0 if s == 0 else own_blocks - 1
            sums[:, :, where * LANES : (where + 1) * LANES] += side_in[s][...]
    rows = own_terms.shape[0]
    top = MIX_OBJECT * jnp.maximum(peak[0:1, 0:1], other_terms[rows : rows + 1, 0:1])
    inverse = 1.0 / ((1.0 - MIX_OBJECT) * cover[...] + top)
    for ch in range(2):
        out[ch] = tile[ch] + sums[ch] * inverse

    pr = probe.shape[1]
    pieces = pr // LANES
    both = (own_terms, other_terms)

    def update(parts):
        flat = [parts[j * len(parts) // pieces] for j in range(pieces)]
        span = flat[0].shape[0] // (pieces // len(parts))
        term = lambda j, ch: flat[j][(j % (pieces // len(parts))) * span + ch * pr :][:pr]
        weights = [term(j, 2) for j in range(pieces)]
        best = functools.reduce(jnp.maximum, weights)
        best = jnp.max(jnp.max(best.reshape(-1, 8, LANES), axis=0), keepdims=True)
        for j in range(pieces):
            cut = slice(j * LANES, (j + 1) * LANES)
            scale = 1.0 / ((1.0 - MIX_PROBE) * weights[j] + MIX_PROBE * best)
            for ch in range(2):
                new_probe[ch, :, cut] = probe[ch, :, cut] + term(j, ch) * scale

    for first in (0, 1):

        @pl.when(place[0] % 2 == first)
        def _():
            update([both[first][0:rows, :], both[1 - first][0:rows, :]])


def update_call(place, tile, middle, cover, peak, near, far_side, side_in, own_terms, other_terms, probe):
    sides = len(side_in)
    return pl.pallas_call(
        functools.partial(update_kernel, sides),
        out_shape=(jax.ShapeDtypeStruct(tile.shape, F32), jax.ShapeDtypeStruct(probe.shape, F32)),
        in_specs=[SMEM] + [VMEM] * (9 + sides),
        out_specs=(VMEM, VMEM),
        scratch_shapes=[pltpu.VMEM(tile.shape, F32)],
        compiler_params=pltpu.CompilerParams(vmem_limit_bytes=32 << 20),
        name="update",
    )(place, tile, middle, cover, peak, near, far_side, *side_in, own_terms, other_terms, probe)


def swap(x, axis, first):
    size = lax.axis_size(axis)
    pairs = []
    for i in range(first, size - 1, 2):
        pairs += [(i, i + 1), (i + 1, i)]
    return lax.ppermute(x, axis, pairs)


def shifted(x, axis, by):
    size = lax.axis_size(axis)
    return lax.ppermute(x, axis, [(i, i + by) for i in range(size) if 0 <= i + by < size])


def to_sides(pieces):
    if len(pieces) == 1:
        return [swap(pieces[0], "narrow", 0)]
    return [shifted(pieces[1], "narrow", 1), shifted(pieces[0], "narrow", -1)]


def bits_of(axis):
    size = lax.axis_size(axis)
    return [1 << b for b in range(size.bit_length() - 1)]


def partner(x, axis, bit):
    size = lax.axis_size(axis)
    return lax.ppermute(x, axis, [(i, i ^ bit) for i in range(size)])


def half_of(x, which):
    rows = x.shape[0] // 2
    return lax.dynamic_slice_in_dim(x, which * rows, rows, axis=0)


def bit_state(axis, bit):
    return (lax.axis_index(axis) // bit) % 2


def halve(terms, axis, bit):
    mine = bit_state(axis, bit)
    return half_of(terms, mine) + partner(half_of(terms, 1 - mine), axis, bit)


def double(terms, peak, axis, bit):
    got = partner(jnp.concatenate([terms, peak], axis=0), axis, bit)
    rows = terms.shape[0]
    return terms + got[:rows], jnp.maximum(peak, got[rows:])


def gather(terms, peak, axis, bit):
    first = bit_state(axis, bit) == 0
    got = partner(jnp.concatenate([terms, peak], axis=0), axis, bit)
    rows = terms.shape[0]
    other, peak = got[:rows], jnp.maximum(peak, got[rows:])
    return jnp.concatenate([jnp.where(first, terms, other), jnp.where(first, other, terms)], axis=0), peak


def to_corners(bands, first):
    wide, narrow = lax.axis_size("wide"), lax.axis_size("narrow")
    steps = [0] if len(bands) == 1 else [-1, 1]
    got = []
    for s, step in enumerate(steps):
        pairs = []
        for i in range(first, wide - 1, 2):
            for n in range(narrow):
                m = 1 - n if step == 0 else n - step
                if 0 <= m < narrow:
                    pairs += [(i * narrow + n, (i + 1) * narrow + m), ((i + 1) * narrow + n, i * narrow + m)]
        band = bands[0] if step == 0 else bands[1 - s]
        got.append(lax.ppermute(band, ("wide", "narrow"), pairs))
    return got


def after(x, *others):
    return lax.optimization_barrier((x, *others))[0]


def body(tile, probe, measured, rows, cols, counts):
    wide, narrow = lax.axis_index("wide"), lax.axis_index("narrow")
    sides = 1 if lax.axis_size("narrow") == 2 else 2
    tile_rows, tile_cols = tile.shape[1:]
    even = wide % 2 == 0
    place = jnp.stack([wide, narrow]).astype(jnp.int32)

    far_band, near_band, edges, far_ends, near_ends = pack_call(place, rows, cols, counts, tile, sides)
    far_side = swap(far_band, "wide", 1)
    far_corners = to_corners(far_ends, 1)
    side_in = to_sides(edges)
    near_corners = to_corners(near_ends, 0)
    near = swap(near_band, "wide", 0)

    middle, near_rim, far_rim, side_rims, probe_sums, got_info = positions_calls(
        place, rows, cols, counts, tile, near, far_side, side_in, near_corners, far_corners, probe, measured
    )
    far_got = swap(far_rim, "wide", 1)
    own_info = edges[0][:1, tile_rows:]

    terms = probe_sums.reshape(-1, LANES)
    wide_bits, narrow_bits = bits_of("wide"), bits_of("narrow")
    terms = halve(terms, "wide", wide_bits[0])
    near_got = swap(after(near_rim, terms), "wide", 0)
    info = jnp.concatenate([own_info, got_info], axis=0)[:, 0, :32].astype(jnp.int32)
    cover, peak = cover_call(place, after(info, terms), probe, tile_rows, tile_cols, sides)
    terms = halve(terms, "wide", wide_bits[1])
    for bit in narrow_bits:
        terms = halve(terms, "narrow", bit)
    for bit in wide_bits[2:]:
        terms, peak = double(terms, peak, "wide", bit)
    for bit in narrow_bits[::-1]:
        terms, peak = gather(terms, peak, "narrow", bit)

    def with_rims(piece, s):
        cut = slice(tile_cols + s * LANES, tile_cols + (s + 1) * LANES)
        below = jnp.where(even, near_got[:, :, cut], far_got[:, :, cut])
        above = jnp.where(even, far_got[:, :, cut], near_got[:, :, cut])
        return piece + jnp.concatenate([above, below], axis=1)

    side_got = to_sides([with_rims(piece, s) for s, piece in enumerate(side_rims)])
    terms, peak = gather(terms, peak, "wide", wide_bits[1])
    other_terms = partner(jnp.concatenate([terms, peak], axis=0), "wide", wide_bits[0])
    return update_call(
        place, tile, middle, cover, peak, near_got, far_got, side_got, terms, other_terms, probe
    )


def solution(mesh):
    placed = (
        P(None, "wide", "narrow"),
        P(),
        P("wide", "narrow", None, None, None),
        P("wide", "narrow", None),
        P("wide", "narrow", None),
        P("wide", "narrow"),
    )
    return jax.shard_map(
        body,
        mesh=mesh,
        in_specs=placed,
        out_specs=(P(None, "wide", "narrow"), P()),
        check_vma=False,
    )
```

```python
import functools
import math

import jax
import jax.numpy as jnp
import ml_dtypes
import numpy as np
from jax import lax
from jax.experimental import pallas as pl
from jax.experimental.pallas import tpu as pltpu
from jax.sharding import PartitionSpec as P

H = 128
LANES = 128
CHUNK = 32
WAYS = 2
INFO = 8
BF = jnp.bfloat16
F32 = jnp.float32
MIX_OBJECT = 0.5
MIX_PROBE = 0.5
VMEM = pl.BlockSpec(memory_space=pltpu.VMEM)
SMEM = pl.BlockSpec(memory_space=pltpu.SMEM)
ANY = pl.BlockSpec(memory_space=pl.ANY)
HBM = pl.BlockSpec(memory_space=pltpu.HBM)
COUNT, ROWS, COLS = 2, 3, 11


def rounded_pair(table):
    table = table.astype(np.float32)
    high = table.astype(ml_dtypes.bfloat16)
    low = (table - high.astype(np.float32)).astype(ml_dtypes.bfloat16)
    return high, low


def dft_tables(length):
    index = np.arange(length)
    angle = 2.0 * np.pi * ((index[:, None] * index[None, :]) % length) / length
    cos_high, cos_low = rounded_pair(np.cos(angle) / math.sqrt(length))
    sin_high, sin_low = rounded_pair(-np.sin(angle) / math.sqrt(length))
    left = np.concatenate([cos_high, sin_high, cos_high, sin_high, cos_low, sin_low], axis=1)
    right_high = np.block([[cos_high, sin_high], [-sin_high, cos_high]])
    right_low = np.block([[cos_low, sin_low], [-sin_low, cos_low]])
    right = np.concatenate([right_high, right_high, right_low], axis=0)
    return left, right


def split(x):
    high = x.astype(BF)
    return high, (x - high.astype(F32)).astype(BF)


def side_block(place, side, sides, blocks):
    if sides == 1:
        return jnp.where(place[1] == 0, blocks - 1, 0)
    return 0 if side == 0 else blocks - 1


def side_step(place, side, sides):
    if sides == 1:
        return jnp.where(place[1] == 0, 1, -1)
    return -1 if side == 0 else 1


def cover_kernel(tile_rows, tile_cols, sides, place, info, probe, cover, peak, total, power):
    pr = probe.shape[1]
    pieces = pr // LANES
    for j in range(pieces):
        cut = slice(j * LANES, (j + 1) * LANES)
        power[j] = probe[0, :, cut] * probe[0, :, cut] + probe[1, :, cut] * probe[1, :, cut]
    total[...] = jnp.zeros_like(total)
    lanes = lax.broadcasted_iota(jnp.int32, (CHUNK, LANES), 1)
    even = place[0] % 2 == 0
    steps_down = (0, jnp.where(even, 1, -1), jnp.where(even, -1, 1))
    steps_right = (0,) + tuple(side_step(place, s, sides) for s in range(sides))
    for v in range(3):
        for h in range(1 + sides):
            source = v * (1 + sides) + h
            down, right = steps_down[v], steps_right[h]

            def visit(k, carry):
                row = info[source, k] + pr - H + down * tile_rows
                col = info[source, 8 + k] + pr - H + right * tile_cols
                inside = (row > 0) & (row < pr + tile_rows) & (col > 0) & (col < pr + tile_cols)

                @pl.when(inside)
                def _():
                    shift = col & (LANES - 1)
                    block = col >> 7
                    low = lanes < shift
                    for q in range(pr // CHUNK):
                        turned = [
                            pltpu.roll(power[j, q * CHUNK : (q + 1) * CHUNK, :], shift, 1)
                            for j in range(pieces)
                        ]
                        here = pl.ds(row + q * CHUNK, CHUNK)
                        zero = jnp.zeros((CHUNK, LANES), F32)
                        total[block, here, :] += jnp.where(low, zero, turned[0])
                        for j in range(1, pieces):
                            total[block + j, here, :] += jnp.where(low, turned[j - 1], turned[j])
                        total[block + pieces, here, :] += jnp.where(low, turned[-1], zero)

                return carry

            lax.fori_loop(0, info[source, 16], visit, 0)
    first = pr // LANES
    best = jnp.zeros((8, LANES), F32)
    for b in range(tile_cols // LANES):
        own = total[first + b, pr : pr + tile_rows, :]
        cover[:, b * LANES : (b + 1) * LANES] = own
        best = jnp.maximum(best, jnp.max(own.reshape(tile_rows // 8, 8, LANES), axis=0))
    peak[...] = jnp.full((8, LANES), jnp.max(best), F32)


def cover_call(place, info, probe, tile_rows, tile_cols, sides):
    pr = probe.shape[1]
    blocks = (tile_cols + 2 * pr) // LANES + 1
    return pl.pallas_call(
        functools.partial(cover_kernel, tile_rows, tile_cols, sides),
        out_shape=(
            jax.ShapeDtypeStruct((tile_rows, tile_cols), F32),
            jax.ShapeDtypeStruct((8, LANES), F32),
        ),
        in_specs=[SMEM, SMEM, VMEM],
        out_specs=(VMEM, VMEM),
        scratch_shapes=[
            pltpu.VMEM((blocks, tile_rows + 2 * pr, LANES), F32),
            pltpu.VMEM((pr // LANES, pr, LANES), F32),
        ],
        compiler_params=pltpu.CompilerParams(vmem_limit_bytes=24 << 20),
        cost_estimate=pl.CostEstimate(flops=4_000_000, bytes_accessed=8_000_000, transcendentals=0),
        name="cover",
    )(place, info, probe)


def pack_kernel(sides, place, tile, *refs):
    far_band, near_band = refs[:2]
    edges, far_ends, near_ends = [refs[2 + i * sides : 2 + (i + 1) * sides] for i in range(3)]
    sems = refs[2 + 3 * sides]
    tile_rows, tile_cols = tile.shape[1:]
    even = place[0] % 2 == 0
    near_start = pl.multiple_of(jnp.where(even, tile_rows - H, 0), 8)
    far_start = pl.multiple_of(jnp.where(even, 0, tile_rows - H), 8)
    if sides == 1:
        starts = [pl.multiple_of(jnp.where(place[1] == 0, tile_cols - H, 0), LANES)]
    else:
        starts = [0, tile_cols - H]
    bands = [(far_band, far_start, H, 0), (near_band, near_start, H, 0)]
    for s, start in enumerate(starts):
        bands += [(edges[s], 0, tile_rows, start), (far_ends[s], far_start, H, start)]
        bands += [(near_ends[s], near_start, H, start)]
    copies = []
    for i, (band, row, height, col) in enumerate(bands):
        copies.append(
            pltpu.make_async_copy(
                tile.at[:, pl.ds(row, height), pl.ds(col, band.shape[2])], band.at[:, pl.ds(0, height), :], sems.at[i]
            )
        )
        copies[-1].start()
    lanes = lax.broadcasted_iota(jnp.int32, (INFO, LANES), 1)
    notes = jnp.where(lanes == 16, place[COUNT], 0)
    for k in range(8):
        notes = jnp.where(lanes == k, place[ROWS + k], jnp.where(lanes == 8 + k, place[COLS + k], notes))
    notes = notes.astype(F32)
    for band, row, height, col in bands:
        for ch in range(2):
            band[ch, height : height + INFO, 0:LANES] = notes
            if band.shape[2] > LANES:
                band[ch, height : height + INFO, LANES:] = jnp.zeros((INFO, band.shape[2] - LANES), F32)
    for copy in copies:
        copy.wait()


def pack_call(place, tile, sides):
    tile_rows, tile_cols = tile.shape[1:]
    shape = lambda height, width: jax.ShapeDtypeStruct((2, height + INFO, width), F32)
    shapes = [shape(H, tile_cols)] * 2 + [shape(tile_rows, LANES)] * sides + [shape(H, LANES)] * (2 * sides)
    out = pl.pallas_call(
        functools.partial(pack_kernel, sides),
        out_shape=shapes,
        in_specs=[SMEM, HBM],
        out_specs=[VMEM] * len(shapes),
        scratch_shapes=[pltpu.SemaphoreType.DMA((len(shapes),))],
        compiler_params=pltpu.CompilerParams(vmem_limit_bytes=8 << 20),
        name="pack",
    )(place, tile)
    return out[0], out[1], *[list(out[2 + i * sides : 2 + (i + 1) * sides]) for i in range(3)]


def positions_kernel(sides, last, *refs):
    place = refs[0]
    if last:
        ext_in, grad_in, sums_in, far_side = refs[1:5]
        far_corners = refs[5 : 5 + sides]
        probe_in, measured, left_in, right_in = refs[5 + sides : 9 + sides]
        middle, near_rim, far_rim, info = refs[9 + sides : 13 + sides]
        side_out = refs[13 + sides : 13 + 2 * sides]
        probe_sums, ext, grad = refs[13 + 2 * sides : 16 + 2 * sides]
        scratch = refs[16 + 2 * sides :]
    else:
        tile, near = refs[1:3]
        side_in, near_corners = refs[3 : 3 + sides], refs[3 + sides : 3 + 2 * sides]
        probe_in, measured, left_in, right_in = refs[3 + 2 * sides : 7 + 2 * sides]
        info, ext, grad, probe_sums = refs[7 + 2 * sides : 11 + 2 * sides]
        scratch = refs[11 + 2 * sides :]
    left, right, levels, order, probe = scratch[:5]
    table_sems, level_sems, ext_sems = scratch[5:8]
    scratch = scratch[8:]
    patches, exits, stacks, wides, fields = [scratch[i * WAYS : (i + 1) * WAYS] for i in range(5)]

    pr = probe_in.shape[1]
    pieces = pr // LANES
    ext_rows = ext.shape[1]
    blocks = ext.shape[0] // 2
    own_blocks = blocks - 2
    tile_rows, tile_cols = ext_rows - 2 * H, own_blocks * LANES
    even = place[0] % 2 == 0
    near_row = pl.multiple_of(jnp.where(even, tile_rows + H, 0), 8)
    far_row = pl.multiple_of(jnp.where(even, 0, tile_rows + H), 8)
    side_blocks = [side_block(place, s, sides, blocks) for s in range(sides)]
    own, near_rows, far_rows = pl.ds(H, tile_rows), pl.ds(near_row, H), pl.ds(far_row, H)

    copies = []

    def fetch(source, target):
        copies.append(pltpu.make_async_copy(source, target, ext_sems.at[len(copies)]))
        copies[-1].start()

    for ch in range(2):
        for b in range(own_blocks):
            at, cut = ch * blocks + 1 + b, pl.ds(b * LANES, LANES)
            if last:
                fetch(far_side.at[ch, pl.ds(0, H), cut], ext.at[at, far_rows, :])
            else:
                fetch(tile.at[ch, :, cut], ext.at[at, own, :])
                fetch(near.at[ch, pl.ds(0, H), cut], ext.at[at, near_rows, :])
        for s in range(sides):
            at = ch * blocks + side_blocks[s]
            if last:
                fetch(far_corners[s].at[ch, pl.ds(0, H), :], ext.at[at, far_rows, :])
            else:
                fetch(side_in[s].at[ch, pl.ds(0, tile_rows), :], ext.at[at, own, :])
                fetch(near_corners[s].at[ch, pl.ds(0, H), :], ext.at[at, near_rows, :])
    for s in range(sides):
        if last:
            fetch(far_corners[s].at[0, pl.ds(H, INFO), :], info.at[1 + s])
        else:
            fetch(side_in[s].at[0, pl.ds(tile_rows, INFO), :], info.at[s])
            fetch(near_corners[s].at[0, pl.ds(H, INFO), :], info.at[sides + 1 + s])
    if last:
        fetch(far_side.at[0, pl.ds(H, INFO), pl.ds(0, LANES)], info.at[0])
    else:
        fetch(near.at[0, pl.ds(H, INFO), pl.ds(0, LANES)], info.at[sides])
    tables = [
        pltpu.make_async_copy(left_in, left, table_sems.at[0]),
        pltpu.make_async_copy(right_in, right, table_sems.at[1]),
        pltpu.make_async_copy(probe_in, probe, table_sems.at[2]),
    ]
    for copy in tables:
        copy.start()

    live_slots = place[COUNT]

    def touches(k):
        row = place[ROWS + k]
        return jnp.where(even, row < H, row > tile_rows - H)

    def pick(wanted):
        def step(k, n):
            @pl.when(touches(k) == wanted)
            def _():
                order[n] = k

            return n + jnp.where(touches(k) == wanted, 1, 0)

        return step

    near_slots = lax.fori_loop(0, live_slots, pick(False), 0)
    lax.fori_loop(0, live_slots, pick(True), near_slots)
    border = near_slots // WAYS * WAYS
    begin, end = (border, live_slots) if last else (0, border)

    def level_copy(i):
        return pltpu.make_async_copy(measured.at[0, 0, order[i]], levels.at[i], level_sems.at[i])

    def start_level(i, carry):
        level_copy(i).start()
        return carry

    lax.fori_loop(begin, end, start_level, 0)
    if last:
        for at in range(2 * blocks):
            ext[at, own, :] = ext_in[at, own, :]
            ext[at, near_rows, :] = ext_in[at, near_rows, :]
        if sides == 1:
            for ch in range(2):
                ext[ch * blocks + blocks - 1 - side_blocks[0], far_rows, :] = jnp.zeros((H, LANES), F32)
        grad[...] = grad_in[...]
        probe_sums[...] = sums_in[...]
    else:
        if sides == 1:
            for ch in range(2):
                ext[ch * blocks + blocks - 1 - side_blocks[0]] = jnp.zeros((ext_rows, LANES), F32)
        grad[...] = jnp.zeros_like(grad)
        probe_sums[...] = jnp.zeros_like(probe_sums)
    for copy in copies + tables:
        copy.wait()
    lanes = lax.broadcasted_iota(jnp.int32, (CHUNK, LANES), 1)

    def put(stack, value, part, q, first):
        width = value.shape[1]
        high, low = split(value)
        rows_at = lambda block: slice(block * pr + q * CHUNK, block * pr + (q + 1) * CHUNK)
        here, there = slice(first, first + width), slice(pr + first, pr + first + width)
        if part == 0:
            stack[rows_at(0), here], stack[rows_at(1), there] = high, high
            stack[rows_at(2), here], stack[rows_at(3), there] = low, low
        else:
            stack[rows_at(0), there], stack[rows_at(1), here] = high, -high
            stack[rows_at(2), there], stack[rows_at(3), here] = low, -low

    def times_left(w):
        stack = jnp.concatenate([stacks[w][...], stacks[w][0 : 2 * pr]], axis=0)
        fields[w][...] = jnp.dot(left[...], stack, preferred_element_type=F32)

    def times_right(w):
        for q in range(pr // CHUNK):
            cut = slice(q * CHUNK, (q + 1) * CHUNK)
            high, low = split(fields[w][cut, :])
            wides[w][cut, 0 : 2 * pr] = high
            wides[w][cut, 2 * pr : 4 * pr] = low
        stack = jnp.concatenate([wides[w][...], wides[w][:, 0 : 2 * pr]], axis=1)
        fields[w][...] = jnp.dot(stack, right[...], preferred_element_type=F32)

    def load(w, k):
        row, col = place[ROWS + order[k]], place[COLS + order[k]]
        shift, block = col & (LANES - 1), col >> 7
        back = (LANES - shift) & (LANES - 1)
        keep = lanes < LANES - shift
        for q in range(pr // CHUNK):
            cut = slice(q * CHUNK, (q + 1) * CHUNK)
            here = pl.ds(row + q * CHUNK, CHUNK)
            seen = []
            for ch in range(2):
                turned = [
                    pltpu.roll(ext[ch * blocks + block + j, here, :], back, 1)
                    for j in range(pieces + 1)
                ]
                seen.append([jnp.where(keep, turned[j], turned[j + 1]) for j in range(pieces)])
            for j in range(pieces):
                part = slice(j * LANES, (j + 1) * LANES)
                probe_real, probe_imag = probe[0, cut, part], probe[1, cut, part]
                real, imag = seen[0][j], seen[1][j]
                patches[w][0, cut, part], patches[w][1, cut, part] = real, imag
                exit_real = probe_real * real - probe_imag * imag
                exit_imag = probe_real * imag + probe_imag * real
                exits[w][0, cut, part], exits[w][1, cut, part] = exit_real, exit_imag
                put(stacks[w], exit_real, 0, q, j * LANES)
                put(stacks[w], exit_imag, 1, q, j * LANES)

    def project(w, k):
        for q in range(pr // CHUNK):
            cut = slice(q * CHUNK, (q + 1) * CHUNK)
            real, imag = fields[w][cut, 0:pr], fields[w][cut, pr : 2 * pr]
            factor = jnp.sqrt(levels[k, cut, :]) * lax.rsqrt(real * real + imag * imag + 1.0)
            put(stacks[w], real * factor, 0, q, 0)
            put(stacks[w], -(imag * factor), 1, q, 0)

    def finish(w, k, live):
        row, col = place[ROWS + order[k]], place[COLS + order[k]]
        shift, block = col & (LANES - 1), col >> 7
        low = lanes < shift
        zero = jnp.zeros((CHUNK, LANES), F32)
        for q in range(pr // CHUNK):
            cut = slice(q * CHUNK, (q + 1) * CHUNK)
            here = pl.ds(row + q * CHUNK, CHUNK)
            turned = [[], []]
            for j in range(pieces):
                part = slice(j * LANES, (j + 1) * LANES)
                other = slice(pr + j * LANES, pr + (j + 1) * LANES)
                diff_real = fields[w][cut, part] - exits[w][0, cut, part]
                diff_imag = -fields[w][cut, other] - exits[w][1, cut, part]
                real, imag = patches[w][0, cut, part], patches[w][1, cut, part]
                weight = real * real + imag * imag
                if live is not None:
                    diff_real, diff_imag = diff_real * live, diff_imag * live
                    weight = weight * live
                probe_real, probe_imag = probe[0, cut, part], probe[1, cut, part]
                turned[0].append(pltpu.roll(probe_real * diff_real + probe_imag * diff_imag, shift, 1))
                turned[1].append(pltpu.roll(probe_real * diff_imag - probe_imag * diff_real, shift, 1))
                probe_sums[j, 0, cut, :] += real * diff_real + imag * diff_imag
                probe_sums[j, 1, cut, :] += real * diff_imag - imag * diff_real
                probe_sums[j, 2, cut, :] += weight
            for ch in range(2):
                at = ch * blocks + block
                grad[at, here, :] += jnp.where(low, zero, turned[ch][0])
                for j in range(1, pieces):
                    grad[at + j, here, :] += jnp.where(low, turned[ch][j - 1], turned[ch][j])
                grad[at + pieces, here, :] += jnp.where(low, turned[ch][-1], zero)

    def visit(i, carry):
        first = begin + i * WAYS
        slots = [jnp.minimum(first + w, end - 1) for w in range(WAYS)]
        lives = [None] + [jnp.where(first + w < end, 1.0, 0.0) for w in range(1, WAYS)]
        for w in range(WAYS):

            @pl.when(first + w < end)
            def _():
                level_copy(slots[w]).wait()

        for w in range(WAYS):
            load(w, slots[w])
            times_left(w)
        for w in range(WAYS):
            times_right(w)
        for w in range(WAYS):
            project(w, slots[w])
            times_left(w)
        for w in range(WAYS):
            times_right(w)
        for w in range(WAYS):
            finish(w, slots[w], lives[w])
        return carry

    lax.fori_loop(0, (end - begin + WAYS - 1) // WAYS, visit, 0)
    if not last:
        return
    for ch in range(2):
        for b in range(own_blocks):
            at, cut = ch * blocks + 1 + b, slice(b * LANES, (b + 1) * LANES)
            middle[ch, :, cut] = grad[at, own, :]
            near_rim[ch, :, cut] = grad[at, near_rows, :]
            far_rim[ch, :, cut] = grad[at, far_rows, :]
        for s in range(sides):
            at = ch * blocks + side_blocks[s]
            cut = slice(tile_cols + s * LANES, tile_cols + (s + 1) * LANES)
            side_out[s][ch] = grad[at, own, :]
            near_rim[ch, :, cut] = grad[at, near_rows, :]
            far_rim[ch, :, cut] = grad[at, far_rows, :]


def positions_calls(place, tile, near, far_side, side_in, near_corners, far_corners, probe, measured):
    pr = probe.shape[1]
    sides = len(side_in)
    tile_rows, tile_cols = tile.shape[1:]
    ext_rows = tile_rows + 2 * H
    blocks = (tile_cols + 2 * H) // LANES
    left, right = (jnp.asarray(table) for table in dft_tables(pr))
    shape = lambda *dims: jax.ShapeDtypeStruct(dims, F32)
    slots = measured.shape[2]
    sums = shape(pr // LANES, 3, pr, LANES)
    field = shape(2 * blocks, ext_rows, LANES)
    rim = shape(2, H, tile_cols + sides * LANES)
    params = pltpu.CompilerParams(vmem_limit_bytes=34 << 20)
    scratch = [
        pltpu.VMEM(left.shape, BF),
        pltpu.VMEM(right.shape, BF),
        pltpu.VMEM((slots, pr, pr), F32),
        pltpu.SMEM((slots,), jnp.int32),
        pltpu.VMEM(probe.shape, F32),
        pltpu.SemaphoreType.DMA((3,)),
        pltpu.SemaphoreType.DMA((slots,)),
        pltpu.SemaphoreType.DMA((4 * blocks + 2 * sides + 1,)),
        *[pltpu.VMEM((2, pr, pr), F32)] * (2 * WAYS),
        *[pltpu.VMEM((4 * pr, 2 * pr), BF)] * WAYS,
        *[pltpu.VMEM((pr, 4 * pr), BF)] * WAYS,
        *[pltpu.VMEM((pr, 2 * pr), F32)] * WAYS,
    ]
    near_info, ext, grad, sums_so_far = pl.pallas_call(
        functools.partial(positions_kernel, sides, False),
        out_shape=(shape(2 * sides + 1, INFO, LANES), field, field, sums),
        in_specs=[SMEM, HBM] + [ANY] * (1 + 2 * sides) + [HBM] * 4,
        out_specs=(VMEM,) * 4,
        scratch_shapes=scratch,
        compiler_params=params,
        cost_estimate=pl.CostEstimate(flops=1, bytes_accessed=1, transcendentals=0),
        name="positions_near",
    )(place, tile, near, *side_in, *near_corners, probe, measured, left, right)
    middle, near_rim, far_rim, far_info, *rest = pl.pallas_call(
        functools.partial(positions_kernel, sides, True),
        out_shape=(
            shape(2, tile_rows, tile_cols),
            rim,
            rim,
            shape(sides + 1, INFO, LANES),
            *[shape(2, tile_rows, LANES)] * sides,
            sums,
        ),
        in_specs=[SMEM] + [VMEM] * 3 + [ANY] * (1 + sides) + [HBM] * 4,
        out_specs=(VMEM,) * (5 + sides),
        scratch_shapes=[pltpu.VMEM(field.shape, F32)] * 2 + scratch,
        compiler_params=params,
        cost_estimate=pl.CostEstimate(
            flops=slots * 48 * pr * pr * pr, bytes_accessed=16_000_000, transcendentals=slots * pr * pr
        ),
        name="positions_far",
    )(place, ext, grad, sums_so_far, far_side, *far_corners, probe, measured, left, right)
    info = jnp.concatenate([near_info, far_info], axis=0)
    return middle, near_rim, far_rim, rest[:sides], rest[sides], info


def update_kernel(sides, *refs):
    place, tile, middle, cover, peak, near, far_side = refs[:7]
    side_in = refs[7 : 7 + sides]
    own_terms, other_terms, probe, out, new_probe, sums = refs[7 + sides :]
    tile_rows, tile_cols = tile.shape[1:]
    own_blocks = tile_cols // LANES
    even = place[0] % 2 == 0
    sums[...] = middle[...]
    near_row = pl.multiple_of(jnp.where(even, tile_rows - H, 0), 8)
    far_row = pl.multiple_of(jnp.where(even, 0, tile_rows - H), 8)
    sums[:, pl.ds(near_row, H), :] += near[:, :, 0:tile_cols]
    sums[:, pl.ds(far_row, H), :] += far_side[:, :, 0:tile_cols]
    for s in range(sides):
        if sides == 1:
            for edge, where in ((0, own_blocks - 1), (1, 0)):

                @pl.when((place[1] == 0) == (edge == 0))
                def _():
                    sums[:, :, where * LANES : (where + 1) * LANES] += side_in[s][...]
        else:
            where = 0 if s == 0 else own_blocks - 1
            sums[:, :, where * LANES : (where + 1) * LANES] += side_in[s][...]
    rows = own_terms.shape[0]
    top = MIX_OBJECT * jnp.maximum(peak[0:1, 0:1], other_terms[rows : rows + 1, 0:1])
    inverse = 1.0 / ((1.0 - MIX_OBJECT) * cover[...] + top)
    for ch in range(2):
        out[ch] = tile[ch] + sums[ch] * inverse

    pr = probe.shape[1]
    pieces = pr // LANES
    both = (own_terms, other_terms)

    def update(parts):
        flat = [parts[j * len(parts) // pieces] for j in range(pieces)]
        span = flat[0].shape[0] // (pieces // len(parts))
        term = lambda j, ch: flat[j][(j % (pieces // len(parts))) * span + ch * pr :][:pr]
        weights = [term(j, 2) for j in range(pieces)]
        best = functools.reduce(jnp.maximum, weights)
        best = jnp.max(jnp.max(best.reshape(-1, 8, LANES), axis=0), keepdims=True)
        for j in range(pieces):
            cut = slice(j * LANES, (j + 1) * LANES)
            scale = 1.0 / ((1.0 - MIX_PROBE) * weights[j] + MIX_PROBE * best)
            for ch in range(2):
                new_probe[ch, :, cut] = probe[ch, :, cut] + term(j, ch) * scale

    for first in (0, 1):

        @pl.when(place[0] % 2 == first)
        def _():
            update([both[first][0:rows, :], both[1 - first][0:rows, :]])


def update_call(place, tile, middle, cover, peak, near, far_side, side_in, own_terms, other_terms, probe):
    sides = len(side_in)
    return pl.pallas_call(
        functools.partial(update_kernel, sides),
        out_shape=(jax.ShapeDtypeStruct(tile.shape, F32), jax.ShapeDtypeStruct(probe.shape, F32)),
        in_specs=[SMEM] + [VMEM] * (9 + sides),
        out_specs=(VMEM, VMEM),
        scratch_shapes=[pltpu.VMEM(tile.shape, F32)],
        compiler_params=pltpu.CompilerParams(vmem_limit_bytes=32 << 20),
        name="update",
    )(place, tile, middle, cover, peak, near, far_side, *side_in, own_terms, other_terms, probe)


def swap(x, axis, first):
    size = lax.axis_size(axis)
    pairs = []
    for i in range(first, size - 1, 2):
        pairs += [(i, i + 1), (i + 1, i)]
    return lax.ppermute(x, axis, pairs)


def shifted(x, axis, by):
    size = lax.axis_size(axis)
    return lax.ppermute(x, axis, [(i, i + by) for i in range(size) if 0 <= i + by < size])


def to_sides(pieces):
    if len(pieces) == 1:
        return [swap(pieces[0], "narrow", 0)]
    return [shifted(pieces[1], "narrow", 1), shifted(pieces[0], "narrow", -1)]


def bits_of(axis):
    size = lax.axis_size(axis)
    return [1 << b for b in range(size.bit_length() - 1)]


def partner(x, axis, bit):
    size = lax.axis_size(axis)
    return lax.ppermute(x, axis, [(i, i ^ bit) for i in range(size)])


def half_of(x, which):
    rows = x.shape[0] // 2
    return lax.dynamic_slice_in_dim(x, which * rows, rows, axis=0)


def bit_state(axis, bit):
    return (lax.axis_index(axis) // bit) % 2


def halve(terms, axis, bit):
    mine = bit_state(axis, bit)
    return half_of(terms, mine) + partner(half_of(terms, 1 - mine), axis, bit)


def double(terms, peak, axis, bit):
    got = partner(jnp.concatenate([terms, peak], axis=0), axis, bit)
    rows = terms.shape[0]
    return terms + got[:rows], jnp.maximum(peak, got[rows:])


def gather(terms, peak, axis, bit):
    first = bit_state(axis, bit) == 0
    got = partner(jnp.concatenate([terms, peak], axis=0), axis, bit)
    rows = terms.shape[0]
    other, peak = got[:rows], jnp.maximum(peak, got[rows:])
    return jnp.concatenate([jnp.where(first, terms, other), jnp.where(first, other, terms)], axis=0), peak


def to_corners(bands, first):
    wide, narrow = lax.axis_size("wide"), lax.axis_size("narrow")
    steps = [0] if len(bands) == 1 else [-1, 1]
    got = []
    for s, step in enumerate(steps):
        pairs = []
        for i in range(first, wide - 1, 2):
            for n in range(narrow):
                m = 1 - n if step == 0 else n - step
                if 0 <= m < narrow:
                    pairs += [(i * narrow + n, (i + 1) * narrow + m), ((i + 1) * narrow + n, i * narrow + m)]
        band = bands[0] if step == 0 else bands[1 - s]
        got.append(lax.ppermute(band, ("wide", "narrow"), pairs))
    return got


def after(x, *others):
    return lax.optimization_barrier((x, *others))[0]


def body(tile, probe, measured, rows, cols, counts):
    wide, narrow = lax.axis_index("wide"), lax.axis_index("narrow")
    sides = 1 if lax.axis_size("narrow") == 2 else 2
    tile_rows, tile_cols = tile.shape[1:]
    even = wide % 2 == 0
    place = jnp.concatenate(
        [jnp.stack([wide, narrow, counts[0, 0]]).astype(jnp.int32), rows.reshape(-1), cols.reshape(-1)]
    )

    far_band, near_band, edges, far_ends, near_ends = pack_call(place, tile, sides)
    far_side = swap(far_band, "wide", 1)
    far_corners = to_corners(far_ends, 1)
    side_in = to_sides(edges)
    near_corners = to_corners(near_ends, 0)
    near = swap(near_band, "wide", 0)

    middle, near_rim, far_rim, side_rims, probe_sums, got_info = positions_calls(
        place, tile, near, far_side, side_in, near_corners, far_corners, probe, measured
    )
    own_info = edges[0][:1, tile_rows:]

    terms = probe_sums.reshape(-1, LANES)
    wide_bits, narrow_bits = bits_of("wide"), bits_of("narrow")
    terms = halve(terms, "wide", wide_bits[0])
    near_got = swap(after(near_rim, terms), "wide", 0)
    info = jnp.concatenate([own_info, got_info], axis=0)[:, 0, :32].astype(jnp.int32)
    cover, peak = cover_call(place, after(info, terms), probe, tile_rows, tile_cols, sides)
    terms = halve(terms, "wide", wide_bits[1])
    far_got = swap(after(far_rim, terms), "wide", 1)
    for bit in narrow_bits:
        terms = halve(terms, "narrow", bit)
    for bit in wide_bits[2:]:
        if bit == wide_bits[-1]:
            terms = after(terms, far_got)
        terms, peak = double(terms, peak, "wide", bit)
    for bit in narrow_bits[::-1]:
        terms, peak = gather(terms, peak, "narrow", bit)

    def with_rims(piece, s):
        cut = slice(tile_cols + s * LANES, tile_cols + (s + 1) * LANES)
        below = jnp.where(even, near_got[:, :, cut], far_got[:, :, cut])
        above = jnp.where(even, far_got[:, :, cut], near_got[:, :, cut])
        return piece + jnp.concatenate([above, below], axis=1)

    side_got = to_sides([with_rims(piece, s) for s, piece in enumerate(side_rims)])
    terms, peak = gather(terms, peak, "wide", wide_bits[1])
    other_terms = partner(jnp.concatenate([terms, peak], axis=0), "wide", wide_bits[0])
    return update_call(
        place, tile, middle, cover, peak, near_got, far_got, side_got, terms, other_terms, probe
    )


def solution(mesh):
    placed = (
        P(None, "wide", "narrow"),
        P(),
        P("wide", "narrow", None, None, None),
        P("wide", "narrow", None),
        P("wide", "narrow", None),
        P("wide", "narrow"),
    )
    return jax.shard_map(
        body,
        mesh=mesh,
        in_specs=placed,
        out_specs=(P(None, "wide", "narrow"), P()),
        check_vma=False,
    )
```

```python
import functools
import math

import jax
import jax.numpy as jnp
import ml_dtypes
import numpy as np
from jax import lax
from jax.experimental import pallas as pl
from jax.experimental.pallas import tpu as pltpu
from jax.sharding import Mesh, PartitionSpec as P

H = 128
LANES = 128
CHUNK = 32
WAYS = 2
INFO = 8
BF = jnp.bfloat16
F32 = jnp.float32
MIX_OBJECT = 0.5
MIX_PROBE = 0.5
VMEM = pl.BlockSpec(memory_space=pltpu.VMEM)
SMEM = pl.BlockSpec(memory_space=pltpu.SMEM)
ANY = pl.BlockSpec(memory_space=pl.ANY)
HBM = pl.BlockSpec(memory_space=pltpu.HBM)
COUNT, ROWS, COLS = 2, 3, 11


def rounded_pair(table):
    table = table.astype(np.float32)
    high = table.astype(ml_dtypes.bfloat16)
    low = (table - high.astype(np.float32)).astype(ml_dtypes.bfloat16)
    return high, low


def dft_tables(length):
    index = np.arange(length)
    angle = 2.0 * np.pi * ((index[:, None] * index[None, :]) % length) / length
    cos_high, cos_low = rounded_pair(np.cos(angle) / math.sqrt(length))
    sin_high, sin_low = rounded_pair(-np.sin(angle) / math.sqrt(length))
    left = np.concatenate([cos_high, sin_high, cos_high, sin_high, cos_low, sin_low], axis=1)
    right_high = np.block([[cos_high, sin_high], [-sin_high, cos_high]])
    right_low = np.block([[cos_low, sin_low], [-sin_low, cos_low]])
    right = np.concatenate([right_high, right_high, right_low], axis=0)
    return left, right


def split(x):
    high = x.astype(BF)
    return high, (x - high.astype(F32)).astype(BF)


def side_block(place, side, sides, blocks):
    if sides == 1:
        return jnp.where(place[1] == 0, blocks - 1, 0)
    return 0 if side == 0 else blocks - 1


def side_step(place, side, sides):
    if sides == 1:
        return jnp.where(place[1] == 0, 1, -1)
    return -1 if side == 0 else 1


def cover_kernel(tile_rows, tile_cols, sides, place, info, probe, cover, peak, total, power):
    pr = probe.shape[1]
    pieces = pr // LANES
    for j in range(pieces):
        cut = slice(j * LANES, (j + 1) * LANES)
        power[j] = probe[0, :, cut] * probe[0, :, cut] + probe[1, :, cut] * probe[1, :, cut]
    total[...] = jnp.zeros_like(total)
    lanes = lax.broadcasted_iota(jnp.int32, (CHUNK, LANES), 1)
    even = place[0] % 2 == 0
    steps_down = (0, jnp.where(even, 1, -1), jnp.where(even, -1, 1))
    steps_right = (0,) + tuple(side_step(place, s, sides) for s in range(sides))
    for v in range(3):
        for h in range(1 + sides):
            source = v * (1 + sides) + h
            down, right = steps_down[v], steps_right[h]

            def visit(k, carry):
                row = info[source, k] + pr - H + down * tile_rows
                col = info[source, 8 + k] + pr - H + right * tile_cols
                inside = (row > 0) & (row < pr + tile_rows) & (col > 0) & (col < pr + tile_cols)

                @pl.when(inside)
                def _():
                    shift = col & (LANES - 1)
                    block = col >> 7
                    low = lanes < shift
                    for q in range(pr // CHUNK):
                        turned = [
                            pltpu.roll(power[j, q * CHUNK : (q + 1) * CHUNK, :], shift, 1)
                            for j in range(pieces)
                        ]
                        here = pl.ds(row + q * CHUNK, CHUNK)
                        zero = jnp.zeros((CHUNK, LANES), F32)
                        total[block, here, :] += jnp.where(low, zero, turned[0])
                        for j in range(1, pieces):
                            total[block + j, here, :] += jnp.where(low, turned[j - 1], turned[j])
                        total[block + pieces, here, :] += jnp.where(low, turned[-1], zero)

                return carry

            lax.fori_loop(0, info[source, 16], visit, 0)
    first = pr // LANES
    best = jnp.zeros((8, LANES), F32)
    for b in range(tile_cols // LANES):
        own = total[first + b, pr : pr + tile_rows, :]
        cover[:, b * LANES : (b + 1) * LANES] = own
        best = jnp.maximum(best, jnp.max(own.reshape(tile_rows // 8, 8, LANES), axis=0))
    peak[...] = jnp.full((8, LANES), jnp.max(best), F32)


def cover_call(place, info, probe, tile_rows, tile_cols, sides):
    pr = probe.shape[1]
    blocks = (tile_cols + 2 * pr) // LANES + 1
    return pl.pallas_call(
        functools.partial(cover_kernel, tile_rows, tile_cols, sides),
        out_shape=(
            jax.ShapeDtypeStruct((tile_rows, tile_cols), F32),
            jax.ShapeDtypeStruct((8, LANES), F32),
        ),
        in_specs=[SMEM, SMEM, VMEM],
        out_specs=(VMEM, VMEM),
        scratch_shapes=[
            pltpu.VMEM((blocks, tile_rows + 2 * pr, LANES), F32),
            pltpu.VMEM((pr // LANES, pr, LANES), F32),
        ],
        compiler_params=pltpu.CompilerParams(vmem_limit_bytes=24 << 20),
        cost_estimate=pl.CostEstimate(flops=4_000_000, bytes_accessed=8_000_000, transcendentals=0),
        name="cover",
    )(place, info, probe)


def pack_kernel(sides, place, tile, *refs):
    far_band, near_band = refs[:2]
    edges, far_ends, near_ends = [refs[2 + i * sides : 2 + (i + 1) * sides] for i in range(3)]
    sems = refs[2 + 3 * sides]
    tile_rows, tile_cols = tile.shape[1:]
    even = place[0] % 2 == 0
    near_start = pl.multiple_of(jnp.where(even, tile_rows - H, 0), 8)
    far_start = pl.multiple_of(jnp.where(even, 0, tile_rows - H), 8)
    if sides == 1:
        starts = [pl.multiple_of(jnp.where(place[1] == 0, tile_cols - H, 0), LANES)]
    else:
        starts = [0, tile_cols - H]
    bands = [(far_band, far_start, H, 0), (near_band, near_start, H, 0)]
    for s, start in enumerate(starts):
        bands += [(edges[s], 0, tile_rows, start), (far_ends[s], far_start, H, start)]
        bands += [(near_ends[s], near_start, H, start)]
    copies = []
    for i, (band, row, height, col) in enumerate(bands):
        copies.append(
            pltpu.make_async_copy(
                tile.at[:, pl.ds(row, height), pl.ds(col, band.shape[2])], band.at[:, pl.ds(0, height), :], sems.at[i]
            )
        )
        copies[-1].start()
    lanes = lax.broadcasted_iota(jnp.int32, (INFO, LANES), 1)
    notes = jnp.where(lanes == 16, place[COUNT], 0)
    for k in range(8):
        notes = jnp.where(lanes == k, place[ROWS + k], jnp.where(lanes == 8 + k, place[COLS + k], notes))
    notes = notes.astype(F32)
    for band, row, height, col in bands:
        for ch in range(2):
            band[ch, height : height + INFO, 0:LANES] = notes
            if band.shape[2] > LANES:
                band[ch, height : height + INFO, LANES:] = jnp.zeros((INFO, band.shape[2] - LANES), F32)
    for copy in copies:
        copy.wait()


def pack_call(place, tile, sides):
    tile_rows, tile_cols = tile.shape[1:]
    shape = lambda height, width: jax.ShapeDtypeStruct((2, height + INFO, width), F32)
    shapes = [shape(H, tile_cols)] * 2 + [shape(tile_rows, LANES)] * sides + [shape(H, LANES)] * (2 * sides)
    out = pl.pallas_call(
        functools.partial(pack_kernel, sides),
        out_shape=shapes,
        in_specs=[SMEM, HBM],
        out_specs=[VMEM] * len(shapes),
        scratch_shapes=[pltpu.SemaphoreType.DMA((len(shapes),))],
        compiler_params=pltpu.CompilerParams(vmem_limit_bytes=8 << 20),
        name="pack",
    )(place, tile)
    return out[0], out[1], *[list(out[2 + i * sides : 2 + (i + 1) * sides]) for i in range(3)]


def positions_kernel(sides, *refs):
    place, tile, near, far_side = refs[:4]
    side_in, near_corners, far_corners = [refs[4 + i * sides : 4 + (i + 1) * sides] for i in range(3)]
    probe_in, measured, left_in, right_in = refs[4 + 3 * sides : 8 + 3 * sides]
    middle, near_rim, far_rim, info = refs[8 + 3 * sides : 12 + 3 * sides]
    side_out = refs[12 + 3 * sides : 12 + 4 * sides]
    probe_sums, ext, grad = refs[12 + 4 * sides : 15 + 4 * sides]
    scratch = refs[15 + 4 * sides :]
    left, right, levels, probe = scratch[:4]
    table_sems, level_sems, ext_sems = scratch[4:7]
    scratch = scratch[7:]
    patches, exits, stacks, wides, fields = [scratch[i * WAYS : (i + 1) * WAYS] for i in range(5)]

    pr = probe_in.shape[1]
    pieces = pr // LANES
    ext_rows = ext.shape[1]
    blocks = ext.shape[0] // 2
    own_blocks = blocks - 2
    tile_rows, tile_cols = ext_rows - 2 * H, own_blocks * LANES
    even = place[0] % 2 == 0
    near_row = pl.multiple_of(jnp.where(even, tile_rows + H, 0), 8)
    far_row = pl.multiple_of(jnp.where(even, 0, tile_rows + H), 8)
    side_blocks = [side_block(place, s, sides, blocks) for s in range(sides)]
    own, near_rows, far_rows = pl.ds(H, tile_rows), pl.ds(near_row, H), pl.ds(far_row, H)

    copies = []

    def fetch(source, target):
        copies.append(pltpu.make_async_copy(source, target, ext_sems.at[len(copies)]))
        copies[-1].start()

    for ch in range(2):
        for b in range(own_blocks):
            at, cut = ch * blocks + 1 + b, pl.ds(b * LANES, LANES)
            fetch(tile.at[ch, :, cut], ext.at[at, own, :])
            fetch(near.at[ch, pl.ds(0, H), cut], ext.at[at, near_rows, :])
            fetch(far_side.at[ch, pl.ds(0, H), cut], ext.at[at, far_rows, :])
        for s in range(sides):
            at = ch * blocks + side_blocks[s]
            fetch(side_in[s].at[ch, pl.ds(0, tile_rows), :], ext.at[at, own, :])
            fetch(near_corners[s].at[ch, pl.ds(0, H), :], ext.at[at, near_rows, :])
            fetch(far_corners[s].at[ch, pl.ds(0, H), :], ext.at[at, far_rows, :])
    for s in range(sides):
        fetch(side_in[s].at[0, pl.ds(tile_rows, INFO), :], info.at[s])
        fetch(near_corners[s].at[0, pl.ds(H, INFO), :], info.at[sides + 1 + s])
        fetch(far_corners[s].at[0, pl.ds(H, INFO), :], info.at[2 * sides + 2 + s])
    fetch(near.at[0, pl.ds(H, INFO), pl.ds(0, LANES)], info.at[sides])
    fetch(far_side.at[0, pl.ds(H, INFO), pl.ds(0, LANES)], info.at[2 * sides + 1])
    tables = [
        pltpu.make_async_copy(left_in, left, table_sems.at[0]),
        pltpu.make_async_copy(right_in, right, table_sems.at[1]),
        pltpu.make_async_copy(probe_in, probe, table_sems.at[2]),
    ]
    for copy in tables:
        copy.start()

    live_slots = place[COUNT]

    def level_copy(i):
        return pltpu.make_async_copy(measured.at[0, 0, i], levels.at[i], level_sems.at[i])

    def start_level(i, carry):
        level_copy(i).start()
        return carry

    lax.fori_loop(0, live_slots, start_level, 0)
    if sides == 1:
        for ch in range(2):
            ext[ch * blocks + blocks - 1 - side_blocks[0]] = jnp.zeros((ext_rows, LANES), F32)
    grad[...] = jnp.zeros_like(grad)
    probe_sums[...] = jnp.zeros_like(probe_sums)
    for copy in copies + tables:
        copy.wait()
    lanes = lax.broadcasted_iota(jnp.int32, (CHUNK, LANES), 1)

    def put(stack, value, part, q, first):
        width = value.shape[1]
        high, low = split(value)
        rows_at = lambda block: slice(block * pr + q * CHUNK, block * pr + (q + 1) * CHUNK)
        here, there = slice(first, first + width), slice(pr + first, pr + first + width)
        if part == 0:
            stack[rows_at(0), here], stack[rows_at(1), there] = high, high
            stack[rows_at(2), here], stack[rows_at(3), there] = low, low
        else:
            stack[rows_at(0), there], stack[rows_at(1), here] = high, -high
            stack[rows_at(2), there], stack[rows_at(3), here] = low, -low

    def times_left(w):
        stack = jnp.concatenate([stacks[w][...], stacks[w][0 : 2 * pr]], axis=0)
        fields[w][...] = jnp.dot(left[...], stack, preferred_element_type=F32)

    def times_right(w):
        for q in range(pr // CHUNK):
            cut = slice(q * CHUNK, (q + 1) * CHUNK)
            high, low = split(fields[w][cut, :])
            wides[w][cut, 0 : 2 * pr] = high
            wides[w][cut, 2 * pr : 4 * pr] = low
        stack = jnp.concatenate([wides[w][...], wides[w][:, 0 : 2 * pr]], axis=1)
        fields[w][...] = jnp.dot(stack, right[...], preferred_element_type=F32)

    def load(w, k):
        row, col = place[ROWS + k], place[COLS + k]
        shift, block = col & (LANES - 1), col >> 7
        back = (LANES - shift) & (LANES - 1)
        keep = lanes < LANES - shift
        for q in range(pr // CHUNK):
            cut = slice(q * CHUNK, (q + 1) * CHUNK)
            here = pl.ds(row + q * CHUNK, CHUNK)
            seen = []
            for ch in range(2):
                turned = [
                    pltpu.roll(ext[ch * blocks + block + j, here, :], back, 1)
                    for j in range(pieces + 1)
                ]
                seen.append([jnp.where(keep, turned[j], turned[j + 1]) for j in range(pieces)])
            for j in range(pieces):
                part = slice(j * LANES, (j + 1) * LANES)
                probe_real, probe_imag = probe[0, cut, part], probe[1, cut, part]
                real, imag = seen[0][j], seen[1][j]
                patches[w][0, cut, part], patches[w][1, cut, part] = real, imag
                exit_real = probe_real * real - probe_imag * imag
                exit_imag = probe_real * imag + probe_imag * real
                exits[w][0, cut, part], exits[w][1, cut, part] = exit_real, exit_imag
                put(stacks[w], exit_real, 0, q, j * LANES)
                put(stacks[w], exit_imag, 1, q, j * LANES)

    def project(w, k):
        for q in range(pr // CHUNK):
            cut = slice(q * CHUNK, (q + 1) * CHUNK)
            real, imag = fields[w][cut, 0:pr], fields[w][cut, pr : 2 * pr]
            factor = jnp.sqrt(levels[k, cut, :]) * lax.rsqrt(real * real + imag * imag + 1.0)
            put(stacks[w], real * factor, 0, q, 0)
            put(stacks[w], -(imag * factor), 1, q, 0)

    def finish(w, k, live):
        row, col = place[ROWS + k], place[COLS + k]
        shift, block = col & (LANES - 1), col >> 7
        low = lanes < shift
        zero = jnp.zeros((CHUNK, LANES), F32)
        for q in range(pr // CHUNK):
            cut = slice(q * CHUNK, (q + 1) * CHUNK)
            here = pl.ds(row + q * CHUNK, CHUNK)
            turned = [[], []]
            for j in range(pieces):
                part = slice(j * LANES, (j + 1) * LANES)
                other = slice(pr + j * LANES, pr + (j + 1) * LANES)
                diff_real = fields[w][cut, part] - exits[w][0, cut, part]
                diff_imag = -fields[w][cut, other] - exits[w][1, cut, part]
                real, imag = patches[w][0, cut, part], patches[w][1, cut, part]
                weight = real * real + imag * imag
                if live is not None:
                    diff_real, diff_imag = diff_real * live, diff_imag * live
                    weight = weight * live
                probe_real, probe_imag = probe[0, cut, part], probe[1, cut, part]
                turned[0].append(pltpu.roll(probe_real * diff_real + probe_imag * diff_imag, shift, 1))
                turned[1].append(pltpu.roll(probe_real * diff_imag - probe_imag * diff_real, shift, 1))
                probe_sums[j, 0, cut, :] += real * diff_real + imag * diff_imag
                probe_sums[j, 1, cut, :] += real * diff_imag - imag * diff_real
                probe_sums[j, 2, cut, :] += weight
            for ch in range(2):
                at = ch * blocks + block
                grad[at, here, :] += jnp.where(low, zero, turned[ch][0])
                for j in range(1, pieces):
                    grad[at + j, here, :] += jnp.where(low, turned[ch][j - 1], turned[ch][j])
                grad[at + pieces, here, :] += jnp.where(low, turned[ch][-1], zero)

    def visit(i, carry):
        first = i * WAYS
        slots = [jnp.minimum(first + w, live_slots - 1) for w in range(WAYS)]
        lives = [None] + [jnp.where(first + w < live_slots, 1.0, 0.0) for w in range(1, WAYS)]
        for w in range(WAYS):

            @pl.when(first + w < live_slots)
            def _():
                level_copy(slots[w]).wait()

        for w in range(WAYS):
            load(w, slots[w])
            times_left(w)
        for w in range(WAYS):
            times_right(w)
        for w in range(WAYS):
            project(w, slots[w])
            times_left(w)
        for w in range(WAYS):
            times_right(w)
        for w in range(WAYS):
            finish(w, slots[w], lives[w])
        return carry

    lax.fori_loop(0, (live_slots + WAYS - 1) // WAYS, visit, 0)
    for ch in range(2):
        for b in range(own_blocks):
            at, cut = ch * blocks + 1 + b, slice(b * LANES, (b + 1) * LANES)
            middle[ch, :, cut] = grad[at, own, :]
            near_rim[ch, :, cut] = grad[at, near_rows, :]
            far_rim[ch, :, cut] = grad[at, far_rows, :]
        for s in range(sides):
            at = ch * blocks + side_blocks[s]
            cut = slice(tile_cols + s * LANES, tile_cols + (s + 1) * LANES)
            side_out[s][ch] = grad[at, own, :]
            near_rim[ch, :, cut] = grad[at, near_rows, :]
            far_rim[ch, :, cut] = grad[at, far_rows, :]


def positions_call(place, tile, near, far_side, side_in, near_corners, far_corners, probe, measured):
    pr = probe.shape[1]
    sides = len(side_in)
    tile_rows, tile_cols = tile.shape[1:]
    ext_rows = tile_rows + 2 * H
    blocks = (tile_cols + 2 * H) // LANES
    left, right = (jnp.asarray(table) for table in dft_tables(pr))
    shape = lambda *dims: jax.ShapeDtypeStruct(dims, F32)
    slots = measured.shape[2]
    rim = shape(2, H, tile_cols + sides * LANES)
    middle, near_rim, far_rim, info, *rest = pl.pallas_call(
        functools.partial(positions_kernel, sides),
        out_shape=(
            shape(2, tile_rows, tile_cols),
            rim,
            rim,
            shape(3 * sides + 2, INFO, LANES),
            *[shape(2, tile_rows, LANES)] * sides,
            shape(pr // LANES, 3, pr, LANES),
        ),
        in_specs=[SMEM, HBM] + [ANY] * (2 + 3 * sides) + [HBM] * 4,
        out_specs=(VMEM,) * (5 + sides),
        scratch_shapes=[
            *[pltpu.VMEM((2 * blocks, ext_rows, LANES), F32)] * 2,
            pltpu.VMEM(left.shape, BF),
            pltpu.VMEM(right.shape, BF),
            pltpu.VMEM((slots, pr, pr), F32),
            pltpu.VMEM(probe.shape, F32),
            pltpu.SemaphoreType.DMA((3,)),
            pltpu.SemaphoreType.DMA((slots,)),
            pltpu.SemaphoreType.DMA((6 * blocks + 3 * sides + 2,)),
            *[pltpu.VMEM((2, pr, pr), F32)] * (2 * WAYS),
            *[pltpu.VMEM((4 * pr, 2 * pr), BF)] * WAYS,
            *[pltpu.VMEM((pr, 4 * pr), BF)] * WAYS,
            *[pltpu.VMEM((pr, 2 * pr), F32)] * WAYS,
        ],
        compiler_params=pltpu.CompilerParams(vmem_limit_bytes=52 << 20),
        cost_estimate=pl.CostEstimate(
            flops=slots * 96 * pr * pr * pr, bytes_accessed=16_000_000, transcendentals=slots * 2 * pr * pr
        ),
        name="positions",
    )(place, tile, near, far_side, *side_in, *near_corners, *far_corners, probe, measured, left, right)
    return middle, near_rim, far_rim, rest[:sides], rest[sides], info


def update_kernel(sides, *refs):
    place, tile, middle, cover, peak, near, far_side = refs[:7]
    side_in = refs[7 : 7 + sides]
    own_terms, other_terms, probe, out, new_probe, sums = refs[7 + sides :]
    tile_rows, tile_cols = tile.shape[1:]
    own_blocks = tile_cols // LANES
    even = place[0] % 2 == 0
    sums[...] = middle[...]
    near_row = pl.multiple_of(jnp.where(even, tile_rows - H, 0), 8)
    far_row = pl.multiple_of(jnp.where(even, 0, tile_rows - H), 8)
    sums[:, pl.ds(near_row, H), :] += near[:, :, 0:tile_cols]
    sums[:, pl.ds(far_row, H), :] += far_side[:, :, 0:tile_cols]
    for s in range(sides):
        if sides == 1:
            for edge, where in ((0, own_blocks - 1), (1, 0)):

                @pl.when((place[1] == 0) == (edge == 0))
                def _():
                    sums[:, :, where * LANES : (where + 1) * LANES] += side_in[s][...]
        else:
            where = 0 if s == 0 else own_blocks - 1
            sums[:, :, where * LANES : (where + 1) * LANES] += side_in[s][...]
    rows = own_terms.shape[0]
    top = MIX_OBJECT * jnp.maximum(peak[0:1, 0:1], other_terms[rows : rows + 1, 0:1])
    inverse = 1.0 / ((1.0 - MIX_OBJECT) * cover[...] + top)
    for ch in range(2):
        out[ch] = tile[ch] + sums[ch] * inverse

    pr = probe.shape[1]
    pieces = pr // LANES
    both = (own_terms, other_terms)

    def update(parts):
        flat = [parts[j * len(parts) // pieces] for j in range(pieces)]
        span = flat[0].shape[0] // (pieces // len(parts))
        term = lambda j, ch: flat[j][(j % (pieces // len(parts))) * span + ch * pr :][:pr]
        weights = [term(j, 2) for j in range(pieces)]
        best = functools.reduce(jnp.maximum, weights)
        best = jnp.max(jnp.max(best.reshape(-1, 8, LANES), axis=0), keepdims=True)
        for j in range(pieces):
            cut = slice(j * LANES, (j + 1) * LANES)
            scale = 1.0 / ((1.0 - MIX_PROBE) * weights[j] + MIX_PROBE * best)
            for ch in range(2):
                new_probe[ch, :, cut] = probe[ch, :, cut] + term(j, ch) * scale

    for first in (0, 1):

        @pl.when(place[0] % 2 == first)
        def _():
            update([both[first][0:rows, :], both[1 - first][0:rows, :]])


def update_call(place, tile, middle, cover, peak, near, far_side, side_in, own_terms, other_terms, probe):
    sides = len(side_in)
    return pl.pallas_call(
        functools.partial(update_kernel, sides),
        out_shape=(jax.ShapeDtypeStruct(tile.shape, F32), jax.ShapeDtypeStruct(probe.shape, F32)),
        in_specs=[SMEM] + [VMEM] * (9 + sides),
        out_specs=(VMEM, VMEM),
        scratch_shapes=[pltpu.VMEM(tile.shape, F32)],
        compiler_params=pltpu.CompilerParams(vmem_limit_bytes=32 << 20),
        name="update",
    )(place, tile, middle, cover, peak, near, far_side, *side_in, own_terms, other_terms, probe)


WIDE = ("rest", "core")
CHIPS = ("rest", "narrow")


def swap(x, axis, first):
    size = lax.axis_size(axis)
    pairs = []
    for i in range(first, size - 1, 2):
        pairs += [(i, i + 1), (i + 1, i)]
    return lax.ppermute(x, axis, pairs)


def shifted(x, axis, by):
    size = lax.axis_size(axis)
    return lax.ppermute(x, axis, [(i, i + by) for i in range(size) if 0 <= i + by < size])


def to_sides(pieces):
    if len(pieces) == 1:
        return [swap(pieces[0], "narrow", 0)]
    return [shifted(pieces[1], "narrow", 1), shifted(pieces[0], "narrow", -1)]


def to_corners(bands, first):
    wide, narrow = lax.axis_size(WIDE), lax.axis_size("narrow")
    steps = [0] if len(bands) == 1 else [-1, 1]
    got = []
    for s, step in enumerate(steps):
        pairs = []
        for i in range(first, wide - 1, 2):
            for n in range(narrow):
                m = 1 - n if step == 0 else n - step
                if 0 <= m < narrow:
                    pairs += [(i * narrow + n, (i + 1) * narrow + m), ((i + 1) * narrow + n, i * narrow + m)]
        band = bands[0] if step == 0 else bands[1 - s]
        got.append(lax.ppermute(band, (*WIDE, "narrow"), pairs))
    return got


def half_of(x, which):
    rows = x.shape[0] // 2
    return lax.dynamic_slice_in_dim(x, which * rows, rows, axis=0)


def chip_exchange(chunks):
    return lax.all_to_all(chunks.reshape(-1, LANES), CHIPS, 0, 0, tiled=True).reshape(chunks.shape)


def after(x, *others):
    return lax.optimization_barrier((x, *others))[0]


def body(tile, probe, measured, rows, cols, counts):
    wide, narrow = lax.axis_index(WIDE), lax.axis_index("narrow")
    sides = 1 if lax.axis_size("narrow") == 2 else 2
    tile_rows, tile_cols = tile.shape[1:]
    even = wide % 2 == 0
    place = jnp.concatenate(
        [jnp.stack([wide, narrow, counts[0, 0]]).astype(jnp.int32), rows.reshape(-1), cols.reshape(-1)]
    )

    far_band, near_band, edges, far_ends, near_ends = pack_call(place, tile, sides)
    far_side = swap(far_band, WIDE, 1)
    far_corners = to_corners(far_ends, 1)
    side_in = to_sides(edges)
    near_corners = to_corners(near_ends, 0)
    near = swap(near_band, "core", 0)

    middle, near_rim, far_rim, side_rims, probe_sums, got_info = positions_call(
        place, tile, near, far_side, side_in, near_corners, far_corners, probe, measured
    )
    own_info = edges[0][:1, tile_rows:]

    core = lax.axis_index("core")
    terms = probe_sums.reshape(-1, LANES)
    terms = half_of(terms, core) + swap(half_of(terms, 1 - core), "core", 0)
    near_got = swap(after(near_rim, terms), "core", 0)
    far_got = swap(after(far_rim, terms), WIDE, 1)
    info = jnp.concatenate([own_info, got_info], axis=0)[:, 0, :32].astype(jnp.int32)
    cover, peak = cover_call(place, after(info, terms), probe, tile_rows, tile_cols, sides)
    chips = lax.axis_size(CHIPS)
    got = chip_exchange(terms.reshape(chips, -1, LANES))
    chunk = jnp.sum(got, axis=0)
    rows_each = chunk.shape[0]
    chunk = after(jnp.concatenate([chunk, peak], axis=0), far_got, near_got)
    got = chip_exchange(jnp.broadcast_to(chunk, (chips, *chunk.shape)))
    terms = got[:, :rows_each].reshape(-1, LANES)
    peak = jnp.max(got[:, rows_each:], axis=0)

    def with_rims(piece, s):
        cut = slice(tile_cols + s * LANES, tile_cols + (s + 1) * LANES)
        below = jnp.where(even, near_got[:, :, cut], far_got[:, :, cut])
        above = jnp.where(even, far_got[:, :, cut], near_got[:, :, cut])
        return piece + jnp.concatenate([above, below], axis=1)

    side_got = to_sides([with_rims(piece, s) for s, piece in enumerate(side_rims)])
    other_terms = swap(after(jnp.concatenate([terms, peak], axis=0), *side_got), "core", 0)
    return update_call(
        place, tile, middle, cover, peak, near_got, far_got, side_got, terms, other_terms, probe
    )


def solution(mesh):
    wide, narrow = mesh.devices.shape
    fine = Mesh(mesh.devices.reshape(wide // 2, 2, narrow), ("rest", "core", "narrow"))
    placed = (
        P(None, WIDE, "narrow"),
        P(),
        P(WIDE, "narrow", None, None, None),
        P(WIDE, "narrow", None),
        P(WIDE, "narrow", None),
        P(WIDE, "narrow"),
    )
    return jax.shard_map(
        body,
        mesh=fine,
        in_specs=placed,
        out_specs=(P(None, WIDE, "narrow"), P()),
        check_vma=False,
    )
```

```python
import functools
import math

import jax
import jax.numpy as jnp
import ml_dtypes
import numpy as np
from jax import lax
from jax.experimental import pallas as pl
from jax.experimental.pallas import tpu as pltpu
from jax.sharding import Mesh, PartitionSpec as P

H = 128
LANES = 128
CHUNK = 32
WAYS = 2
INFO = 8
BF = jnp.bfloat16
F32 = jnp.float32
MIX_OBJECT = 0.5
MIX_PROBE = 0.5
VMEM = pl.BlockSpec(memory_space=pltpu.VMEM)
SMEM = pl.BlockSpec(memory_space=pltpu.SMEM)
ANY = pl.BlockSpec(memory_space=pl.ANY)
HBM = pl.BlockSpec(memory_space=pltpu.HBM)
COUNT, ROWS, COLS = 2, 3, 11


def rounded_pair(table):
    table = table.astype(np.float32)
    high = table.astype(ml_dtypes.bfloat16)
    low = (table - high.astype(np.float32)).astype(ml_dtypes.bfloat16)
    return high, low


def dft_tables(length):
    index = np.arange(length)
    angle = 2.0 * np.pi * ((index[:, None] * index[None, :]) % length) / length
    cos_high, cos_low = rounded_pair(np.cos(angle) / math.sqrt(length))
    sin_high, sin_low = rounded_pair(-np.sin(angle) / math.sqrt(length))
    left = np.concatenate([cos_high, sin_high, cos_high, sin_high, cos_low, sin_low], axis=1)
    right_high = np.block([[cos_high, sin_high], [-sin_high, cos_high]])
    right_low = np.block([[cos_low, sin_low], [-sin_low, cos_low]])
    right = np.concatenate([right_high, right_high, right_low], axis=0)
    return left, right


def split(x):
    high = x.astype(BF)
    return high, (x - high.astype(F32)).astype(BF)


def side_block(place, side, sides, blocks):
    if sides == 1:
        return jnp.where(place[1] == 0, blocks - 1, 0)
    return 0 if side == 0 else blocks - 1


def side_step(place, side, sides):
    if sides == 1:
        return jnp.where(place[1] == 0, 1, -1)
    return -1 if side == 0 else 1


def cover_kernel(tile_rows, tile_cols, sides, place, info, probe, cover, peak, total, power):
    pr = probe.shape[1]
    pieces = pr // LANES
    for j in range(pieces):
        cut = slice(j * LANES, (j + 1) * LANES)
        power[j] = probe[0, :, cut] * probe[0, :, cut] + probe[1, :, cut] * probe[1, :, cut]
    total[...] = jnp.zeros_like(total)
    lanes = lax.broadcasted_iota(jnp.int32, (CHUNK, LANES), 1)
    even = place[0] % 2 == 0
    steps_down = (0, jnp.where(even, 1, -1), jnp.where(even, -1, 1))
    steps_right = (0,) + tuple(side_step(place, s, sides) for s in range(sides))
    for v in range(3):
        for h in range(1 + sides):
            source = v * (1 + sides) + h
            down, right = steps_down[v], steps_right[h]

            def visit(k, carry):
                row = info[source, k] + pr - H + down * tile_rows
                col = info[source, 8 + k] + pr - H + right * tile_cols
                inside = (row > 0) & (row < pr + tile_rows) & (col > 0) & (col < pr + tile_cols)

                @pl.when(inside)
                def _():
                    shift = col & (LANES - 1)
                    block = col >> 7
                    low = lanes < shift
                    for q in range(pr // CHUNK):
                        turned = [
                            pltpu.roll(power[j, q * CHUNK : (q + 1) * CHUNK, :], shift, 1)
                            for j in range(pieces)
                        ]
                        here = pl.ds(row + q * CHUNK, CHUNK)
                        zero = jnp.zeros((CHUNK, LANES), F32)
                        total[block, here, :] += jnp.where(low, zero, turned[0])
                        for j in range(1, pieces):
                            total[block + j, here, :] += jnp.where(low, turned[j - 1], turned[j])
                        total[block + pieces, here, :] += jnp.where(low, turned[-1], zero)

                return carry

            lax.fori_loop(0, info[source, 16], visit, 0)
    first = pr // LANES
    best = jnp.zeros((8, LANES), F32)
    for b in range(tile_cols // LANES):
        own = total[first + b, pr : pr + tile_rows, :]
        cover[:, b * LANES : (b + 1) * LANES] = own
        best = jnp.maximum(best, jnp.max(own.reshape(tile_rows // 8, 8, LANES), axis=0))
    peak[...] = jnp.full((8, LANES), jnp.max(best), F32)


def cover_call(place, info, probe, tile_rows, tile_cols, sides):
    pr = probe.shape[1]
    blocks = (tile_cols + 2 * pr) // LANES + 1
    return pl.pallas_call(
        functools.partial(cover_kernel, tile_rows, tile_cols, sides),
        out_shape=(
            jax.ShapeDtypeStruct((tile_rows, tile_cols), F32),
            jax.ShapeDtypeStruct((8, LANES), F32),
        ),
        in_specs=[SMEM, SMEM, VMEM],
        out_specs=(VMEM, VMEM),
        scratch_shapes=[
            pltpu.VMEM((blocks, tile_rows + 2 * pr, LANES), F32),
            pltpu.VMEM((pr // LANES, pr, LANES), F32),
        ],
        compiler_params=pltpu.CompilerParams(vmem_limit_bytes=24 << 20),
        cost_estimate=pl.CostEstimate(flops=4_000_000, bytes_accessed=8_000_000, transcendentals=0),
        name="cover",
    )(place, info, probe)


def pack_kernel(sides, place, tile, *refs):
    far_band, near_band = refs[:2]
    edges, far_ends, near_ends = [refs[2 + i * sides : 2 + (i + 1) * sides] for i in range(3)]
    sems = refs[2 + 3 * sides]
    tile_rows, tile_cols = tile.shape[1:]
    even = place[0] % 2 == 0
    near_start = pl.multiple_of(jnp.where(even, tile_rows - H, 0), 8)
    far_start = pl.multiple_of(jnp.where(even, 0, tile_rows - H), 8)
    if sides == 1:
        starts = [pl.multiple_of(jnp.where(place[1] == 0, tile_cols - H, 0), LANES)]
    else:
        starts = [0, tile_cols - H]
    bands = [(far_band, far_start, H, 0), (near_band, near_start, H, 0)]
    for s, start in enumerate(starts):
        bands += [(edges[s], 0, tile_rows, start), (far_ends[s], far_start, H, start)]
        bands += [(near_ends[s], near_start, H, start)]
    copies = []
    for i, (band, row, height, col) in enumerate(bands):
        copies.append(
            pltpu.make_async_copy(
                tile.at[:, pl.ds(row, height), pl.ds(col, band.shape[2])], band.at[:, pl.ds(0, height), :], sems.at[i]
            )
        )
        copies[-1].start()
    lanes = lax.broadcasted_iota(jnp.int32, (INFO, LANES), 1)
    notes = jnp.where(lanes == 16, place[COUNT], 0)
    for k in range(8):
        notes = jnp.where(lanes == k, place[ROWS + k], jnp.where(lanes == 8 + k, place[COLS + k], notes))
    notes = notes.astype(F32)
    for band, row, height, col in bands:
        for ch in range(2):
            band[ch, height : height + INFO, 0:LANES] = notes
            if band.shape[2] > LANES:
                band[ch, height : height + INFO, LANES:] = jnp.zeros((INFO, band.shape[2] - LANES), F32)
    for copy in copies:
        copy.wait()


def pack_call(place, tile, sides):
    tile_rows, tile_cols = tile.shape[1:]
    shape = lambda height, width: jax.ShapeDtypeStruct((2, height + INFO, width), F32)
    shapes = [shape(H, tile_cols)] * 2 + [shape(tile_rows, LANES)] * sides + [shape(H, LANES)] * (2 * sides)
    out = pl.pallas_call(
        functools.partial(pack_kernel, sides),
        out_shape=shapes,
        in_specs=[SMEM, HBM],
        out_specs=[VMEM] * len(shapes),
        scratch_shapes=[pltpu.SemaphoreType.DMA((len(shapes),))],
        compiler_params=pltpu.CompilerParams(vmem_limit_bytes=8 << 20),
        name="pack",
    )(place, tile)
    return out[0], out[1], *[list(out[2 + i * sides : 2 + (i + 1) * sides]) for i in range(3)]


def positions_kernel(sides, *refs):
    place, tile, near, far_side = refs[:4]
    side_in, near_corners, far_corners = [refs[4 + i * sides : 4 + (i + 1) * sides] for i in range(3)]
    probe_in, measured, left_in, right_in = refs[4 + 3 * sides : 8 + 3 * sides]
    middle, near_rim, far_rim, info = refs[8 + 3 * sides : 12 + 3 * sides]
    side_out = refs[12 + 3 * sides : 12 + 4 * sides]
    kept, sent, probe_sums, ext, grad = refs[12 + 4 * sides : 17 + 4 * sides]
    scratch = refs[17 + 4 * sides :]
    left, right, levels, probe = scratch[:4]
    table_sems, level_sems, ext_sems = scratch[4:7]
    scratch = scratch[7:]
    patches, exits, stacks, wides, fields = [scratch[i * WAYS : (i + 1) * WAYS] for i in range(5)]

    pr = probe_in.shape[1]
    pieces = pr // LANES
    ext_rows = ext.shape[1]
    blocks = ext.shape[0] // 2
    own_blocks = blocks - 2
    tile_rows, tile_cols = ext_rows - 2 * H, own_blocks * LANES
    even = place[0] % 2 == 0
    near_row = pl.multiple_of(jnp.where(even, tile_rows + H, 0), 8)
    far_row = pl.multiple_of(jnp.where(even, 0, tile_rows + H), 8)
    side_blocks = [side_block(place, s, sides, blocks) for s in range(sides)]
    own, near_rows, far_rows = pl.ds(H, tile_rows), pl.ds(near_row, H), pl.ds(far_row, H)

    copies = []

    def fetch(source, target):
        copies.append(pltpu.make_async_copy(source, target, ext_sems.at[len(copies)]))
        copies[-1].start()

    for ch in range(2):
        for b in range(own_blocks):
            at, cut = ch * blocks + 1 + b, pl.ds(b * LANES, LANES)
            fetch(tile.at[ch, :, cut], ext.at[at, own, :])
            fetch(near.at[ch, pl.ds(0, H), cut], ext.at[at, near_rows, :])
            fetch(far_side.at[ch, pl.ds(0, H), cut], ext.at[at, far_rows, :])
        for s in range(sides):
            at = ch * blocks + side_blocks[s]
            fetch(side_in[s].at[ch, pl.ds(0, tile_rows), :], ext.at[at, own, :])
            fetch(near_corners[s].at[ch, pl.ds(0, H), :], ext.at[at, near_rows, :])
            fetch(far_corners[s].at[ch, pl.ds(0, H), :], ext.at[at, far_rows, :])
    for s in range(sides):
        fetch(side_in[s].at[0, pl.ds(tile_rows, INFO), :], info.at[s])
        fetch(near_corners[s].at[0, pl.ds(H, INFO), :], info.at[sides + 1 + s])
        fetch(far_corners[s].at[0, pl.ds(H, INFO), :], info.at[2 * sides + 2 + s])
    fetch(near.at[0, pl.ds(H, INFO), pl.ds(0, LANES)], info.at[sides])
    fetch(far_side.at[0, pl.ds(H, INFO), pl.ds(0, LANES)], info.at[2 * sides + 1])
    tables = [
        pltpu.make_async_copy(left_in, left, table_sems.at[0]),
        pltpu.make_async_copy(right_in, right, table_sems.at[1]),
        pltpu.make_async_copy(probe_in, probe, table_sems.at[2]),
    ]
    for copy in tables:
        copy.start()

    live_slots = place[COUNT]

    def level_copy(i):
        return pltpu.make_async_copy(measured.at[0, 0, i], levels.at[i], level_sems.at[i])

    def start_level(i, carry):
        level_copy(i).start()
        return carry

    lax.fori_loop(0, live_slots, start_level, 0)
    if sides == 1:
        for ch in range(2):
            ext[ch * blocks + blocks - 1 - side_blocks[0]] = jnp.zeros((ext_rows, LANES), F32)
    grad[...] = jnp.zeros_like(grad)
    probe_sums[...] = jnp.zeros_like(probe_sums)
    for copy in copies:
        copy.wait()
    tables[2].wait()
    lanes = lax.broadcasted_iota(jnp.int32, (CHUNK, LANES), 1)

    def put(stack, value, part, q, first):
        width = value.shape[1]
        high, low = split(value)
        rows_at = lambda block: slice(block * pr + q * CHUNK, block * pr + (q + 1) * CHUNK)
        here, there = slice(first, first + width), slice(pr + first, pr + first + width)
        if part == 0:
            stack[rows_at(0), here], stack[rows_at(1), there] = high, high
            stack[rows_at(2), here], stack[rows_at(3), there] = low, low
        else:
            stack[rows_at(0), there], stack[rows_at(1), here] = high, -high
            stack[rows_at(2), there], stack[rows_at(3), here] = low, -low

    def times_left(w):
        stack = jnp.concatenate([stacks[w][...], stacks[w][0 : 2 * pr]], axis=0)
        fields[w][...] = jnp.dot(left[...], stack, preferred_element_type=F32)

    def times_right(w):
        for q in range(pr // CHUNK):
            cut = slice(q * CHUNK, (q + 1) * CHUNK)
            high, low = split(fields[w][cut, :])
            wides[w][cut, 0 : 2 * pr] = high
            wides[w][cut, 2 * pr : 4 * pr] = low
        stack = jnp.concatenate([wides[w][...], wides[w][:, 0 : 2 * pr]], axis=1)
        fields[w][...] = jnp.dot(stack, right[...], preferred_element_type=F32)

    def load(w, k):
        row, col = place[ROWS + k], place[COLS + k]
        shift, block = col & (LANES - 1), col >> 7
        back = (LANES - shift) & (LANES - 1)
        keep = lanes < LANES - shift
        for q in range(pr // CHUNK):
            cut = slice(q * CHUNK, (q + 1) * CHUNK)
            here = pl.ds(row + q * CHUNK, CHUNK)
            seen = []
            for ch in range(2):
                turned = [
                    pltpu.roll(ext[ch * blocks + block + j, here, :], back, 1)
                    for j in range(pieces + 1)
                ]
                seen.append([jnp.where(keep, turned[j], turned[j + 1]) for j in range(pieces)])
            for j in range(pieces):
                part = slice(j * LANES, (j + 1) * LANES)
                probe_real, probe_imag = probe[0, cut, part], probe[1, cut, part]
                real, imag = seen[0][j], seen[1][j]
                patches[w][0, cut, part], patches[w][1, cut, part] = real, imag
                exit_real = probe_real * real - probe_imag * imag
                exit_imag = probe_real * imag + probe_imag * real
                exits[w][0, cut, part], exits[w][1, cut, part] = exit_real, exit_imag
                put(stacks[w], exit_real, 0, q, j * LANES)
                put(stacks[w], exit_imag, 1, q, j * LANES)

    def project(w, k):
        for q in range(pr // CHUNK):
            cut = slice(q * CHUNK, (q + 1) * CHUNK)
            real, imag = fields[w][cut, 0:pr], fields[w][cut, pr : 2 * pr]
            factor = jnp.sqrt(levels[k, cut, :]) * lax.rsqrt(real * real + imag * imag + 1.0)
            put(stacks[w], real * factor, 0, q, 0)
            put(stacks[w], -(imag * factor), 1, q, 0)

    def finish(w, k, live):
        row, col = place[ROWS + k], place[COLS + k]
        shift, block = col & (LANES - 1), col >> 7
        low = lanes < shift
        zero = jnp.zeros((CHUNK, LANES), F32)
        for q in range(pr // CHUNK):
            cut = slice(q * CHUNK, (q + 1) * CHUNK)
            here = pl.ds(row + q * CHUNK, CHUNK)
            turned = [[], []]
            for j in range(pieces):
                part = slice(j * LANES, (j + 1) * LANES)
                other = slice(pr + j * LANES, pr + (j + 1) * LANES)
                diff_real = fields[w][cut, part] - exits[w][0, cut, part]
                diff_imag = -fields[w][cut, other] - exits[w][1, cut, part]
                real, imag = patches[w][0, cut, part], patches[w][1, cut, part]
                weight = real * real + imag * imag
                if live is not None:
                    diff_real, diff_imag = diff_real * live, diff_imag * live
                    weight = weight * live
                probe_real, probe_imag = probe[0, cut, part], probe[1, cut, part]
                turned[0].append(pltpu.roll(probe_real * diff_real + probe_imag * diff_imag, shift, 1))
                turned[1].append(pltpu.roll(probe_real * diff_imag - probe_imag * diff_real, shift, 1))
                probe_sums[j, 0, cut, :] += real * diff_real + imag * diff_imag
                probe_sums[j, 1, cut, :] += real * diff_imag - imag * diff_real
                probe_sums[j, 2, cut, :] += weight
            for ch in range(2):
                at = ch * blocks + block
                grad[at, here, :] += jnp.where(low, zero, turned[ch][0])
                for j in range(1, pieces):
                    grad[at + j, here, :] += jnp.where(low, turned[ch][j - 1], turned[ch][j])
                grad[at + pieces, here, :] += jnp.where(low, turned[ch][-1], zero)

    def visit(i, carry):
        first = i * WAYS
        slots = [jnp.minimum(first + w, live_slots - 1) for w in range(WAYS)]
        lives = [None] + [jnp.where(first + w < live_slots, 1.0, 0.0) for w in range(1, WAYS)]
        for w in range(WAYS):

            @pl.when(first + w < live_slots)
            def _():
                level_copy(slots[w]).wait()

        @pl.when(i == 0)
        def _():
            tables[0].wait()
            tables[1].wait()

        for w in range(WAYS):
            load(w, slots[w])
            times_left(w)
        for w in range(WAYS):
            times_right(w)
        for w in range(WAYS):
            project(w, slots[w])
            times_left(w)
        for w in range(WAYS):
            times_right(w)
        for w in range(WAYS):
            finish(w, slots[w], lives[w])
        return carry

    lax.fori_loop(0, (live_slots + WAYS - 1) // WAYS, visit, 0)
    core = place[0] % 2
    span = pieces // 2
    for j in range(span):
        for ch in range(3):
            at = pl.ds((j * 3 + ch) * pr, pr)
            kept[at, :] = probe_sums[core * span + j, ch]
            sent[at, :] = probe_sums[(1 - core) * span + j, ch]
    for ch in range(2):
        for b in range(own_blocks):
            at, cut = ch * blocks + 1 + b, slice(b * LANES, (b + 1) * LANES)
            middle[ch, :, cut] = grad[at, own, :]
            near_rim[ch, :, cut] = grad[at, near_rows, :]
            far_rim[ch, :, cut] = grad[at, far_rows, :]
        for s in range(sides):
            at = ch * blocks + side_blocks[s]
            cut = slice(tile_cols + s * LANES, tile_cols + (s + 1) * LANES)
            side_out[s][ch] = grad[at, own, :]
            near_rim[ch, :, cut] = grad[at, near_rows, :]
            far_rim[ch, :, cut] = grad[at, far_rows, :]


def positions_call(place, tile, near, far_side, side_in, near_corners, far_corners, probe, measured):
    pr = probe.shape[1]
    sides = len(side_in)
    tile_rows, tile_cols = tile.shape[1:]
    ext_rows = tile_rows + 2 * H
    blocks = (tile_cols + 2 * H) // LANES
    left, right = (jnp.asarray(table) for table in dft_tables(pr))
    shape = lambda *dims: jax.ShapeDtypeStruct(dims, F32)
    slots = measured.shape[2]
    rim = shape(2, H, tile_cols + sides * LANES)
    middle, near_rim, far_rim, info, *rest = pl.pallas_call(
        functools.partial(positions_kernel, sides),
        out_shape=(
            shape(2, tile_rows, tile_cols),
            rim,
            rim,
            shape(3 * sides + 2, INFO, LANES),
            *[shape(2, tile_rows, LANES)] * sides,
            shape(3 * pr * pr // LANES // 2, LANES),
            shape(3 * pr * pr // LANES // 2, LANES),
        ),
        in_specs=[SMEM, HBM] + [ANY] * (2 + 3 * sides) + [HBM] * 4,
        out_specs=(VMEM,) * (6 + sides),
        scratch_shapes=[
            pltpu.VMEM((pr // LANES, 3, pr, LANES), F32),
            *[pltpu.VMEM((2 * blocks, ext_rows, LANES), F32)] * 2,
            pltpu.VMEM(left.shape, BF),
            pltpu.VMEM(right.shape, BF),
            pltpu.VMEM((slots, pr, pr), F32),
            pltpu.VMEM(probe.shape, F32),
            pltpu.SemaphoreType.DMA((3,)),
            pltpu.SemaphoreType.DMA((slots,)),
            pltpu.SemaphoreType.DMA((6 * blocks + 3 * sides + 2,)),
            *[pltpu.VMEM((2, pr, pr), F32)] * (2 * WAYS),
            *[pltpu.VMEM((4 * pr, 2 * pr), BF)] * WAYS,
            *[pltpu.VMEM((pr, 4 * pr), BF)] * WAYS,
            *[pltpu.VMEM((pr, 2 * pr), F32)] * WAYS,
        ],
        compiler_params=pltpu.CompilerParams(vmem_limit_bytes=52 << 20),
        cost_estimate=pl.CostEstimate(
            flops=slots * 96 * pr * pr * pr, bytes_accessed=16_000_000, transcendentals=slots * 2 * pr * pr
        ),
        name="positions",
    )(place, tile, near, far_side, *side_in, *near_corners, *far_corners, probe, measured, left, right)
    return middle, near_rim, far_rim, rest[:sides], rest[sides], rest[sides + 1], info


def update_kernel(sides, *refs):
    place, tile, middle, cover, near, far_side = refs[:6]
    side_in = refs[6 : 6 + sides]
    own_got, other_got, probe, out, new_probe, sums = refs[6 + sides :]
    tile_rows, tile_cols = tile.shape[1:]
    own_blocks = tile_cols // LANES
    even = place[0] % 2 == 0
    sums[...] = middle[...]
    near_row = pl.multiple_of(jnp.where(even, tile_rows - H, 0), 8)
    far_row = pl.multiple_of(jnp.where(even, 0, tile_rows - H), 8)
    sums[:, pl.ds(near_row, H), :] += near[:, :, 0:tile_cols]
    sums[:, pl.ds(far_row, H), :] += far_side[:, :, 0:tile_cols]
    for s in range(sides):
        if sides == 1:
            for edge, where in ((0, own_blocks - 1), (1, 0)):

                @pl.when((place[1] == 0) == (edge == 0))
                def _():
                    sums[:, :, where * LANES : (where + 1) * LANES] += side_in[s][...]
        else:
            where = 0 if s == 0 else own_blocks - 1
            sums[:, :, where * LANES : (where + 1) * LANES] += side_in[s][...]
    rows = own_got.shape[1] - 8
    peak = jnp.maximum(jnp.max(own_got[:, rows:, :], axis=0), jnp.max(other_got[:, rows:, :], axis=0))
    top = MIX_OBJECT * jnp.max(peak, keepdims=True)
    inverse = 1.0 / ((1.0 - MIX_OBJECT) * cover[...] + top)
    for ch in range(2):
        out[ch] = tile[ch] + sums[ch] * inverse

    pr = probe.shape[1]
    pieces = pr // LANES
    both = [ref[:, 0:rows, :].reshape(-1, LANES) for ref in (own_got, other_got)]

    def update(parts):
        flat = [parts[j * len(parts) // pieces] for j in range(pieces)]
        span = flat[0].shape[0] // (pieces // len(parts))
        term = lambda j, ch: flat[j][(j % (pieces // len(parts))) * span + ch * pr :][:pr]
        weights = [term(j, 2) for j in range(pieces)]
        best = functools.reduce(jnp.maximum, weights)
        best = jnp.max(jnp.max(best.reshape(-1, 8, LANES), axis=0), keepdims=True)
        for j in range(pieces):
            cut = slice(j * LANES, (j + 1) * LANES)
            scale = 1.0 / ((1.0 - MIX_PROBE) * weights[j] + MIX_PROBE * best)
            for ch in range(2):
                new_probe[ch, :, cut] = probe[ch, :, cut] + term(j, ch) * scale

    for first in (0, 1):

        @pl.when(place[0] % 2 == first)
        def _():
            update([both[first], both[1 - first]])


def update_call(place, tile, middle, cover, near, far_side, side_in, own, other, probe):
    sides = len(side_in)
    return pl.pallas_call(
        functools.partial(update_kernel, sides),
        out_shape=(jax.ShapeDtypeStruct(tile.shape, F32), jax.ShapeDtypeStruct(probe.shape, F32)),
        in_specs=[SMEM] + [VMEM] * (8 + sides),
        out_specs=(VMEM, VMEM),
        scratch_shapes=[pltpu.VMEM(tile.shape, F32)],
        compiler_params=pltpu.CompilerParams(vmem_limit_bytes=32 << 20),
        name="update",
    )(place, tile, middle, cover, near, far_side, *side_in, own, other, probe)


WIDE = ("rest", "core")
CHIPS = ("rest", "narrow")


def swap(x, axis, first):
    size = lax.axis_size(axis)
    pairs = []
    for i in range(first, size - 1, 2):
        pairs += [(i, i + 1), (i + 1, i)]
    return lax.ppermute(x, axis, pairs)


def shifted(x, axis, by):
    size = lax.axis_size(axis)
    return lax.ppermute(x, axis, [(i, i + by) for i in range(size) if 0 <= i + by < size])


def to_sides(pieces):
    if len(pieces) == 1:
        return [swap(pieces[0], "narrow", 0)]
    return [shifted(pieces[1], "narrow", 1), shifted(pieces[0], "narrow", -1)]


def to_corners(bands, first):
    wide, narrow = lax.axis_size(WIDE), lax.axis_size("narrow")
    steps = [0] if len(bands) == 1 else [-1, 1]
    got = []
    for s, step in enumerate(steps):
        pairs = []
        for i in range(first, wide - 1, 2):
            for n in range(narrow):
                m = 1 - n if step == 0 else n - step
                if 0 <= m < narrow:
                    pairs += [(i * narrow + n, (i + 1) * narrow + m), ((i + 1) * narrow + n, i * narrow + m)]
        band = bands[0] if step == 0 else bands[1 - s]
        got.append(lax.ppermute(band, (*WIDE, "narrow"), pairs))
    return got


def chip_exchange(chunks):
    return lax.all_to_all(chunks.reshape(-1, LANES), CHIPS, 0, 0, tiled=True).reshape(chunks.shape)


def after(x, *others):
    return lax.optimization_barrier((x, *others))[0]


def body(tile, probe, measured, rows, cols, counts):
    wide, narrow = lax.axis_index(WIDE), lax.axis_index("narrow")
    sides = 1 if lax.axis_size("narrow") == 2 else 2
    tile_rows, tile_cols = tile.shape[1:]
    even = wide % 2 == 0
    place = jnp.concatenate(
        [jnp.stack([wide, narrow, counts[0, 0]]).astype(jnp.int32), rows.reshape(-1), cols.reshape(-1)]
    )

    far_band, near_band, edges, far_ends, near_ends = pack_call(place, tile, sides)
    far_side = swap(far_band, WIDE, 1)
    far_corners = to_corners(far_ends, 1)
    side_in = to_sides(edges)
    near_corners = to_corners(near_ends, 0)
    near = swap(near_band, "core", 0)

    middle, near_rim, far_rim, side_rims, kept, sent, got_info = positions_call(
        place, tile, near, far_side, side_in, near_corners, far_corners, probe, measured
    )
    own_info = edges[0][:1, tile_rows:]

    terms = kept + swap(sent, "core", 0)
    near_got = swap(after(near_rim, terms), "core", 0)
    far_got = swap(after(far_rim, terms), WIDE, 1)
    info = jnp.concatenate([own_info, got_info], axis=0)[:, 0, :32].astype(jnp.int32)
    cover, peak = cover_call(place, after(info, terms), probe, tile_rows, tile_cols, sides)
    chips = lax.axis_size(CHIPS)
    got = chip_exchange(terms.reshape(chips, -1, LANES))
    chunk = jnp.sum(got, axis=0)
    rows_each = chunk.shape[0]
    chunk = after(jnp.concatenate([chunk, peak], axis=0), far_got, near_got)
    got = chip_exchange(jnp.broadcast_to(chunk, (chips, *chunk.shape)))
    if rows_each % 8:
        peak = jnp.max(got[:, rows_each:], axis=0)
        got = jnp.concatenate([got[:, :rows_each].reshape(-1, LANES), peak], axis=0)[None]

    def with_rims(piece, s):
        cut = slice(tile_cols + s * LANES, tile_cols + (s + 1) * LANES)
        below = jnp.where(even, near_got[:, :, cut], far_got[:, :, cut])
        above = jnp.where(even, far_got[:, :, cut], near_got[:, :, cut])
        return piece + jnp.concatenate([above, below], axis=1)

    side_got = to_sides([with_rims(piece, s) for s, piece in enumerate(side_rims)])
    other = swap(after(got, *side_got), "core", 0)
    return update_call(place, tile, middle, cover, near_got, far_got, side_got, got, other, probe)


def solution(mesh):
    wide, narrow = mesh.devices.shape
    fine = Mesh(mesh.devices.reshape(wide // 2, 2, narrow), ("rest", "core", "narrow"))
    placed = (
        P(None, WIDE, "narrow"),
        P(),
        P(WIDE, "narrow", None, None, None),
        P(WIDE, "narrow", None),
        P(WIDE, "narrow", None),
        P(WIDE, "narrow"),
    )
    return jax.shard_map(
        body,
        mesh=fine,
        in_specs=placed,
        out_specs=(P(None, WIDE, "narrow"), P()),
        check_vma=False,
    )
```

```python
import functools
import math

import jax
import jax.numpy as jnp
import ml_dtypes
import numpy as np
from jax import lax
from jax.experimental import pallas as pl
from jax.experimental.pallas import tpu as pltpu
from jax.sharding import Mesh, PartitionSpec as P

H = 128
LANES = 128
CHUNK = 32
WAYS = 2
INFO = 8
GRANT = 50176 << 10
BF = jnp.bfloat16
F32 = jnp.float32
MIX_OBJECT = 0.5
MIX_PROBE = 0.5
VMEM = pl.BlockSpec(memory_space=pltpu.VMEM)
SMEM = pl.BlockSpec(memory_space=pltpu.SMEM)
ANY = pl.BlockSpec(memory_space=pl.ANY)
HBM = pl.BlockSpec(memory_space=pltpu.HBM)
COUNT, ROWS, COLS = 2, 3, 11


def rounded_pair(table):
    table = table.astype(np.float32)
    high = table.astype(ml_dtypes.bfloat16)
    low = (table - high.astype(np.float32)).astype(ml_dtypes.bfloat16)
    return high, low


def dft_tables(length):
    index = np.arange(length)
    angle = 2.0 * np.pi * ((index[:, None] * index[None, :]) % length) / length
    cos_high, cos_low = rounded_pair(np.cos(angle) / math.sqrt(length))
    sin_high, sin_low = rounded_pair(-np.sin(angle) / math.sqrt(length))
    left = np.concatenate([cos_high, sin_high, cos_high, sin_high, cos_low, sin_low], axis=1)
    right_high = np.block([[cos_high, sin_high], [-sin_high, cos_high]])
    right_low = np.block([[cos_low, sin_low], [-sin_low, cos_low]])
    right = np.concatenate([right_high, right_high, right_low], axis=0)
    return left, right


def split(x):
    high = x.astype(BF)
    return high, (x - high.astype(F32)).astype(BF)


def side_block(place, side, sides, blocks):
    if sides == 1:
        return jnp.where(place[1] == 0, blocks - 1, 0)
    return 0 if side == 0 else blocks - 1


def side_step(place, side, sides):
    if sides == 1:
        return jnp.where(place[1] == 0, 1, -1)
    return -1 if side == 0 else 1


def cover_kernel(tile_rows, tile_cols, sides, place, info, probe, cover, peak, total, power):
    pr = probe.shape[1]
    pieces = pr // LANES
    for j in range(pieces):
        cut = slice(j * LANES, (j + 1) * LANES)
        power[j] = probe[0, :, cut] * probe[0, :, cut] + probe[1, :, cut] * probe[1, :, cut]
    total[...] = jnp.zeros_like(total)
    lanes = lax.broadcasted_iota(jnp.int32, (CHUNK, LANES), 1)
    even = place[0] % 2 == 0
    steps_down = (0, jnp.where(even, 1, -1), jnp.where(even, -1, 1))
    steps_right = (0,) + tuple(side_step(place, s, sides) for s in range(sides))
    for v in range(3):
        for h in range(1 + sides):
            source = v * (1 + sides) + h
            down, right = steps_down[v], steps_right[h]

            def visit(k, carry):
                row = info[source, k] + pr - H + down * tile_rows
                col = info[source, 8 + k] + pr - H + right * tile_cols
                inside = (row > 0) & (row < pr + tile_rows) & (col > 0) & (col < pr + tile_cols)

                @pl.when(inside)
                def _():
                    shift = col & (LANES - 1)
                    block = col >> 7
                    low = lanes < shift
                    for q in range(pr // CHUNK):
                        turned = [
                            pltpu.roll(power[j, q * CHUNK : (q + 1) * CHUNK, :], shift, 1)
                            for j in range(pieces)
                        ]
                        here = pl.ds(row + q * CHUNK, CHUNK)
                        zero = jnp.zeros((CHUNK, LANES), F32)
                        total[block, here, :] += jnp.where(low, zero, turned[0])
                        for j in range(1, pieces):
                            total[block + j, here, :] += jnp.where(low, turned[j - 1], turned[j])
                        total[block + pieces, here, :] += jnp.where(low, turned[-1], zero)

                return carry

            lax.fori_loop(0, info[source, 16], visit, 0)
    first = pr // LANES
    best = jnp.zeros((8, LANES), F32)
    for b in range(tile_cols // LANES):
        own = total[first + b, pr : pr + tile_rows, :]
        cover[:, b * LANES : (b + 1) * LANES] = own
        best = jnp.maximum(best, jnp.max(own.reshape(tile_rows // 8, 8, LANES), axis=0))
    peak[...] = jnp.full((8, LANES), jnp.max(best), F32)


def cover_call(place, info, probe, tile_rows, tile_cols, sides):
    pr = probe.shape[1]
    blocks = (tile_cols + 2 * pr) // LANES + 1
    return pl.pallas_call(
        functools.partial(cover_kernel, tile_rows, tile_cols, sides),
        out_shape=(
            jax.ShapeDtypeStruct((tile_rows, tile_cols), F32),
            jax.ShapeDtypeStruct((8, LANES), F32),
        ),
        in_specs=[SMEM, SMEM, VMEM],
        out_specs=(VMEM, VMEM),
        scratch_shapes=[
            pltpu.VMEM((blocks, tile_rows + 2 * pr, LANES), F32),
            pltpu.VMEM((pr // LANES, pr, LANES), F32),
        ],
        compiler_params=pltpu.CompilerParams(vmem_limit_bytes=16 << 20),
        cost_estimate=pl.CostEstimate(flops=4_000_000, bytes_accessed=8_000_000, transcendentals=0),
        name="cover",
    )(place, info, probe)


def pack_kernel(sides, place, tile, *refs):
    far_band, near_band = refs[:2]
    edges, far_ends, near_ends = [refs[2 + i * sides : 2 + (i + 1) * sides] for i in range(3)]
    sems = refs[2 + 3 * sides]
    tile_rows, tile_cols = tile.shape[1:]
    even = place[0] % 2 == 0
    near_start = pl.multiple_of(jnp.where(even, tile_rows - H, 0), 8)
    far_start = pl.multiple_of(jnp.where(even, 0, tile_rows - H), 8)
    if sides == 1:
        starts = [pl.multiple_of(jnp.where(place[1] == 0, tile_cols - H, 0), LANES)]
    else:
        starts = [0, tile_cols - H]
    bands = [(far_band, far_start, H, 0), (near_band, near_start, H, 0)]
    for s, start in enumerate(starts):
        bands += [(edges[s], 0, tile_rows, start), (far_ends[s], far_start, H, start)]
        bands += [(near_ends[s], near_start, H, start)]
    copies = []
    for i, (band, row, height, col) in enumerate(bands):
        copies.append(
            pltpu.make_async_copy(
                tile.at[:, pl.ds(row, height), pl.ds(col, band.shape[2])], band.at[:, pl.ds(0, height), :], sems.at[i]
            )
        )
        copies[-1].start()
    lanes = lax.broadcasted_iota(jnp.int32, (INFO, LANES), 1)
    notes = jnp.where(lanes == 16, place[COUNT], 0)
    for k in range(8):
        notes = jnp.where(lanes == k, place[ROWS + k], jnp.where(lanes == 8 + k, place[COLS + k], notes))
    notes = notes.astype(F32)
    for band, row, height, col in bands:
        for ch in range(2):
            band[ch, height : height + INFO, 0:LANES] = notes
            if band.shape[2] > LANES:
                band[ch, height : height + INFO, LANES:] = jnp.zeros((INFO, band.shape[2] - LANES), F32)
    for copy in copies:
        copy.wait()


def pack_call(place, tile, sides):
    tile_rows, tile_cols = tile.shape[1:]
    shape = lambda height, width: jax.ShapeDtypeStruct((2, height + INFO, width), F32)
    shapes = [shape(H, tile_cols)] * 2 + [shape(tile_rows, LANES)] * sides + [shape(H, LANES)] * (2 * sides)
    out = pl.pallas_call(
        functools.partial(pack_kernel, sides),
        out_shape=shapes,
        in_specs=[SMEM, HBM],
        out_specs=[VMEM] * len(shapes),
        scratch_shapes=[pltpu.SemaphoreType.DMA((len(shapes),))],
        compiler_params=pltpu.CompilerParams(vmem_limit_bytes=8 << 20),
        name="pack",
    )(place, tile)
    return out[0], out[1], *[list(out[2 + i * sides : 2 + (i + 1) * sides]) for i in range(3)]


def positions_kernel(sides, *refs):
    place, tile, near, far_side = refs[:4]
    side_in, near_corners, far_corners = [refs[4 + i * sides : 4 + (i + 1) * sides] for i in range(3)]
    probe_in, measured, left_in, right_in = refs[4 + 3 * sides : 8 + 3 * sides]
    middle, near_rim, far_rim, info = refs[8 + 3 * sides : 12 + 3 * sides]
    side_out, near_ends, far_ends = [refs[12 + i * sides : 12 + (i + 1) * sides] for i in range(3, 6)]
    kept, sent, probe_sums, ext, grad = refs[12 + 6 * sides : 17 + 6 * sides]
    scratch = refs[17 + 6 * sides :]
    left, right, levels, probe = scratch[:4]
    table_sems, level_sems, ext_sems = scratch[4:7]
    scratch = scratch[7:]
    patches, exits, stacks, wides, fields = [scratch[i * WAYS : (i + 1) * WAYS] for i in range(5)]

    pr = probe_in.shape[1]
    pieces = pr // LANES
    ext_rows = ext.shape[1]
    blocks = ext.shape[0] // 2
    own_blocks = blocks - 2
    tile_rows, tile_cols = ext_rows - 2 * H, own_blocks * LANES
    even = place[0] % 2 == 0
    near_row = pl.multiple_of(jnp.where(even, tile_rows + H, 0), 8)
    far_row = pl.multiple_of(jnp.where(even, 0, tile_rows + H), 8)
    side_blocks = [side_block(place, s, sides, blocks) for s in range(sides)]
    own, near_rows, far_rows = pl.ds(H, tile_rows), pl.ds(near_row, H), pl.ds(far_row, H)

    copies = []

    def fetch(source, target):
        copies.append(pltpu.make_async_copy(source, target, ext_sems.at[len(copies)]))
        copies[-1].start()

    for ch in range(2):
        for b in range(own_blocks):
            at, cut = ch * blocks + 1 + b, pl.ds(b * LANES, LANES)
            fetch(tile.at[ch, :, cut], ext.at[at, own, :])
            fetch(near.at[ch, pl.ds(0, H), cut], ext.at[at, near_rows, :])
            fetch(far_side.at[ch, pl.ds(0, H), cut], ext.at[at, far_rows, :])
        for s in range(sides):
            at = ch * blocks + side_blocks[s]
            fetch(side_in[s].at[ch, pl.ds(0, tile_rows), :], ext.at[at, own, :])
            fetch(near_corners[s].at[ch, pl.ds(0, H), :], ext.at[at, near_rows, :])
            fetch(far_corners[s].at[ch, pl.ds(0, H), :], ext.at[at, far_rows, :])
    for s in range(sides):
        fetch(side_in[s].at[0, pl.ds(tile_rows, INFO), :], info.at[s])
        fetch(near_corners[s].at[0, pl.ds(H, INFO), :], info.at[sides + 1 + s])
        fetch(far_corners[s].at[0, pl.ds(H, INFO), :], info.at[2 * sides + 2 + s])
    fetch(near.at[0, pl.ds(H, INFO), pl.ds(0, LANES)], info.at[sides])
    fetch(far_side.at[0, pl.ds(H, INFO), pl.ds(0, LANES)], info.at[2 * sides + 1])
    tables = [
        pltpu.make_async_copy(left_in, left, table_sems.at[0]),
        pltpu.make_async_copy(right_in, right, table_sems.at[1]),
        pltpu.make_async_copy(probe_in, probe, table_sems.at[2]),
    ]
    for copy in tables:
        copy.start()

    live_slots = place[COUNT]

    def level_copy(i):
        return pltpu.make_async_copy(measured.at[0, 0, i], levels.at[i], level_sems.at[i])

    def start_level(i, carry):
        level_copy(i).start()
        return carry

    lax.fori_loop(0, live_slots, start_level, 0)
    if sides == 1:
        for ch in range(2):
            ext[ch * blocks + blocks - 1 - side_blocks[0]] = jnp.zeros((ext_rows, LANES), F32)
    grad[...] = jnp.zeros_like(grad)
    probe_sums[...] = jnp.zeros_like(probe_sums)
    for copy in copies:
        copy.wait()
    tables[2].wait()
    lanes = lax.broadcasted_iota(jnp.int32, (CHUNK, LANES), 1)

    def put(stack, value, part, q, first):
        width = value.shape[1]
        high, low = split(value)
        rows_at = lambda block: slice(block * pr + q * CHUNK, block * pr + (q + 1) * CHUNK)
        here, there = slice(first, first + width), slice(pr + first, pr + first + width)
        if part == 0:
            stack[rows_at(0), here], stack[rows_at(1), there] = high, high
            stack[rows_at(2), here], stack[rows_at(3), there] = low, low
        else:
            stack[rows_at(0), there], stack[rows_at(1), here] = high, -high
            stack[rows_at(2), there], stack[rows_at(3), here] = low, -low

    def times_left(w):
        stack = jnp.concatenate([stacks[w][...], stacks[w][0 : 2 * pr]], axis=0)
        fields[w][...] = jnp.dot(left[...], stack, preferred_element_type=F32)

    def times_right(w):
        for q in range(pr // CHUNK):
            cut = slice(q * CHUNK, (q + 1) * CHUNK)
            high, low = split(fields[w][cut, :])
            wides[w][cut, 0 : 2 * pr] = high
            wides[w][cut, 2 * pr : 4 * pr] = low
        stack = jnp.concatenate([wides[w][...], wides[w][:, 0 : 2 * pr]], axis=1)
        fields[w][...] = jnp.dot(stack, right[...], preferred_element_type=F32)

    def load(w, k):
        row, col = place[ROWS + k], place[COLS + k]
        shift, block = col & (LANES - 1), col >> 7
        back = (LANES - shift) & (LANES - 1)
        keep = lanes < LANES - shift
        for q in range(pr // CHUNK):
            cut = slice(q * CHUNK, (q + 1) * CHUNK)
            here = pl.ds(row + q * CHUNK, CHUNK)
            seen = []
            for ch in range(2):
                turned = [
                    pltpu.roll(ext[ch * blocks + block + j, here, :], back, 1)
                    for j in range(pieces + 1)
                ]
                seen.append([jnp.where(keep, turned[j], turned[j + 1]) for j in range(pieces)])
            for j in range(pieces):
                part = slice(j * LANES, (j + 1) * LANES)
                probe_real, probe_imag = probe[0, cut, part], probe[1, cut, part]
                real, imag = seen[0][j], seen[1][j]
                patches[w][0, cut, part], patches[w][1, cut, part] = real, imag
                exit_real = probe_real * real - probe_imag * imag
                exit_imag = probe_real * imag + probe_imag * real
                exits[w][0, cut, part], exits[w][1, cut, part] = exit_real, exit_imag
                put(stacks[w], exit_real, 0, q, j * LANES)
                put(stacks[w], exit_imag, 1, q, j * LANES)

    def project(w, k):
        for q in range(pr // CHUNK):
            cut = slice(q * CHUNK, (q + 1) * CHUNK)
            real, imag = fields[w][cut, 0:pr], fields[w][cut, pr : 2 * pr]
            factor = jnp.sqrt(levels[k, cut, :]) * lax.rsqrt(real * real + imag * imag + 1.0)
            put(stacks[w], real * factor, 0, q, 0)
            put(stacks[w], -(imag * factor), 1, q, 0)

    def finish(w, k, live):
        row, col = place[ROWS + k], place[COLS + k]
        shift, block = col & (LANES - 1), col >> 7
        low = lanes < shift
        zero = jnp.zeros((CHUNK, LANES), F32)
        for q in range(pr // CHUNK):
            cut = slice(q * CHUNK, (q + 1) * CHUNK)
            here = pl.ds(row + q * CHUNK, CHUNK)
            turned = [[], []]
            for j in range(pieces):
                part = slice(j * LANES, (j + 1) * LANES)
                other = slice(pr + j * LANES, pr + (j + 1) * LANES)
                diff_real = fields[w][cut, part] - exits[w][0, cut, part]
                diff_imag = -fields[w][cut, other] - exits[w][1, cut, part]
                real, imag = patches[w][0, cut, part], patches[w][1, cut, part]
                weight = real * real + imag * imag
                if live is not None:
                    diff_real, diff_imag = diff_real * live, diff_imag * live
                    weight = weight * live
                probe_real, probe_imag = probe[0, cut, part], probe[1, cut, part]
                turned[0].append(pltpu.roll(probe_real * diff_real + probe_imag * diff_imag, shift, 1))
                turned[1].append(pltpu.roll(probe_real * diff_imag - probe_imag * diff_real, shift, 1))
                probe_sums[j, 0, cut, :] += real * diff_real + imag * diff_imag
                probe_sums[j, 1, cut, :] += real * diff_imag - imag * diff_real
                probe_sums[j, 2, cut, :] += weight
            for ch in range(2):
                at = ch * blocks + block
                grad[at, here, :] += jnp.where(low, zero, turned[ch][0])
                for j in range(1, pieces):
                    grad[at + j, here, :] += jnp.where(low, turned[ch][j - 1], turned[ch][j])
                grad[at + pieces, here, :] += jnp.where(low, turned[ch][-1], zero)

    def visit(i, carry):
        first = i * WAYS
        slots = [jnp.minimum(first + w, live_slots - 1) for w in range(WAYS)]
        lives = [None] + [jnp.where(first + w < live_slots, 1.0, 0.0) for w in range(1, WAYS)]
        for w in range(WAYS):

            @pl.when(first + w < live_slots)
            def _():
                level_copy(slots[w]).wait()

        @pl.when(i == 0)
        def _():
            tables[0].wait()
            tables[1].wait()

        for w in range(WAYS):
            load(w, slots[w])
            times_left(w)
        for w in range(WAYS):
            times_right(w)
        for w in range(WAYS):
            project(w, slots[w])
            times_left(w)
        for w in range(WAYS):
            times_right(w)
        for w in range(WAYS):
            finish(w, slots[w], lives[w])
        return carry

    lax.fori_loop(0, (live_slots + WAYS - 1) // WAYS, visit, 0)
    core = place[0] % 2
    span = pieces // 2
    for j in range(span):
        for ch in range(3):
            at = pl.ds((j * 3 + ch) * pr, pr)
            kept[at, :] = probe_sums[core * span + j, ch]
            sent[at, :] = probe_sums[(1 - core) * span + j, ch]
    for ch in range(2):
        for b in range(own_blocks):
            at, cut = ch * blocks + 1 + b, slice(b * LANES, (b + 1) * LANES)
            middle[ch, :, cut] = grad[at, own, :]
            near_rim[ch, :, cut] = grad[at, near_rows, :]
            far_rim[ch, :, cut] = grad[at, far_rows, :]
        for s in range(sides):
            at = ch * blocks + side_blocks[s]
            side_out[s][ch] = grad[at, own, :]
            near_ends[s][ch] = grad[at, near_rows, :]
            far_ends[s][ch] = grad[at, far_rows, :]


def positions_call(place, tile, near, far_side, side_in, near_corners, far_corners, probe, measured):
    pr = probe.shape[1]
    sides = len(side_in)
    tile_rows, tile_cols = tile.shape[1:]
    ext_rows = tile_rows + 2 * H
    blocks = (tile_cols + 2 * H) // LANES
    left, right = (jnp.asarray(table) for table in dft_tables(pr))
    shape = lambda *dims: jax.ShapeDtypeStruct(dims, F32)
    slots = measured.shape[2]
    rim = shape(2, H, tile_cols)
    middle, near_rim, far_rim, info, *rest = pl.pallas_call(
        functools.partial(positions_kernel, sides),
        out_shape=(
            shape(2, tile_rows, tile_cols),
            rim,
            rim,
            shape(3 * sides + 2, INFO, LANES),
            *[shape(2, tile_rows, LANES)] * sides,
            *[shape(2, H, LANES)] * (2 * sides),
            shape(3 * pr * pr // LANES // 2, LANES),
            shape(3 * pr * pr // LANES // 2, LANES),
        ),
        in_specs=[SMEM, HBM] + [ANY] * (2 + 3 * sides) + [HBM] * 4,
        out_specs=(VMEM,) * (6 + 3 * sides),
        scratch_shapes=[
            pltpu.VMEM((pr // LANES, 3, pr, LANES), F32),
            *[pltpu.VMEM((2 * blocks, ext_rows, LANES), F32)] * 2,
            pltpu.VMEM(left.shape, BF),
            pltpu.VMEM(right.shape, BF),
            pltpu.VMEM((slots, pr, pr), F32),
            pltpu.VMEM(probe.shape, F32),
            pltpu.SemaphoreType.DMA((3,)),
            pltpu.SemaphoreType.DMA((slots,)),
            pltpu.SemaphoreType.DMA((6 * blocks + 3 * sides + 2,)),
            *[pltpu.VMEM((2, pr, pr), F32)] * (2 * WAYS),
            *[pltpu.VMEM((4 * pr, 2 * pr), BF)] * WAYS,
            *[pltpu.VMEM((pr, 4 * pr), BF)] * WAYS,
            *[pltpu.VMEM((pr, 2 * pr), F32)] * WAYS,
        ],
        compiler_params=pltpu.CompilerParams(vmem_limit_bytes=GRANT),
        cost_estimate=pl.CostEstimate(
            flops=slots * 96 * pr * pr * pr, bytes_accessed=16_000_000, transcendentals=slots * 2 * pr * pr
        ),
        name="positions",
    )(place, tile, near, far_side, *side_in, *near_corners, *far_corners, probe, measured, left, right)
    ends = [rest[i * sides : (i + 1) * sides] for i in range(3)]
    return middle, near_rim, far_rim, *ends, *rest[3 * sides :], info


def update_kernel(sides, *refs):
    place, tile, middle, cover, near, far_side = refs[:6]
    side_in, near_ends, far_ends = [refs[6 + i * sides : 6 + (i + 1) * sides] for i in range(3)]
    own_got, other_got, probe, out, new_probe, sums = refs[6 + 3 * sides :]
    tile_rows, tile_cols = tile.shape[1:]
    own_blocks = tile_cols // LANES
    even = place[0] % 2 == 0
    sums[...] = middle[...]
    near_row = pl.multiple_of(jnp.where(even, tile_rows - H, 0), 8)
    far_row = pl.multiple_of(jnp.where(even, 0, tile_rows - H), 8)
    sums[:, pl.ds(near_row, H), :] += near[...]
    sums[:, pl.ds(far_row, H), :] += far_side[...]
    for s in range(sides):
        if sides == 1:
            edge = jnp.where(place[1] == 0, tile_cols - LANES, 0)
        else:
            edge = 0 if s == 0 else tile_cols - LANES
        at = pl.ds(pl.multiple_of(edge, LANES), LANES)
        sums[:, :, at] += side_in[s][...]
        sums[:, pl.ds(near_row, H), at] += near_ends[s][...]
        sums[:, pl.ds(far_row, H), at] += far_ends[s][...]
    rows = own_got.shape[1] - 8
    peak = jnp.maximum(jnp.max(own_got[:, rows:, :], axis=0), jnp.max(other_got[:, rows:, :], axis=0))
    top = MIX_OBJECT * jnp.max(peak, keepdims=True)
    inverse = 1.0 / ((1.0 - MIX_OBJECT) * cover[...] + top)
    for ch in range(2):
        out[ch] = tile[ch] + sums[ch] * inverse

    pr = probe.shape[1]
    pieces = pr // LANES
    both = [ref[:, 0:rows, :].reshape(-1, LANES) for ref in (own_got, other_got)]

    def update(parts):
        flat = [parts[j * len(parts) // pieces] for j in range(pieces)]
        span = flat[0].shape[0] // (pieces // len(parts))
        term = lambda j, ch: flat[j][(j % (pieces // len(parts))) * span + ch * pr :][:pr]
        weights = [term(j, 2) for j in range(pieces)]
        best = functools.reduce(jnp.maximum, weights)
        best = jnp.max(jnp.max(best.reshape(-1, 8, LANES), axis=0), keepdims=True)
        for j in range(pieces):
            cut = slice(j * LANES, (j + 1) * LANES)
            scale = 1.0 / ((1.0 - MIX_PROBE) * weights[j] + MIX_PROBE * best)
            for ch in range(2):
                new_probe[ch, :, cut] = probe[ch, :, cut] + term(j, ch) * scale

    for first in (0, 1):

        @pl.when(place[0] % 2 == first)
        def _():
            update([both[first], both[1 - first]])


def update_call(place, tile, middle, cover, near, far_side, side_in, ends, own, other, probe):
    sides = len(side_in)
    return pl.pallas_call(
        functools.partial(update_kernel, sides),
        out_shape=(jax.ShapeDtypeStruct(tile.shape, F32), jax.ShapeDtypeStruct(probe.shape, F32)),
        in_specs=[SMEM] + [VMEM] * (8 + 3 * sides),
        out_specs=(VMEM, VMEM),
        scratch_shapes=[pltpu.VMEM(tile.shape, F32)],
        compiler_params=pltpu.CompilerParams(vmem_limit_bytes=16 << 20),
        name="update",
    )(place, tile, middle, cover, near, far_side, *side_in, *ends, own, other, probe)


WIDE = ("rest", "core")
CHIPS = ("rest", "narrow")


def swap(x, axis, first):
    size = lax.axis_size(axis)
    pairs = []
    for i in range(first, size - 1, 2):
        pairs += [(i, i + 1), (i + 1, i)]
    return lax.ppermute(x, axis, pairs)


def shifted(x, axis, by):
    size = lax.axis_size(axis)
    return lax.ppermute(x, axis, [(i, i + by) for i in range(size) if 0 <= i + by < size])


def to_sides(pieces):
    if len(pieces) == 1:
        return [swap(pieces[0], "narrow", 0)]
    return [shifted(pieces[1], "narrow", 1), shifted(pieces[0], "narrow", -1)]


def to_corners(bands, first):
    wide, narrow = lax.axis_size(WIDE), lax.axis_size("narrow")
    steps = [0] if len(bands) == 1 else [-1, 1]
    got = []
    for s, step in enumerate(steps):
        pairs = []
        for i in range(first, wide - 1, 2):
            for n in range(narrow):
                m = 1 - n if step == 0 else n - step
                if 0 <= m < narrow:
                    pairs += [(i * narrow + n, (i + 1) * narrow + m), ((i + 1) * narrow + n, i * narrow + m)]
        band = bands[0] if step == 0 else bands[1 - s]
        got.append(lax.ppermute(band, (*WIDE, "narrow"), pairs))
    return got


def chip_exchange(chunks):
    return lax.all_to_all(chunks.reshape(-1, LANES), CHIPS, 0, 0, tiled=True).reshape(chunks.shape)


def after(x, *others):
    return lax.optimization_barrier((x, *others))[0]


def body(tile, probe, measured, rows, cols, counts):
    wide, narrow = lax.axis_index(WIDE), lax.axis_index("narrow")
    sides = 1 if lax.axis_size("narrow") == 2 else 2
    tile_rows, tile_cols = tile.shape[1:]
    even = wide % 2 == 0
    place = jnp.concatenate(
        [jnp.stack([wide, narrow, counts[0, 0]]).astype(jnp.int32), rows.reshape(-1), cols.reshape(-1)]
    )

    far_band, near_band, edges, far_ends, near_ends = pack_call(place, tile, sides)
    far_side = swap(far_band, WIDE, 1)
    far_corners = to_corners(far_ends, 1)
    side_in = to_sides(edges)
    near_corners = to_corners(near_ends, 0)
    near = swap(near_band, "core", 0)

    middle, near_rim, far_rim, side_rims, near_rim_ends, far_rim_ends, kept, sent, got_info = positions_call(
        place, tile, near, far_side, side_in, near_corners, far_corners, probe, measured
    )
    own_info = edges[0][:1, tile_rows:]

    terms = kept + swap(sent, "core", 0)
    near_got = swap(near_rim, "core", 0)
    far_got = swap(far_rim, WIDE, 1)
    side_got = to_sides(side_rims)
    info = jnp.concatenate([own_info, got_info], axis=0)[:, 0, :32].astype(jnp.int32)
    cover, peak = cover_call(place, after(info, terms), probe, tile_rows, tile_cols, sides)
    chips = lax.axis_size(CHIPS)
    got = chip_exchange(terms.reshape(chips, -1, LANES))
    chunk = jnp.sum(got, axis=0)
    rows_each = chunk.shape[0]
    chunk = after(jnp.concatenate([chunk, peak], axis=0), far_got, near_got, *side_got)
    got = chip_exchange(jnp.broadcast_to(chunk, (chips, *chunk.shape)))
    if rows_each % 8:
        peak = jnp.max(got[:, rows_each:], axis=0)
        got = jnp.concatenate([got[:, :rows_each].reshape(-1, LANES), peak], axis=0)[None]

    near_ends_got = to_corners(near_rim_ends, 0)
    far_ends_got = to_corners(far_rim_ends, 1)
    ends_got = near_ends_got + far_ends_got
    other = swap(after(got, *ends_got), "core", 0)
    return update_call(place, tile, middle, cover, near_got, far_got, side_got, ends_got, got, other, probe)


def solution(mesh):
    wide, narrow = mesh.devices.shape
    fine = Mesh(mesh.devices.reshape(wide // 2, 2, narrow), ("rest", "core", "narrow"))
    placed = (
        P(None, WIDE, "narrow"),
        P(),
        P(WIDE, "narrow", None, None, None),
        P(WIDE, "narrow", None),
        P(WIDE, "narrow", None),
        P(WIDE, "narrow"),
    )
    return jax.shard_map(
        body,
        mesh=fine,
        in_specs=placed,
        out_specs=(P(None, WIDE, "narrow"), P()),
        check_vma=False,
    )
```

```python
import functools
import math

import jax
import jax.numpy as jnp
import ml_dtypes
import numpy as np
from jax import lax
from jax.experimental import pallas as pl
from jax.experimental.pallas import tpu as pltpu
from jax.sharding import Mesh, PartitionSpec as P

H = 128
LANES = 128
CHUNK = 32
WAYS = 2
INFO = 8
GRANT = 50176 << 10
BF = jnp.bfloat16
F32 = jnp.float32
MIX_OBJECT = 0.5
MIX_PROBE = 0.5
VMEM = pl.BlockSpec(memory_space=pltpu.VMEM)
SMEM = pl.BlockSpec(memory_space=pltpu.SMEM)
ANY = pl.BlockSpec(memory_space=pl.ANY)
HBM = pl.BlockSpec(memory_space=pltpu.HBM)
COUNT, ROWS, COLS = 2, 3, 11


def rounded_pair(table):
    table = table.astype(np.float32)
    high = table.astype(ml_dtypes.bfloat16)
    low = (table - high.astype(np.float32)).astype(ml_dtypes.bfloat16)
    return high, low


def dft_tables(length):
    index = np.arange(length)
    angle = 2.0 * np.pi * ((index[:, None] * index[None, :]) % length) / length
    cos_high, cos_low = rounded_pair(np.cos(angle) / math.sqrt(length))
    sin_high, sin_low = rounded_pair(-np.sin(angle) / math.sqrt(length))
    left = np.concatenate([cos_high, sin_high, cos_high, sin_high, cos_low, sin_low], axis=1)
    right_high = np.block([[cos_high, sin_high], [-sin_high, cos_high]])
    right_low = np.block([[cos_low, sin_low], [-sin_low, cos_low]])
    right = np.concatenate([right_high, right_high, right_low], axis=0)
    return left, right


def split(x):
    high = x.astype(BF)
    return high, (x - high.astype(F32)).astype(BF)


def side_block(place, side, sides, blocks):
    if sides == 1:
        return jnp.where(place[1] == 0, blocks - 1, 0)
    return 0 if side == 0 else blocks - 1


def side_step(place, side, sides):
    if sides == 1:
        return jnp.where(place[1] == 0, 1, -1)
    return -1 if side == 0 else 1


def cover_kernel(tile_rows, tile_cols, sides, place, info, probe, cover, peak, total, power):
    pr = probe.shape[1]
    pieces = pr // LANES
    for j in range(pieces):
        cut = slice(j * LANES, (j + 1) * LANES)
        power[j] = probe[0, :, cut] * probe[0, :, cut] + probe[1, :, cut] * probe[1, :, cut]
    total[...] = jnp.zeros_like(total)
    lanes = lax.broadcasted_iota(jnp.int32, (CHUNK, LANES), 1)
    even = place[0] % 2 == 0
    steps_down = (0, jnp.where(even, 1, -1), jnp.where(even, -1, 1))
    steps_right = (0,) + tuple(side_step(place, s, sides) for s in range(sides))
    for v in range(3):
        for h in range(1 + sides):
            source = v * (1 + sides) + h
            down, right = steps_down[v], steps_right[h]

            def visit(k, carry):
                row = info[source, k] + pr - H + down * tile_rows
                col = info[source, 8 + k] + pr - H + right * tile_cols
                inside = (row > 0) & (row < pr + tile_rows) & (col > 0) & (col < pr + tile_cols)

                @pl.when(inside)
                def _():
                    shift = col & (LANES - 1)
                    block = col >> 7
                    low = lanes < shift
                    for q in range(pr // CHUNK):
                        turned = [
                            pltpu.roll(power[j, q * CHUNK : (q + 1) * CHUNK, :], shift, 1)
                            for j in range(pieces)
                        ]
                        here = pl.ds(row + q * CHUNK, CHUNK)
                        zero = jnp.zeros((CHUNK, LANES), F32)
                        total[block, here, :] += jnp.where(low, zero, turned[0])
                        for j in range(1, pieces):
                            total[block + j, here, :] += jnp.where(low, turned[j - 1], turned[j])
                        total[block + pieces, here, :] += jnp.where(low, turned[-1], zero)

                return carry

            lax.fori_loop(0, info[source, 16], visit, 0)
    first = pr // LANES
    best = jnp.zeros((8, LANES), F32)
    for b in range(tile_cols // LANES):
        own = total[first + b, pr : pr + tile_rows, :]
        cover[:, b * LANES : (b + 1) * LANES] = own
        best = jnp.maximum(best, jnp.max(own.reshape(tile_rows // 8, 8, LANES), axis=0))
    peak[...] = jnp.full((8, LANES), jnp.max(best), F32)


def cover_call(place, info, probe, tile_rows, tile_cols, sides):
    pr = probe.shape[1]
    blocks = (tile_cols + 2 * pr) // LANES + 1
    return pl.pallas_call(
        functools.partial(cover_kernel, tile_rows, tile_cols, sides),
        out_shape=(
            jax.ShapeDtypeStruct((tile_rows, tile_cols), F32),
            jax.ShapeDtypeStruct((8, LANES), F32),
        ),
        in_specs=[SMEM, SMEM, VMEM],
        out_specs=(VMEM, VMEM),
        scratch_shapes=[
            pltpu.VMEM((blocks, tile_rows + 2 * pr, LANES), F32),
            pltpu.VMEM((pr // LANES, pr, LANES), F32),
        ],
        compiler_params=pltpu.CompilerParams(vmem_limit_bytes=16 << 20),
        cost_estimate=pl.CostEstimate(flops=4_000_000, bytes_accessed=8_000_000, transcendentals=0),
        name="cover",
    )(place, info, probe)


def pack_kernel(sides, place, tile, *refs):
    far_band, near_band = refs[:2]
    edges, far_ends, near_ends = [refs[2 + i * sides : 2 + (i + 1) * sides] for i in range(3)]
    sems = refs[2 + 3 * sides]
    tile_rows, tile_cols = tile.shape[1:]
    even = place[0] % 2 == 0
    near_start = pl.multiple_of(jnp.where(even, tile_rows - H, 0), 8)
    far_start = pl.multiple_of(jnp.where(even, 0, tile_rows - H), 8)
    if sides == 1:
        starts = [pl.multiple_of(jnp.where(place[1] == 0, tile_cols - H, 0), LANES)]
    else:
        starts = [0, tile_cols - H]
    bands = [(far_band, far_start, H, 0), (near_band, near_start, H, 0)]
    for s, start in enumerate(starts):
        bands += [(edges[s], 0, tile_rows, start), (far_ends[s], far_start, H, start)]
        bands += [(near_ends[s], near_start, H, start)]
    copies = []
    for i, (band, row, height, col) in enumerate(bands):
        copies.append(
            pltpu.make_async_copy(
                tile.at[:, pl.ds(row, height), pl.ds(col, band.shape[2])], band.at[:, pl.ds(0, height), :], sems.at[i]
            )
        )
        copies[-1].start()
    lanes = lax.broadcasted_iota(jnp.int32, (INFO, LANES), 1)
    notes = jnp.where(lanes == 16, place[COUNT], 0)
    for k in range(8):
        notes = jnp.where(lanes == k, place[ROWS + k], jnp.where(lanes == 8 + k, place[COLS + k], notes))
    notes = notes.astype(F32)
    for band, row, height, col in bands:
        for ch in range(2):
            band[ch, height : height + INFO, 0:LANES] = notes
            if band.shape[2] > LANES:
                band[ch, height : height + INFO, LANES:] = jnp.zeros((INFO, band.shape[2] - LANES), F32)
    for copy in copies:
        copy.wait()


def pack_call(place, tile, sides):
    tile_rows, tile_cols = tile.shape[1:]
    shape = lambda height, width: jax.ShapeDtypeStruct((2, height + INFO, width), F32)
    shapes = [shape(H, tile_cols)] * 2 + [shape(tile_rows, LANES)] * sides + [shape(H, LANES)] * (2 * sides)
    out = pl.pallas_call(
        functools.partial(pack_kernel, sides),
        out_shape=shapes,
        in_specs=[SMEM, HBM],
        out_specs=[VMEM] * len(shapes),
        scratch_shapes=[pltpu.SemaphoreType.DMA((len(shapes),))],
        compiler_params=pltpu.CompilerParams(vmem_limit_bytes=8 << 20),
        name="pack",
    )(place, tile)
    return out[0], out[1], *[list(out[2 + i * sides : 2 + (i + 1) * sides]) for i in range(3)]


def positions_kernel(sides, *refs):
    place, tile, near, far_side = refs[:4]
    side_in, near_corners, far_corners = [refs[4 + i * sides : 4 + (i + 1) * sides] for i in range(3)]
    probe_in, measured, left_in, right_in = refs[4 + 3 * sides : 8 + 3 * sides]
    middle, near_rim, far_rim, info = refs[8 + 3 * sides : 12 + 3 * sides]
    side_out, near_ends, far_ends = [refs[12 + i * sides : 12 + (i + 1) * sides] for i in range(3, 6)]
    kept, sent, probe_sums, ext, grad = refs[12 + 6 * sides : 17 + 6 * sides]
    scratch = refs[17 + 6 * sides :]
    left, right, levels, probe = scratch[:4]
    table_sems, level_sems, ext_sems = scratch[4:7]
    scratch = scratch[7:]
    patches, exits, stacks, wides, fields = [scratch[i * WAYS : (i + 1) * WAYS] for i in range(5)]

    pr = probe_in.shape[1]
    pieces = pr // LANES
    ext_rows = ext.shape[1]
    blocks = ext.shape[0] // 2
    own_blocks = blocks - 2
    tile_rows, tile_cols = ext_rows - 2 * H, own_blocks * LANES
    even = place[0] % 2 == 0
    near_row = pl.multiple_of(jnp.where(even, tile_rows + H, 0), 8)
    far_row = pl.multiple_of(jnp.where(even, 0, tile_rows + H), 8)
    side_blocks = [side_block(place, s, sides, blocks) for s in range(sides)]
    own, near_rows, far_rows = pl.ds(H, tile_rows), pl.ds(near_row, H), pl.ds(far_row, H)

    copies = []

    def fetch(source, target):
        copies.append(pltpu.make_async_copy(source, target, ext_sems.at[len(copies)]))
        copies[-1].start()

    for ch in range(2):
        for b in range(own_blocks):
            at, cut = ch * blocks + 1 + b, pl.ds(b * LANES, LANES)
            fetch(tile.at[ch, :, cut], ext.at[at, own, :])
            fetch(near.at[ch, pl.ds(0, H), cut], ext.at[at, near_rows, :])
            fetch(far_side.at[ch, pl.ds(0, H), cut], ext.at[at, far_rows, :])
        for s in range(sides):
            at = ch * blocks + side_blocks[s]
            fetch(side_in[s].at[ch, pl.ds(0, tile_rows), :], ext.at[at, own, :])
            fetch(near_corners[s].at[ch, pl.ds(0, H), :], ext.at[at, near_rows, :])
            fetch(far_corners[s].at[ch, pl.ds(0, H), :], ext.at[at, far_rows, :])
    for s in range(sides):
        fetch(side_in[s].at[0, pl.ds(tile_rows, INFO), :], info.at[s])
        fetch(near_corners[s].at[0, pl.ds(H, INFO), :], info.at[sides + 1 + s])
        fetch(far_corners[s].at[0, pl.ds(H, INFO), :], info.at[2 * sides + 2 + s])
    fetch(near.at[0, pl.ds(H, INFO), pl.ds(0, LANES)], info.at[sides])
    fetch(far_side.at[0, pl.ds(H, INFO), pl.ds(0, LANES)], info.at[2 * sides + 1])
    tables = [
        pltpu.make_async_copy(left_in, left, table_sems.at[0]),
        pltpu.make_async_copy(right_in, right, table_sems.at[1]),
        pltpu.make_async_copy(probe_in, probe, table_sems.at[2]),
    ]
    for copy in tables:
        copy.start()

    live_slots = place[COUNT]

    def level_copy(i):
        return pltpu.make_async_copy(measured.at[0, 0, i], levels.at[i], level_sems.at[i])

    def start_levels(first):
        for w in range(WAYS):

            @pl.when(first + w < live_slots)
            def _():
                level_copy(first + w).start()

    start_levels(0)
    if sides == 1:
        for ch in range(2):
            ext[ch * blocks + blocks - 1 - side_blocks[0]] = jnp.zeros((ext_rows, LANES), F32)
    grad[...] = jnp.zeros_like(grad)
    probe_sums[...] = jnp.zeros_like(probe_sums)
    for copy in copies:
        copy.wait()
    tables[2].wait()
    lanes = lax.broadcasted_iota(jnp.int32, (CHUNK, LANES), 1)

    def put(stack, value, part, q, first):
        width = value.shape[1]
        high, low = split(value)
        rows_at = lambda block: slice(block * pr + q * CHUNK, block * pr + (q + 1) * CHUNK)
        here, there = slice(first, first + width), slice(pr + first, pr + first + width)
        if part == 0:
            stack[rows_at(0), here], stack[rows_at(1), there] = high, high
            stack[rows_at(2), here], stack[rows_at(3), there] = low, low
        else:
            stack[rows_at(0), there], stack[rows_at(1), here] = high, -high
            stack[rows_at(2), there], stack[rows_at(3), here] = low, -low

    def times_left(w):
        stack = jnp.concatenate([stacks[w][...], stacks[w][0 : 2 * pr]], axis=0)
        fields[w][...] = jnp.dot(left[...], stack, preferred_element_type=F32)

    def times_right(w):
        for q in range(pr // CHUNK):
            cut = slice(q * CHUNK, (q + 1) * CHUNK)
            high, low = split(fields[w][cut, :])
            wides[w][cut, 0 : 2 * pr] = high
            wides[w][cut, 2 * pr : 4 * pr] = low
        stack = jnp.concatenate([wides[w][...], wides[w][:, 0 : 2 * pr]], axis=1)
        fields[w][...] = jnp.dot(stack, right[...], preferred_element_type=F32)

    def load(w, k):
        row, col = place[ROWS + k], place[COLS + k]
        shift, block = col & (LANES - 1), col >> 7
        back = (LANES - shift) & (LANES - 1)
        keep = lanes < LANES - shift
        for q in range(pr // CHUNK):
            cut = slice(q * CHUNK, (q + 1) * CHUNK)
            here = pl.ds(row + q * CHUNK, CHUNK)
            seen = []
            for ch in range(2):
                turned = [
                    pltpu.roll(ext[ch * blocks + block + j, here, :], back, 1)
                    for j in range(pieces + 1)
                ]
                seen.append([jnp.where(keep, turned[j], turned[j + 1]) for j in range(pieces)])
            for j in range(pieces):
                part = slice(j * LANES, (j + 1) * LANES)
                probe_real, probe_imag = probe[0, cut, part], probe[1, cut, part]
                real, imag = seen[0][j], seen[1][j]
                patches[w][0, cut, part], patches[w][1, cut, part] = real, imag
                exit_real = probe_real * real - probe_imag * imag
                exit_imag = probe_real * imag + probe_imag * real
                exits[w][0, cut, part], exits[w][1, cut, part] = exit_real, exit_imag
                put(stacks[w], exit_real, 0, q, j * LANES)
                put(stacks[w], exit_imag, 1, q, j * LANES)

    def project(w, k):
        for q in range(pr // CHUNK):
            cut = slice(q * CHUNK, (q + 1) * CHUNK)
            real, imag = fields[w][cut, 0:pr], fields[w][cut, pr : 2 * pr]
            factor = jnp.sqrt(levels[k, cut, :]) * lax.rsqrt(real * real + imag * imag + 1.0)
            put(stacks[w], real * factor, 0, q, 0)
            put(stacks[w], -(imag * factor), 1, q, 0)

    def finish(w, k, live):
        row, col = place[ROWS + k], place[COLS + k]
        shift, block = col & (LANES - 1), col >> 7
        low = lanes < shift
        zero = jnp.zeros((CHUNK, LANES), F32)
        for q in range(pr // CHUNK):
            cut = slice(q * CHUNK, (q + 1) * CHUNK)
            here = pl.ds(row + q * CHUNK, CHUNK)
            turned = [[], []]
            for j in range(pieces):
                part = slice(j * LANES, (j + 1) * LANES)
                other = slice(pr + j * LANES, pr + (j + 1) * LANES)
                diff_real = fields[w][cut, part] - exits[w][0, cut, part]
                diff_imag = -fields[w][cut, other] - exits[w][1, cut, part]
                real, imag = patches[w][0, cut, part], patches[w][1, cut, part]
                weight = real * real + imag * imag
                if live is not None:
                    diff_real, diff_imag = diff_real * live, diff_imag * live
                    weight = weight * live
                probe_real, probe_imag = probe[0, cut, part], probe[1, cut, part]
                turned[0].append(pltpu.roll(probe_real * diff_real + probe_imag * diff_imag, shift, 1))
                turned[1].append(pltpu.roll(probe_real * diff_imag - probe_imag * diff_real, shift, 1))
                probe_sums[j, 0, cut, :] += real * diff_real + imag * diff_imag
                probe_sums[j, 1, cut, :] += real * diff_imag - imag * diff_real
                probe_sums[j, 2, cut, :] += weight
            for ch in range(2):
                at = ch * blocks + block
                grad[at, here, :] += jnp.where(low, zero, turned[ch][0])
                for j in range(1, pieces):
                    grad[at + j, here, :] += jnp.where(low, turned[ch][j - 1], turned[ch][j])
                grad[at + pieces, here, :] += jnp.where(low, turned[ch][-1], zero)

    def visit(i, carry):
        first = i * WAYS
        slots = [jnp.minimum(first + w, live_slots - 1) for w in range(WAYS)]
        lives = [None] + [jnp.where(first + w < live_slots, 1.0, 0.0) for w in range(1, WAYS)]
        for w in range(WAYS):

            @pl.when(first + w < live_slots)
            def _():
                level_copy(slots[w]).wait()

        start_levels(first + WAYS)

        @pl.when(i == 0)
        def _():
            tables[0].wait()
            tables[1].wait()

        for w in range(WAYS):
            load(w, slots[w])
            times_left(w)
        for w in range(WAYS):
            times_right(w)
        for w in range(WAYS):
            project(w, slots[w])
            times_left(w)
        for w in range(WAYS):
            times_right(w)
        for w in range(WAYS):
            finish(w, slots[w], lives[w])
        return carry

    lax.fori_loop(0, (live_slots + WAYS - 1) // WAYS, visit, 0)
    core = place[0] % 2
    span = pieces // 2
    for j in range(span):
        for ch in range(3):
            at = pl.ds((j * 3 + ch) * pr, pr)
            kept[at, :] = probe_sums[core * span + j, ch]
            sent[at, :] = probe_sums[(1 - core) * span + j, ch]
    for ch in range(2):
        for b in range(own_blocks):
            at, cut = ch * blocks + 1 + b, slice(b * LANES, (b + 1) * LANES)
            middle[ch, :, cut] = grad[at, own, :]
            near_rim[ch, :, cut] = grad[at, near_rows, :]
            far_rim[ch, :, cut] = grad[at, far_rows, :]
        for s in range(sides):
            at = ch * blocks + side_blocks[s]
            side_out[s][ch] = grad[at, own, :]
            near_ends[s][ch] = grad[at, near_rows, :]
            far_ends[s][ch] = grad[at, far_rows, :]


def positions_call(place, tile, near, far_side, side_in, near_corners, far_corners, probe, measured):
    pr = probe.shape[1]
    sides = len(side_in)
    tile_rows, tile_cols = tile.shape[1:]
    ext_rows = tile_rows + 2 * H
    blocks = (tile_cols + 2 * H) // LANES
    left, right = (jnp.asarray(table) for table in dft_tables(pr))
    shape = lambda *dims: jax.ShapeDtypeStruct(dims, F32)
    slots = measured.shape[2]
    rim = shape(2, H, tile_cols)
    middle, near_rim, far_rim, info, *rest = pl.pallas_call(
        functools.partial(positions_kernel, sides),
        out_shape=(
            shape(2, tile_rows, tile_cols),
            rim,
            rim,
            shape(3 * sides + 2, INFO, LANES),
            *[shape(2, tile_rows, LANES)] * sides,
            *[shape(2, H, LANES)] * (2 * sides),
            shape(3 * pr * pr // LANES // 2, LANES),
            shape(3 * pr * pr // LANES // 2, LANES),
        ),
        in_specs=[SMEM, HBM] + [ANY] * (2 + 3 * sides) + [HBM] * 4,
        out_specs=(VMEM,) * (6 + 3 * sides),
        scratch_shapes=[
            pltpu.VMEM((pr // LANES, 3, pr, LANES), F32),
            *[pltpu.VMEM((2 * blocks, ext_rows, LANES), F32)] * 2,
            pltpu.VMEM(left.shape, BF),
            pltpu.VMEM(right.shape, BF),
            pltpu.VMEM((slots, pr, pr), F32),
            pltpu.VMEM(probe.shape, F32),
            pltpu.SemaphoreType.DMA((3,)),
            pltpu.SemaphoreType.DMA((slots,)),
            pltpu.SemaphoreType.DMA((6 * blocks + 3 * sides + 2,)),
            *[pltpu.VMEM((2, pr, pr), F32)] * (2 * WAYS),
            *[pltpu.VMEM((4 * pr, 2 * pr), BF)] * WAYS,
            *[pltpu.VMEM((pr, 4 * pr), BF)] * WAYS,
            *[pltpu.VMEM((pr, 2 * pr), F32)] * WAYS,
        ],
        compiler_params=pltpu.CompilerParams(vmem_limit_bytes=GRANT),
        cost_estimate=pl.CostEstimate(
            flops=slots * 96 * pr * pr * pr, bytes_accessed=16_000_000, transcendentals=slots * 2 * pr * pr
        ),
        name="positions",
    )(place, tile, near, far_side, *side_in, *near_corners, *far_corners, probe, measured, left, right)
    ends = [rest[i * sides : (i + 1) * sides] for i in range(3)]
    return middle, near_rim, far_rim, *ends, *rest[3 * sides :], info


def update_kernel(sides, *refs):
    place, tile, middle, cover, near, far_side = refs[:6]
    side_in, near_ends, far_ends = [refs[6 + i * sides : 6 + (i + 1) * sides] for i in range(3)]
    own_got, other_got, probe, out, new_probe, sums = refs[6 + 3 * sides :]
    tile_rows, tile_cols = tile.shape[1:]
    own_blocks = tile_cols // LANES
    even = place[0] % 2 == 0
    sums[...] = middle[...]
    near_row = pl.multiple_of(jnp.where(even, tile_rows - H, 0), 8)
    far_row = pl.multiple_of(jnp.where(even, 0, tile_rows - H), 8)
    sums[:, pl.ds(near_row, H), :] += near[...]
    sums[:, pl.ds(far_row, H), :] += far_side[...]
    for s in range(sides):
        if sides == 1:
            edge = jnp.where(place[1] == 0, tile_cols - LANES, 0)
        else:
            edge = 0 if s == 0 else tile_cols - LANES
        at = pl.ds(pl.multiple_of(edge, LANES), LANES)
        sums[:, :, at] += side_in[s][...]
        sums[:, pl.ds(near_row, H), at] += near_ends[s][...]
        sums[:, pl.ds(far_row, H), at] += far_ends[s][...]
    rows = own_got.shape[1] - 8
    peak = jnp.maximum(jnp.max(own_got[:, rows:, :], axis=0), jnp.max(other_got[:, rows:, :], axis=0))
    top = MIX_OBJECT * jnp.max(peak, keepdims=True)
    inverse = 1.0 / ((1.0 - MIX_OBJECT) * cover[...] + top)
    for ch in range(2):
        out[ch] = tile[ch] + sums[ch] * inverse

    pr = probe.shape[1]
    pieces = pr // LANES
    both = [ref[:, 0:rows, :].reshape(-1, LANES) for ref in (own_got, other_got)]

    def update(parts):
        flat = [parts[j * len(parts) // pieces] for j in range(pieces)]
        span = flat[0].shape[0] // (pieces // len(parts))
        term = lambda j, ch: flat[j][(j % (pieces // len(parts))) * span + ch * pr :][:pr]
        weights = [term(j, 2) for j in range(pieces)]
        best = functools.reduce(jnp.maximum, weights)
        best = jnp.max(jnp.max(best.reshape(-1, 8, LANES), axis=0), keepdims=True)
        for j in range(pieces):
            cut = slice(j * LANES, (j + 1) * LANES)
            scale = 1.0 / ((1.0 - MIX_PROBE) * weights[j] + MIX_PROBE * best)
            for ch in range(2):
                new_probe[ch, :, cut] = probe[ch, :, cut] + term(j, ch) * scale

    for first in (0, 1):

        @pl.when(place[0] % 2 == first)
        def _():
            update([both[first], both[1 - first]])


def update_call(place, tile, middle, cover, near, far_side, side_in, ends, own, other, probe):
    sides = len(side_in)
    return pl.pallas_call(
        functools.partial(update_kernel, sides),
        out_shape=(jax.ShapeDtypeStruct(tile.shape, F32), jax.ShapeDtypeStruct(probe.shape, F32)),
        in_specs=[SMEM] + [VMEM] * (8 + 3 * sides),
        out_specs=(VMEM, VMEM),
        scratch_shapes=[pltpu.VMEM(tile.shape, F32)],
        compiler_params=pltpu.CompilerParams(vmem_limit_bytes=51 << 20),
        name="update",
    )(place, tile, middle, cover, near, far_side, *side_in, *ends, own, other, probe)


WIDE = ("rest", "core")
CHIPS = ("rest", "narrow")


def swap(x, axis, first):
    size = lax.axis_size(axis)
    pairs = []
    for i in range(first, size - 1, 2):
        pairs += [(i, i + 1), (i + 1, i)]
    return lax.ppermute(x, axis, pairs)


def shifted(x, axis, by):
    size = lax.axis_size(axis)
    return lax.ppermute(x, axis, [(i, i + by) for i in range(size) if 0 <= i + by < size])


def to_sides(pieces):
    if len(pieces) == 1:
        return [swap(pieces[0], "narrow", 0)]
    return [shifted(pieces[1], "narrow", 1), shifted(pieces[0], "narrow", -1)]


def to_corners(bands, first):
    wide, narrow = lax.axis_size(WIDE), lax.axis_size("narrow")
    steps = [0] if len(bands) == 1 else [-1, 1]
    got = []
    for s, step in enumerate(steps):
        pairs = []
        for i in range(first, wide - 1, 2):
            for n in range(narrow):
                m = 1 - n if step == 0 else n - step
                if 0 <= m < narrow:
                    pairs += [(i * narrow + n, (i + 1) * narrow + m), ((i + 1) * narrow + n, i * narrow + m)]
        band = bands[0] if step == 0 else bands[1 - s]
        got.append(lax.ppermute(band, (*WIDE, "narrow"), pairs))
    return got


def chip_exchange(chunks):
    return lax.all_to_all(chunks.reshape(-1, LANES), CHIPS, 0, 0, tiled=True).reshape(chunks.shape)


def after(x, *others):
    return lax.optimization_barrier((x, *others))[0]


def body(tile, probe, measured, rows, cols, counts):
    wide, narrow = lax.axis_index(WIDE), lax.axis_index("narrow")
    sides = 1 if lax.axis_size("narrow") == 2 else 2
    tile_rows, tile_cols = tile.shape[1:]
    even = wide % 2 == 0
    place = jnp.concatenate(
        [jnp.stack([wide, narrow, counts[0, 0]]).astype(jnp.int32), rows.reshape(-1), cols.reshape(-1)]
    )

    far_band, near_band, edges, far_ends, near_ends = pack_call(place, tile, sides)
    far_side = swap(far_band, WIDE, 1)
    far_corners = to_corners(far_ends, 1)
    side_in = to_sides(edges)
    near_corners = to_corners(near_ends, 0)
    near = swap(near_band, "core", 0)

    middle, near_rim, far_rim, side_rims, near_rim_ends, far_rim_ends, kept, sent, got_info = positions_call(
        place, tile, near, far_side, side_in, near_corners, far_corners, probe, measured
    )
    own_info = edges[0][:1, tile_rows:]

    terms = kept + swap(sent, "core", 0)
    near_got = swap(near_rim, "core", 0)
    far_got = swap(far_rim, WIDE, 1)
    side_got = to_sides(side_rims)
    info = jnp.concatenate([own_info, got_info], axis=0)[:, 0, :32].astype(jnp.int32)
    cover, peak = cover_call(place, after(info, terms), probe, tile_rows, tile_cols, sides)
    chips = lax.axis_size(CHIPS)
    got = chip_exchange(terms.reshape(chips, -1, LANES))
    chunk = jnp.sum(got, axis=0)
    rows_each = chunk.shape[0]
    chunk = after(jnp.concatenate([chunk, peak], axis=0), far_got, near_got, *side_got)
    got = chip_exchange(jnp.broadcast_to(chunk, (chips, *chunk.shape)))
    if rows_each % 8:
        peak = jnp.max(got[:, rows_each:], axis=0)
        got = jnp.concatenate([got[:, :rows_each].reshape(-1, LANES), peak], axis=0)[None]

    near_ends_got = to_corners(near_rim_ends, 0)
    far_ends_got = to_corners(far_rim_ends, 1)
    ends_got = near_ends_got + far_ends_got
    other = swap(after(got, *ends_got), "core", 0)
    return update_call(place, tile, middle, cover, near_got, far_got, side_got, ends_got, got, other, probe)


def solution(mesh):
    wide, narrow = mesh.devices.shape
    fine = Mesh(mesh.devices.reshape(wide // 2, 2, narrow), ("rest", "core", "narrow"))
    placed = (
        P(None, WIDE, "narrow"),
        P(),
        P(WIDE, "narrow", None, None, None),
        P(WIDE, "narrow", None),
        P(WIDE, "narrow", None),
        P(WIDE, "narrow"),
    )
    return jax.shard_map(
        body,
        mesh=fine,
        in_specs=placed,
        out_specs=(P(None, WIDE, "narrow"), P()),
        check_vma=False,
    )
```

```python
import functools
import math

import jax
import jax.numpy as jnp
import ml_dtypes
import numpy as np
from jax import lax
from jax.experimental import pallas as pl
from jax.experimental.pallas import tpu as pltpu
from jax.sharding import Mesh, PartitionSpec as P

H = 128
LANES = 128
CHUNK = 32
WAYS = 2
INFO = 8
GRANT = 50176 << 10
BF = jnp.bfloat16
F32 = jnp.float32
MIX_OBJECT = 0.5
MIX_PROBE = 0.5
VMEM = pl.BlockSpec(memory_space=pltpu.VMEM)
SMEM = pl.BlockSpec(memory_space=pltpu.SMEM)
ANY = pl.BlockSpec(memory_space=pl.ANY)
HBM = pl.BlockSpec(memory_space=pltpu.HBM)
COUNT, ROWS, COLS = 2, 3, 11


def rounded_pair(table):
    table = table.astype(np.float32)
    high = table.astype(ml_dtypes.bfloat16)
    low = (table - high.astype(np.float32)).astype(ml_dtypes.bfloat16)
    return high, low


def dft_tables(length):
    index = np.arange(length)
    angle = 2.0 * np.pi * ((index[:, None] * index[None, :]) % length) / length
    cos_high, cos_low = rounded_pair(np.cos(angle) / math.sqrt(length))
    sin_high, sin_low = rounded_pair(-np.sin(angle) / math.sqrt(length))
    left = np.concatenate([cos_high, sin_high, cos_high, sin_high, cos_low, sin_low], axis=1)
    right_high = np.block([[cos_high, sin_high], [-sin_high, cos_high]])
    right_low = np.block([[cos_low, sin_low], [-sin_low, cos_low]])
    right = np.concatenate([right_high, right_high, right_low], axis=0)
    return left, right


def split(x):
    high = x.astype(BF)
    return high, (x - high.astype(F32)).astype(BF)


def side_block(place, side, sides, blocks):
    if sides == 1:
        return jnp.where(place[1] == 0, blocks - 1, 0)
    return 0 if side == 0 else blocks - 1


def side_step(place, side, sides):
    if sides == 1:
        return jnp.where(place[1] == 0, 1, -1)
    return -1 if side == 0 else 1


def cover_kernel(tile_rows, tile_cols, sides, place, info, probe, cover, peak, total, power):
    pr = probe.shape[1]
    pieces = pr // LANES
    for j in range(pieces):
        cut = slice(j * LANES, (j + 1) * LANES)
        power[j] = probe[0, :, cut] * probe[0, :, cut] + probe[1, :, cut] * probe[1, :, cut]
    total[...] = jnp.zeros_like(total)
    lanes = lax.broadcasted_iota(jnp.int32, (CHUNK, LANES), 1)
    even = place[0] % 2 == 0
    steps_down = (0, jnp.where(even, 1, -1), jnp.where(even, -1, 1))
    steps_right = (0,) + tuple(side_step(place, s, sides) for s in range(sides))
    for v in range(3):
        for h in range(1 + sides):
            source = v * (1 + sides) + h
            down, right = steps_down[v], steps_right[h]

            def visit(k, carry):
                row = info[source, k] + pr - H + down * tile_rows
                col = info[source, 8 + k] + pr - H + right * tile_cols
                inside = (row > 0) & (row < pr + tile_rows) & (col > 0) & (col < pr + tile_cols)

                @pl.when(inside)
                def _():
                    shift = col & (LANES - 1)
                    block = col >> 7
                    low = lanes < shift
                    for q in range(pr // CHUNK):
                        turned = [
                            pltpu.roll(power[j, q * CHUNK : (q + 1) * CHUNK, :], shift, 1)
                            for j in range(pieces)
                        ]
                        here = pl.ds(row + q * CHUNK, CHUNK)
                        zero = jnp.zeros((CHUNK, LANES), F32)
                        total[block, here, :] += jnp.where(low, zero, turned[0])
                        for j in range(1, pieces):
                            total[block + j, here, :] += jnp.where(low, turned[j - 1], turned[j])
                        total[block + pieces, here, :] += jnp.where(low, turned[-1], zero)

                return carry

            lax.fori_loop(0, info[source, 16], visit, 0)
    first = pr // LANES
    best = jnp.zeros((8, LANES), F32)
    for b in range(tile_cols // LANES):
        own = total[first + b, pr : pr + tile_rows, :]
        cover[:, b * LANES : (b + 1) * LANES] = own
        best = jnp.maximum(best, jnp.max(own.reshape(tile_rows // 8, 8, LANES), axis=0))
    peak[...] = jnp.full((8, LANES), jnp.max(best), F32)


def cover_call(place, info, probe, tile_rows, tile_cols, sides):
    pr = probe.shape[1]
    blocks = (tile_cols + 2 * pr) // LANES + 1
    return pl.pallas_call(
        functools.partial(cover_kernel, tile_rows, tile_cols, sides),
        out_shape=(
            jax.ShapeDtypeStruct((tile_rows, tile_cols), F32),
            jax.ShapeDtypeStruct((8, LANES), F32),
        ),
        in_specs=[SMEM, SMEM, VMEM],
        out_specs=(VMEM, VMEM),
        scratch_shapes=[
            pltpu.VMEM((blocks, tile_rows + 2 * pr, LANES), F32),
            pltpu.VMEM((pr // LANES, pr, LANES), F32),
        ],
        compiler_params=pltpu.CompilerParams(vmem_limit_bytes=16 << 20),
        cost_estimate=pl.CostEstimate(flops=4_000_000, bytes_accessed=8_000_000, transcendentals=0),
        name="cover",
    )(place, info, probe)


def pack_kernel(sides, place, tile, *refs):
    far_band, near_band = refs[:2]
    edges, far_ends, near_ends = [refs[2 + i * sides : 2 + (i + 1) * sides] for i in range(3)]
    sems = refs[2 + 3 * sides]
    tile_rows, tile_cols = tile.shape[1:]
    even = place[0] % 2 == 0
    near_start = pl.multiple_of(jnp.where(even, tile_rows - H, 0), 8)
    far_start = pl.multiple_of(jnp.where(even, 0, tile_rows - H), 8)
    if sides == 1:
        starts = [pl.multiple_of(jnp.where(place[1] == 0, tile_cols - H, 0), LANES)]
    else:
        starts = [0, tile_cols - H]
    bands = [(far_band, far_start, H, 0), (near_band, near_start, H, 0)]
    for s, start in enumerate(starts):
        bands += [(edges[s], 0, tile_rows, start), (far_ends[s], far_start, H, start)]
        bands += [(near_ends[s], near_start, H, start)]
    copies = []
    for i, (band, row, height, col) in enumerate(bands):
        copies.append(
            pltpu.make_async_copy(
                tile.at[:, pl.ds(row, height), pl.ds(col, band.shape[2])], band.at[:, pl.ds(0, height), :], sems.at[i]
            )
        )
        copies[-1].start()
    lanes = lax.broadcasted_iota(jnp.int32, (INFO, LANES), 1)
    notes = jnp.where(lanes == 16, place[COUNT], 0)
    for k in range(8):
        notes = jnp.where(lanes == k, place[ROWS + k], jnp.where(lanes == 8 + k, place[COLS + k], notes))
    notes = notes.astype(F32)
    for band, row, height, col in bands:
        for ch in range(2):
            band[ch, height : height + INFO, 0:LANES] = notes
            if band.shape[2] > LANES:
                band[ch, height : height + INFO, LANES:] = jnp.zeros((INFO, band.shape[2] - LANES), F32)
    for copy in copies:
        copy.wait()


def pack_call(place, tile, sides):
    tile_rows, tile_cols = tile.shape[1:]
    shape = lambda height, width: jax.ShapeDtypeStruct((2, height + INFO, width), F32)
    shapes = [shape(H, tile_cols)] * 2 + [shape(tile_rows, LANES)] * sides + [shape(H, LANES)] * (2 * sides)
    out = pl.pallas_call(
        functools.partial(pack_kernel, sides),
        out_shape=shapes,
        in_specs=[SMEM, HBM],
        out_specs=[VMEM] * len(shapes),
        scratch_shapes=[pltpu.SemaphoreType.DMA((len(shapes),))],
        compiler_params=pltpu.CompilerParams(vmem_limit_bytes=8 << 20),
        name="pack",
    )(place, tile)
    return out[0], out[1], *[list(out[2 + i * sides : 2 + (i + 1) * sides]) for i in range(3)]


def positions_kernel(sides, *refs):
    place, tile, far_side, near = refs[0], refs[1], refs[2 + sides], refs[3 + 3 * sides]
    far_corners, side_in, near_corners = [
        refs[at : at + sides] for at in (2, 3 + sides, 3 + 2 * sides)
    ]
    probe_in, measured, left_in, right_in = refs[4 + 3 * sides : 8 + 3 * sides]
    middle, near_rim, far_rim, info = refs[8 + 3 * sides : 12 + 3 * sides]
    side_out, near_ends, far_ends = [refs[12 + i * sides : 12 + (i + 1) * sides] for i in range(3, 6)]
    kept, sent, probe_sums, ext, grad = refs[12 + 6 * sides : 17 + 6 * sides]
    scratch = refs[17 + 6 * sides :]
    left, right, levels, probe = scratch[:4]
    table_sems, level_sems, ext_sems = scratch[4:7]
    scratch = scratch[7:]
    patches, exits, stacks, wides, fields = [scratch[i * WAYS : (i + 1) * WAYS] for i in range(5)]

    pr = probe_in.shape[1]
    pieces = pr // LANES
    ext_rows = ext.shape[1]
    blocks = ext.shape[0] // 2
    own_blocks = blocks - 2
    tile_rows, tile_cols = ext_rows - 2 * H, own_blocks * LANES
    even = place[0] % 2 == 0
    near_row = pl.multiple_of(jnp.where(even, tile_rows + H, 0), 8)
    far_row = pl.multiple_of(jnp.where(even, 0, tile_rows + H), 8)
    side_blocks = [side_block(place, s, sides, blocks) for s in range(sides)]
    own, near_rows, far_rows = pl.ds(H, tile_rows), pl.ds(near_row, H), pl.ds(far_row, H)

    copies = []

    def fetch(source, target):
        copies.append(pltpu.make_async_copy(source, target, ext_sems.at[len(copies)]))
        copies[-1].start()

    for ch in range(2):
        for b in range(own_blocks):
            at, cut = ch * blocks + 1 + b, pl.ds(b * LANES, LANES)
            fetch(tile.at[ch, :, cut], ext.at[at, own, :])
            fetch(near.at[ch, pl.ds(0, H), cut], ext.at[at, near_rows, :])
            fetch(far_side.at[ch, pl.ds(0, H), cut], ext.at[at, far_rows, :])
        for s in range(sides):
            at = ch * blocks + side_blocks[s]
            fetch(side_in[s].at[ch, pl.ds(0, tile_rows), :], ext.at[at, own, :])
            fetch(near_corners[s].at[ch, pl.ds(0, H), :], ext.at[at, near_rows, :])
            fetch(far_corners[s].at[ch, pl.ds(0, H), :], ext.at[at, far_rows, :])
    for s in range(sides):
        fetch(side_in[s].at[0, pl.ds(tile_rows, INFO), :], info.at[s])
        fetch(near_corners[s].at[0, pl.ds(H, INFO), :], info.at[sides + 1 + s])
        fetch(far_corners[s].at[0, pl.ds(H, INFO), :], info.at[2 * sides + 2 + s])
    fetch(near.at[0, pl.ds(H, INFO), pl.ds(0, LANES)], info.at[sides])
    fetch(far_side.at[0, pl.ds(H, INFO), pl.ds(0, LANES)], info.at[2 * sides + 1])
    tables = [
        pltpu.make_async_copy(left_in, left, table_sems.at[0]),
        pltpu.make_async_copy(right_in, right, table_sems.at[1]),
        pltpu.make_async_copy(probe_in, probe, table_sems.at[2]),
    ]
    for copy in tables:
        copy.start()

    live_slots = place[COUNT]

    def level_copy(i):
        return pltpu.make_async_copy(measured.at[0, 0, i], levels.at[i], level_sems.at[i])

    def start_levels(first):
        for w in range(WAYS):

            @pl.when(first + w < live_slots)
            def _():
                level_copy(first + w).start()

    start_levels(0)
    if sides == 1:
        for ch in range(2):
            ext[ch * blocks + blocks - 1 - side_blocks[0]] = jnp.zeros((ext_rows, LANES), F32)
    grad[...] = jnp.zeros_like(grad)
    probe_sums[...] = jnp.zeros_like(probe_sums)
    for copy in copies:
        copy.wait()
    tables[2].wait()
    lanes = lax.broadcasted_iota(jnp.int32, (CHUNK, LANES), 1)

    def put(stack, value, part, q, first):
        width = value.shape[1]
        high, low = split(value)
        rows_at = lambda block: slice(block * pr + q * CHUNK, block * pr + (q + 1) * CHUNK)
        here, there = slice(first, first + width), slice(pr + first, pr + first + width)
        if part == 0:
            stack[rows_at(0), here], stack[rows_at(1), there] = high, high
            stack[rows_at(2), here], stack[rows_at(3), there] = low, low
        else:
            stack[rows_at(0), there], stack[rows_at(1), here] = high, -high
            stack[rows_at(2), there], stack[rows_at(3), here] = low, -low

    def times_left(w):
        stack = jnp.concatenate([stacks[w][...], stacks[w][0 : 2 * pr]], axis=0)
        fields[w][...] = jnp.dot(left[...], stack, preferred_element_type=F32)

    def times_right(w):
        for q in range(pr // CHUNK):
            cut = slice(q * CHUNK, (q + 1) * CHUNK)
            high, low = split(fields[w][cut, :])
            wides[w][cut, 0 : 2 * pr] = high
            wides[w][cut, 2 * pr : 4 * pr] = low
        stack = jnp.concatenate([wides[w][...], wides[w][:, 0 : 2 * pr]], axis=1)
        fields[w][...] = jnp.dot(stack, right[...], preferred_element_type=F32)

    def load(w, k):
        row, col = place[ROWS + k], place[COLS + k]
        shift, block = col & (LANES - 1), col >> 7
        back = (LANES - shift) & (LANES - 1)
        keep = lanes < LANES - shift
        for q in range(pr // CHUNK):
            cut = slice(q * CHUNK, (q + 1) * CHUNK)
            here = pl.ds(row + q * CHUNK, CHUNK)
            seen = []
            for ch in range(2):
                turned = [
                    pltpu.roll(ext[ch * blocks + block + j, here, :], back, 1)
                    for j in range(pieces + 1)
                ]
                seen.append([jnp.where(keep, turned[j], turned[j + 1]) for j in range(pieces)])
            for j in range(pieces):
                part = slice(j * LANES, (j + 1) * LANES)
                probe_real, probe_imag = probe[0, cut, part], probe[1, cut, part]
                real, imag = seen[0][j], seen[1][j]
                patches[w][0, cut, part], patches[w][1, cut, part] = real, imag
                exit_real = probe_real * real - probe_imag * imag
                exit_imag = probe_real * imag + probe_imag * real
                exits[w][0, cut, part], exits[w][1, cut, part] = exit_real, exit_imag
                put(stacks[w], exit_real, 0, q, j * LANES)
                put(stacks[w], exit_imag, 1, q, j * LANES)

    def project(w, k):
        for q in range(pr // CHUNK):
            cut = slice(q * CHUNK, (q + 1) * CHUNK)
            real, imag = fields[w][cut, 0:pr], fields[w][cut, pr : 2 * pr]
            factor = jnp.sqrt(levels[k, cut, :]) * lax.rsqrt(real * real + imag * imag + 1.0)
            put(stacks[w], real * factor, 0, q, 0)
            put(stacks[w], -(imag * factor), 1, q, 0)

    def finish(w, k, live):
        row, col = place[ROWS + k], place[COLS + k]
        shift, block = col & (LANES - 1), col >> 7
        low = lanes < shift
        zero = jnp.zeros((CHUNK, LANES), F32)
        for q in range(pr // CHUNK):
            cut = slice(q * CHUNK, (q + 1) * CHUNK)
            here = pl.ds(row + q * CHUNK, CHUNK)
            turned = [[], []]
            for j in range(pieces):
                part = slice(j * LANES, (j + 1) * LANES)
                other = slice(pr + j * LANES, pr + (j + 1) * LANES)
                diff_real = fields[w][cut, part] - exits[w][0, cut, part]
                diff_imag = -fields[w][cut, other] - exits[w][1, cut, part]
                real, imag = patches[w][0, cut, part], patches[w][1, cut, part]
                weight = real * real + imag * imag
                if live is not None:
                    diff_real, diff_imag = diff_real * live, diff_imag * live
                    weight = weight * live
                probe_real, probe_imag = probe[0, cut, part], probe[1, cut, part]
                turned[0].append(pltpu.roll(probe_real * diff_real + probe_imag * diff_imag, shift, 1))
                turned[1].append(pltpu.roll(probe_real * diff_imag - probe_imag * diff_real, shift, 1))
                probe_sums[j, 0, cut, :] += real * diff_real + imag * diff_imag
                probe_sums[j, 1, cut, :] += real * diff_imag - imag * diff_real
                probe_sums[j, 2, cut, :] += weight
            for ch in range(2):
                at = ch * blocks + block
                grad[at, here, :] += jnp.where(low, zero, turned[ch][0])
                for j in range(1, pieces):
                    grad[at + j, here, :] += jnp.where(low, turned[ch][j - 1], turned[ch][j])
                grad[at + pieces, here, :] += jnp.where(low, turned[ch][-1], zero)

    def visit(i, carry):
        first = i * WAYS
        slots = [jnp.minimum(first + w, live_slots - 1) for w in range(WAYS)]
        lives = [None] + [jnp.where(first + w < live_slots, 1.0, 0.0) for w in range(1, WAYS)]
        for w in range(WAYS):

            @pl.when(first + w < live_slots)
            def _():
                level_copy(slots[w]).wait()

        start_levels(first + WAYS)

        @pl.when(i == 0)
        def _():
            tables[0].wait()
            tables[1].wait()

        for w in range(WAYS):
            load(w, slots[w])
            times_left(w)
        for w in range(WAYS):
            times_right(w)
        for w in range(WAYS):
            project(w, slots[w])
            times_left(w)
        for w in range(WAYS):
            times_right(w)
        for w in range(WAYS):
            finish(w, slots[w], lives[w])
        return carry

    lax.fori_loop(0, (live_slots + WAYS - 1) // WAYS, visit, 0)
    core = place[0] % 2
    span = pieces // 2
    for j in range(span):
        for ch in range(3):
            at = pl.ds((j * 3 + ch) * pr, pr)
            kept[at, :] = probe_sums[core * span + j, ch]
            sent[at, :] = probe_sums[(1 - core) * span + j, ch]
    for ch in range(2):
        for b in range(own_blocks):
            at, cut = ch * blocks + 1 + b, slice(b * LANES, (b + 1) * LANES)
            middle[ch, :, cut] = grad[at, own, :]
            near_rim[ch, :, cut] = grad[at, near_rows, :]
            far_rim[ch, :, cut] = grad[at, far_rows, :]
        for s in range(sides):
            at = ch * blocks + side_blocks[s]
            side_out[s][ch] = grad[at, own, :]
            near_ends[s][ch] = grad[at, near_rows, :]
            far_ends[s][ch] = grad[at, far_rows, :]


def positions_call(place, tile, near, far_side, side_in, near_corners, far_corners, probe, measured):
    pr = probe.shape[1]
    sides = len(side_in)
    tile_rows, tile_cols = tile.shape[1:]
    ext_rows = tile_rows + 2 * H
    blocks = (tile_cols + 2 * H) // LANES
    left, right = (jnp.asarray(table) for table in dft_tables(pr))
    shape = lambda *dims: jax.ShapeDtypeStruct(dims, F32)
    slots = measured.shape[2]
    rim = shape(2, H, tile_cols)
    middle, near_rim, far_rim, info, *rest = pl.pallas_call(
        functools.partial(positions_kernel, sides),
        out_shape=(
            shape(2, tile_rows, tile_cols),
            rim,
            rim,
            shape(3 * sides + 2, INFO, LANES),
            *[shape(2, tile_rows, LANES)] * sides,
            *[shape(2, H, LANES)] * (2 * sides),
            shape(3 * pr * pr // LANES // 2, LANES),
            shape(3 * pr * pr // LANES // 2, LANES),
        ),
        in_specs=[SMEM, HBM] + [ANY] * (2 + 3 * sides) + [HBM] * 4,
        out_specs=(VMEM,) * (6 + 3 * sides),
        scratch_shapes=[
            pltpu.VMEM((pr // LANES, 3, pr, LANES), F32),
            *[pltpu.VMEM((2 * blocks, ext_rows, LANES), F32)] * 2,
            pltpu.VMEM(left.shape, BF),
            pltpu.VMEM(right.shape, BF),
            pltpu.VMEM((slots, pr, pr), F32),
            pltpu.VMEM(probe.shape, F32),
            pltpu.SemaphoreType.DMA((3,)),
            pltpu.SemaphoreType.DMA((slots,)),
            pltpu.SemaphoreType.DMA((6 * blocks + 3 * sides + 2,)),
            *[pltpu.VMEM((2, pr, pr), F32)] * (2 * WAYS),
            *[pltpu.VMEM((4 * pr, 2 * pr), BF)] * WAYS,
            *[pltpu.VMEM((pr, 4 * pr), BF)] * WAYS,
            *[pltpu.VMEM((pr, 2 * pr), F32)] * WAYS,
        ],
        compiler_params=pltpu.CompilerParams(vmem_limit_bytes=GRANT),
        cost_estimate=pl.CostEstimate(
            flops=slots * 96 * pr * pr * pr, bytes_accessed=16_000_000, transcendentals=slots * 2 * pr * pr
        ),
        name="positions",
    )(place, tile, *far_corners, far_side, *side_in, *near_corners, near, probe, measured, left, right)
    ends = [rest[i * sides : (i + 1) * sides] for i in range(3)]
    return middle, near_rim, far_rim, *ends, *rest[3 * sides :], info


def update_kernel(sides, *refs):
    place, tile, middle, cover, near, far_side = refs[:6]
    side_in, near_ends, far_ends = [refs[6 + i * sides : 6 + (i + 1) * sides] for i in range(3)]
    own_got, other_got, probe, out, new_probe, sums = refs[6 + 3 * sides :]
    tile_rows, tile_cols = tile.shape[1:]
    own_blocks = tile_cols // LANES
    even = place[0] % 2 == 0
    sums[...] = middle[...]
    near_row = pl.multiple_of(jnp.where(even, tile_rows - H, 0), 8)
    far_row = pl.multiple_of(jnp.where(even, 0, tile_rows - H), 8)
    sums[:, pl.ds(near_row, H), :] += near[...]
    sums[:, pl.ds(far_row, H), :] += far_side[...]
    for s in range(sides):
        if sides == 1:
            edge = jnp.where(place[1] == 0, tile_cols - LANES, 0)
        else:
            edge = 0 if s == 0 else tile_cols - LANES
        at = pl.ds(pl.multiple_of(edge, LANES), LANES)
        sums[:, :, at] += side_in[s][...]
        sums[:, pl.ds(near_row, H), at] += near_ends[s][...]
        sums[:, pl.ds(far_row, H), at] += far_ends[s][...]
    rows = own_got.shape[1] - 8
    peak = jnp.maximum(jnp.max(own_got[:, rows:, :], axis=0), jnp.max(other_got[:, rows:, :], axis=0))
    top = MIX_OBJECT * jnp.max(peak, keepdims=True)
    inverse = 1.0 / ((1.0 - MIX_OBJECT) * cover[...] + top)
    for ch in range(2):
        out[ch] = tile[ch] + sums[ch] * inverse

    pr = probe.shape[1]
    pieces = pr // LANES
    both = [ref[:, 0:rows, :].reshape(-1, LANES) for ref in (own_got, other_got)]

    def update(parts):
        flat = [parts[j * len(parts) // pieces] for j in range(pieces)]
        span = flat[0].shape[0] // (pieces // len(parts))
        term = lambda j, ch: flat[j][(j % (pieces // len(parts))) * span + ch * pr :][:pr]
        weights = [term(j, 2) for j in range(pieces)]
        best = functools.reduce(jnp.maximum, weights)
        best = jnp.max(jnp.max(best.reshape(-1, 8, LANES), axis=0), keepdims=True)
        for j in range(pieces):
            cut = slice(j * LANES, (j + 1) * LANES)
            scale = 1.0 / ((1.0 - MIX_PROBE) * weights[j] + MIX_PROBE * best)
            for ch in range(2):
                new_probe[ch, :, cut] = probe[ch, :, cut] + term(j, ch) * scale

    for first in (0, 1):

        @pl.when(place[0] % 2 == first)
        def _():
            update([both[first], both[1 - first]])


def update_call(place, tile, middle, cover, near, far_side, side_in, ends, own, other, probe):
    sides = len(side_in)
    return pl.pallas_call(
        functools.partial(update_kernel, sides),
        out_shape=(jax.ShapeDtypeStruct(tile.shape, F32), jax.ShapeDtypeStruct(probe.shape, F32)),
        in_specs=[SMEM] + [VMEM] * (8 + 3 * sides),
        out_specs=(VMEM, VMEM),
        scratch_shapes=[pltpu.VMEM(tile.shape, F32)],
        compiler_params=pltpu.CompilerParams(vmem_limit_bytes=51 << 20),
        name="update",
    )(place, tile, middle, cover, near, far_side, *side_in, *ends, own, other, probe)


WIDE = ("rest", "core")
CHIPS = ("rest", "narrow")


def swap(x, axis, first):
    size = lax.axis_size(axis)
    pairs = []
    for i in range(first, size - 1, 2):
        pairs += [(i, i + 1), (i + 1, i)]
    return lax.ppermute(x, axis, pairs)


def shifted(x, axis, by):
    size = lax.axis_size(axis)
    return lax.ppermute(x, axis, [(i, i + by) for i in range(size) if 0 <= i + by < size])


def to_sides(pieces):
    if len(pieces) == 1:
        return [swap(pieces[0], "narrow", 0)]
    return [shifted(pieces[1], "narrow", 1), shifted(pieces[0], "narrow", -1)]


def to_corners(bands, first):
    wide, narrow = lax.axis_size(WIDE), lax.axis_size("narrow")
    steps = [0] if len(bands) == 1 else [-1, 1]
    got = []
    for s, step in enumerate(steps):
        pairs = []
        for i in range(first, wide - 1, 2):
            for n in range(narrow):
                m = 1 - n if step == 0 else n - step
                if 0 <= m < narrow:
                    pairs += [(i * narrow + n, (i + 1) * narrow + m), ((i + 1) * narrow + n, i * narrow + m)]
        band = bands[0] if step == 0 else bands[1 - s]
        got.append(lax.ppermute(band, (*WIDE, "narrow"), pairs))
    return got


def chip_exchange(chunks):
    return lax.all_to_all(chunks.reshape(-1, LANES), CHIPS, 0, 0, tiled=True).reshape(chunks.shape)


def after(x, *others):
    return lax.optimization_barrier((x, *others))[0]


def body(tile, probe, measured, rows, cols, counts):
    wide, narrow = lax.axis_index(WIDE), lax.axis_index("narrow")
    sides = 1 if lax.axis_size("narrow") == 2 else 2
    tile_rows, tile_cols = tile.shape[1:]
    even = wide % 2 == 0
    place = jnp.concatenate(
        [jnp.stack([wide, narrow, counts[0, 0]]).astype(jnp.int32), rows.reshape(-1), cols.reshape(-1)]
    )

    far_band, near_band, edges, far_ends, near_ends = pack_call(place, tile, sides)
    far_side = swap(far_band, WIDE, 1)
    far_corners = to_corners(far_ends, 1)
    side_in = to_sides(edges)
    near_corners = to_corners(near_ends, 0)
    near = swap(near_band, "core", 0)

    middle, near_rim, far_rim, side_rims, near_rim_ends, far_rim_ends, kept, sent, got_info = positions_call(
        place, tile, near, far_side, side_in, near_corners, far_corners, probe, measured
    )
    own_info = edges[0][:1, tile_rows:]

    terms = kept + swap(sent, "core", 0)
    near_got = swap(near_rim, "core", 0)
    far_got = swap(far_rim, WIDE, 1)
    side_got = to_sides(side_rims)
    info = jnp.concatenate([own_info, got_info], axis=0)[:, 0, :32].astype(jnp.int32)
    cover, peak = cover_call(place, after(info, terms), probe, tile_rows, tile_cols, sides)
    chips = lax.axis_size(CHIPS)
    got = chip_exchange(terms.reshape(chips, -1, LANES))
    chunk = jnp.sum(got, axis=0)
    rows_each = chunk.shape[0]
    chunk = after(jnp.concatenate([chunk, peak], axis=0), far_got, near_got, *side_got)
    got = chip_exchange(jnp.broadcast_to(chunk, (chips, *chunk.shape)))
    if rows_each % 8:
        peak = jnp.max(got[:, rows_each:], axis=0)
        got = jnp.concatenate([got[:, :rows_each].reshape(-1, LANES), peak], axis=0)[None]

    near_ends_got = to_corners(near_rim_ends, 0)
    far_ends_got = to_corners(far_rim_ends, 1)
    ends_got = near_ends_got + far_ends_got
    other = swap(after(got, *ends_got), "core", 0)
    return update_call(place, tile, middle, cover, near_got, far_got, side_got, ends_got, got, other, probe)


def solution(mesh):
    wide, narrow = mesh.devices.shape
    fine = Mesh(mesh.devices.reshape(wide // 2, 2, narrow), ("rest", "core", "narrow"))
    placed = (
        P(None, WIDE, "narrow"),
        P(),
        P(WIDE, "narrow", None, None, None),
        P(WIDE, "narrow", None),
        P(WIDE, "narrow", None),
        P(WIDE, "narrow"),
    )
    return jax.shard_map(
        body,
        mesh=fine,
        in_specs=placed,
        out_specs=(P(None, WIDE, "narrow"), P()),
        check_vma=False,
    )
```

```python
import functools
import math

import jax
import jax.numpy as jnp
import ml_dtypes
import numpy as np
from jax import lax
from jax.experimental import pallas as pl
from jax.experimental.pallas import tpu as pltpu
from jax.sharding import Mesh, PartitionSpec as P

H = 128
LANES = 128
CHUNK = 32
WAYS = 2
INFO = 8
GRANT = 50176 << 10
BF = jnp.bfloat16
F32 = jnp.float32
MIX_OBJECT = 0.5
MIX_PROBE = 0.5
VMEM = pl.BlockSpec(memory_space=pltpu.VMEM)
SMEM = pl.BlockSpec(memory_space=pltpu.SMEM)
ANY = pl.BlockSpec(memory_space=pl.ANY)
HBM = pl.BlockSpec(memory_space=pltpu.HBM)
COUNT, ROWS, COLS = 2, 3, 11


def rounded_pair(table):
    table = table.astype(np.float32)
    high = table.astype(ml_dtypes.bfloat16)
    low = (table - high.astype(np.float32)).astype(ml_dtypes.bfloat16)
    return high, low


def dft_tables(length):
    index = np.arange(length)
    angle = 2.0 * np.pi * ((index[:, None] * index[None, :]) % length) / length
    cos_high, cos_low = rounded_pair(np.cos(angle) / math.sqrt(length))
    sin_high, sin_low = rounded_pair(-np.sin(angle) / math.sqrt(length))
    left = np.concatenate([cos_high, sin_high, cos_high, sin_high, cos_low, sin_low], axis=1)
    right_high = np.block([[cos_high, sin_high], [-sin_high, cos_high]])
    right_low = np.block([[cos_low, sin_low], [-sin_low, cos_low]])
    right = np.concatenate([right_high, right_high, right_low], axis=0)
    return left, right


def split(x):
    high = x.astype(BF)
    return high, (x - high.astype(F32)).astype(BF)


def side_block(place, side, sides, blocks):
    if sides == 1:
        return jnp.where(place[1] == 0, blocks - 1, 0)
    return 0 if side == 0 else blocks - 1


def side_step(place, side, sides):
    if sides == 1:
        return jnp.where(place[1] == 0, 1, -1)
    return -1 if side == 0 else 1


def cover_kernel(tile_rows, tile_cols, sides, place, info, probe, cover, peak, total, power):
    pr = probe.shape[1]
    pieces = pr // LANES
    for j in range(pieces):
        cut = slice(j * LANES, (j + 1) * LANES)
        power[j] = probe[0, :, cut] * probe[0, :, cut] + probe[1, :, cut] * probe[1, :, cut]
    total[...] = jnp.zeros_like(total)
    lanes = lax.broadcasted_iota(jnp.int32, (CHUNK, LANES), 1)
    even = place[0] % 2 == 0
    steps_down = (0, jnp.where(even, 1, -1), jnp.where(even, -1, 1))
    steps_right = (0,) + tuple(side_step(place, s, sides) for s in range(sides))
    for v in range(3):
        for h in range(1 + sides):
            source = v * (1 + sides) + h
            down, right = steps_down[v], steps_right[h]

            def visit(k, carry):
                row = info[source, k] + pr - H + down * tile_rows
                col = info[source, 8 + k] + pr - H + right * tile_cols
                inside = (row > 0) & (row < pr + tile_rows) & (col > 0) & (col < pr + tile_cols)

                @pl.when(inside)
                def _():
                    shift = col & (LANES - 1)
                    block = col >> 7
                    low = lanes < shift
                    for q in range(pr // CHUNK):
                        turned = [
                            pltpu.roll(power[j, q * CHUNK : (q + 1) * CHUNK, :], shift, 1)
                            for j in range(pieces)
                        ]
                        here = pl.ds(row + q * CHUNK, CHUNK)
                        zero = jnp.zeros((CHUNK, LANES), F32)
                        total[block, here, :] += jnp.where(low, zero, turned[0])
                        for j in range(1, pieces):
                            total[block + j, here, :] += jnp.where(low, turned[j - 1], turned[j])
                        total[block + pieces, here, :] += jnp.where(low, turned[-1], zero)

                return carry

            lax.fori_loop(0, info[source, 16], visit, 0)
    first = pr // LANES
    best = jnp.zeros((8, LANES), F32)
    for b in range(tile_cols // LANES):
        own = total[first + b, pr : pr + tile_rows, :]
        cover[:, b * LANES : (b + 1) * LANES] = own
        best = jnp.maximum(best, jnp.max(own.reshape(tile_rows // 8, 8, LANES), axis=0))
    peak[...] = jnp.full((8, LANES), jnp.max(best), F32)


def cover_call(place, info, probe, tile_rows, tile_cols, sides):
    pr = probe.shape[1]
    blocks = (tile_cols + 2 * pr) // LANES + 1
    return pl.pallas_call(
        functools.partial(cover_kernel, tile_rows, tile_cols, sides),
        out_shape=(
            jax.ShapeDtypeStruct((tile_rows, tile_cols), F32),
            jax.ShapeDtypeStruct((8, LANES), F32),
        ),
        in_specs=[SMEM, SMEM, VMEM],
        out_specs=(VMEM, VMEM),
        scratch_shapes=[
            pltpu.VMEM((blocks, tile_rows + 2 * pr, LANES), F32),
            pltpu.VMEM((pr // LANES, pr, LANES), F32),
        ],
        compiler_params=pltpu.CompilerParams(vmem_limit_bytes=16 << 20),
        cost_estimate=pl.CostEstimate(flops=4_000_000, bytes_accessed=8_000_000, transcendentals=0),
        name="cover",
    )(place, info, probe)


def pack_kernel(sides, place, tile, *refs):
    far_band, near_band = refs[:2]
    edges, far_ends, near_ends = [refs[2 + i * sides : 2 + (i + 1) * sides] for i in range(3)]
    sems = refs[2 + 3 * sides]
    tile_rows, tile_cols = tile.shape[1:]
    even = place[0] % 2 == 0
    near_start = pl.multiple_of(jnp.where(even, tile_rows - H, 0), 8)
    far_start = pl.multiple_of(jnp.where(even, 0, tile_rows - H), 8)
    if sides == 1:
        starts = [pl.multiple_of(jnp.where(place[1] == 0, tile_cols - H, 0), LANES)]
    else:
        starts = [0, tile_cols - H]
    bands = [(far_band, far_start, H, 0), (near_band, near_start, H, 0)]
    for s, start in enumerate(starts):
        bands += [(edges[s], 0, tile_rows, start), (far_ends[s], far_start, H, start)]
        bands += [(near_ends[s], near_start, H, start)]
    copies = []
    for i, (band, row, height, col) in enumerate(bands):
        copies.append(
            pltpu.make_async_copy(
                tile.at[:, pl.ds(row, height), pl.ds(col, band.shape[2])], band.at[:, pl.ds(0, height), :], sems.at[i]
            )
        )
        copies[-1].start()
    lanes = lax.broadcasted_iota(jnp.int32, (INFO, LANES), 1)
    notes = jnp.where(lanes == 16, place[COUNT], 0)
    for k in range(8):
        notes = jnp.where(lanes == k, place[ROWS + k], jnp.where(lanes == 8 + k, place[COLS + k], notes))
    notes = notes.astype(F32)
    for band, row, height, col in bands:
        for ch in range(2):
            band[ch, height : height + INFO, 0:LANES] = notes
            if band.shape[2] > LANES:
                band[ch, height : height + INFO, LANES:] = jnp.zeros((INFO, band.shape[2] - LANES), F32)
    for copy in copies:
        copy.wait()


def pack_call(place, tile, sides):
    tile_rows, tile_cols = tile.shape[1:]
    shape = lambda height, width: jax.ShapeDtypeStruct((2, height + INFO, width), F32)
    shapes = [shape(H, tile_cols)] * 2 + [shape(tile_rows, LANES)] * sides + [shape(H, LANES)] * (2 * sides)
    out = pl.pallas_call(
        functools.partial(pack_kernel, sides),
        out_shape=shapes,
        in_specs=[SMEM, HBM],
        out_specs=[VMEM] * len(shapes),
        scratch_shapes=[pltpu.SemaphoreType.DMA((len(shapes),))],
        compiler_params=pltpu.CompilerParams(vmem_limit_bytes=8 << 20),
        name="pack",
    )(place, tile)
    return out[0], out[1], *[list(out[2 + i * sides : 2 + (i + 1) * sides]) for i in range(3)]


def positions_kernel(sides, *refs):
    place, tile, far_side, near = refs[0], refs[1], refs[2 + sides], refs[3 + 3 * sides]
    far_corners, side_in, near_corners = [
        refs[at : at + sides] for at in (2, 3 + sides, 3 + 2 * sides)
    ]
    probe_in, measured, left_in, right_in = refs[4 + 3 * sides : 8 + 3 * sides]
    middle, near_rim, far_rim, info = refs[8 + 3 * sides : 12 + 3 * sides]
    side_out, near_ends, far_ends = [refs[12 + i * sides : 12 + (i + 1) * sides] for i in range(3, 6)]
    kept, sent, probe_sums, ext, grad = refs[12 + 6 * sides : 17 + 6 * sides]
    scratch = refs[17 + 6 * sides :]
    left, right, levels, probe = scratch[:4]
    table_sems, level_sems, ext_sems = scratch[4:7]
    scratch = scratch[7:]
    patches, exits, stacks, wides, fields = [scratch[i * WAYS : (i + 1) * WAYS] for i in range(5)]

    pr = probe_in.shape[1]
    pieces = pr // LANES
    ext_rows = ext.shape[1]
    blocks = ext.shape[0] // 2
    own_blocks = blocks - 2
    tile_rows, tile_cols = ext_rows - 2 * H, own_blocks * LANES
    even = place[0] % 2 == 0
    near_row = pl.multiple_of(jnp.where(even, tile_rows + H, 0), 8)
    far_row = pl.multiple_of(jnp.where(even, 0, tile_rows + H), 8)
    side_blocks = [side_block(place, s, sides, blocks) for s in range(sides)]
    own, near_rows, far_rows = pl.ds(H, tile_rows), pl.ds(near_row, H), pl.ds(far_row, H)

    copies = []

    def fetch(source, target):
        copies.append(pltpu.make_async_copy(source, target, ext_sems.at[len(copies)]))
        copies[-1].start()

    for ch in range(2):
        for b in range(own_blocks):
            at, cut = ch * blocks + 1 + b, pl.ds(b * LANES, LANES)
            fetch(tile.at[ch, :, cut], ext.at[at, own, :])
            fetch(near.at[ch, pl.ds(0, H), cut], ext.at[at, near_rows, :])
            fetch(far_side.at[ch, pl.ds(0, H), cut], ext.at[at, far_rows, :])
        for s in range(sides):
            at = ch * blocks + side_blocks[s]
            fetch(side_in[s].at[ch, pl.ds(0, tile_rows), :], ext.at[at, own, :])
            fetch(near_corners[s].at[ch, pl.ds(0, H), :], ext.at[at, near_rows, :])
            fetch(far_corners[s].at[ch, pl.ds(0, H), :], ext.at[at, far_rows, :])
    for s in range(sides):
        fetch(side_in[s].at[0, pl.ds(tile_rows, INFO), :], info.at[s])
        fetch(near_corners[s].at[0, pl.ds(H, INFO), :], info.at[sides + 1 + s])
        fetch(far_corners[s].at[0, pl.ds(H, INFO), :], info.at[2 * sides + 2 + s])
    fetch(near.at[0, pl.ds(H, INFO), pl.ds(0, LANES)], info.at[sides])
    fetch(far_side.at[0, pl.ds(H, INFO), pl.ds(0, LANES)], info.at[2 * sides + 1])
    tables = [
        pltpu.make_async_copy(left_in, left, table_sems.at[0]),
        pltpu.make_async_copy(right_in, right, table_sems.at[1]),
        pltpu.make_async_copy(probe_in, probe, table_sems.at[2]),
    ]
    for copy in tables:
        copy.start()

    live_slots = place[COUNT]

    def level_copy(i):
        return pltpu.make_async_copy(measured.at[0, 0, i], levels.at[i], level_sems.at[i])

    def start_levels(first):
        for w in range(WAYS):

            @pl.when(first + w < live_slots)
            def _():
                level_copy(first + w).start()

    start_levels(0)
    if sides == 1:
        for ch in range(2):
            ext[ch * blocks + blocks - 1 - side_blocks[0]] = jnp.zeros((ext_rows, LANES), F32)
    grad[...] = jnp.zeros_like(grad)
    probe_sums[...] = jnp.zeros_like(probe_sums)
    for copy in copies:
        copy.wait()
    tables[2].wait()
    lanes = lax.broadcasted_iota(jnp.int32, (CHUNK, LANES), 1)

    def put(stack, value, part, q, first):
        width = value.shape[1]
        high, low = split(value)
        rows_at = lambda block: slice(block * pr + q * CHUNK, block * pr + (q + 1) * CHUNK)
        here, there = slice(first, first + width), slice(pr + first, pr + first + width)
        if part == 0:
            stack[rows_at(0), here], stack[rows_at(1), there] = high, high
            stack[rows_at(2), here], stack[rows_at(3), there] = low, low
        else:
            stack[rows_at(0), there], stack[rows_at(1), here] = high, -high
            stack[rows_at(2), there], stack[rows_at(3), here] = low, -low

    def times_left(w):
        stack = jnp.concatenate([stacks[w][...], stacks[w][0 : 2 * pr]], axis=0)
        fields[w][...] = jnp.dot(left[...], stack, preferred_element_type=F32)

    def times_right(w):
        for q in range(pr // CHUNK):
            cut = slice(q * CHUNK, (q + 1) * CHUNK)
            high, low = split(fields[w][cut, :])
            wides[w][cut, 0 : 2 * pr] = high
            wides[w][cut, 2 * pr : 4 * pr] = low
        stack = jnp.concatenate([wides[w][...], wides[w][:, 0 : 2 * pr]], axis=1)
        fields[w][...] = jnp.dot(stack, right[...], preferred_element_type=F32)

    def load(w, k):
        row, col = place[ROWS + k], place[COLS + k]
        shift, block = col & (LANES - 1), col >> 7
        back = (LANES - shift) & (LANES - 1)
        keep = lanes < LANES - shift
        for q in range(pr // CHUNK):
            cut = slice(q * CHUNK, (q + 1) * CHUNK)
            here = pl.ds(row + q * CHUNK, CHUNK)
            seen = []
            for ch in range(2):
                turned = [
                    pltpu.roll(ext[ch * blocks + block + j, here, :], back, 1)
                    for j in range(pieces + 1)
                ]
                seen.append([jnp.where(keep, turned[j], turned[j + 1]) for j in range(pieces)])
            for j in range(pieces):
                part = slice(j * LANES, (j + 1) * LANES)
                probe_real, probe_imag = probe[0, cut, part], probe[1, cut, part]
                real, imag = seen[0][j], seen[1][j]
                patches[w][0, cut, part], patches[w][1, cut, part] = real, imag
                exit_real = probe_real * real - probe_imag * imag
                exit_imag = probe_real * imag + probe_imag * real
                exits[w][0, cut, part], exits[w][1, cut, part] = exit_real, exit_imag
                put(stacks[w], exit_real, 0, q, j * LANES)
                put(stacks[w], exit_imag, 1, q, j * LANES)

    def project(w, k):
        for q in range(pr // CHUNK):
            cut = slice(q * CHUNK, (q + 1) * CHUNK)
            real, imag = fields[w][cut, 0:pr], fields[w][cut, pr : 2 * pr]
            factor = jnp.sqrt(levels[k, cut, :]) * lax.rsqrt(real * real + imag * imag + 1.0)
            put(stacks[w], real * factor, 0, q, 0)
            put(stacks[w], -(imag * factor), 1, q, 0)

    def finish(w, k, live):
        row, col = place[ROWS + k], place[COLS + k]
        shift, block = col & (LANES - 1), col >> 7
        low = lanes < shift
        zero = jnp.zeros((CHUNK, LANES), F32)
        for q in range(pr // CHUNK):
            cut = slice(q * CHUNK, (q + 1) * CHUNK)
            here = pl.ds(row + q * CHUNK, CHUNK)
            turned = [[], []]
            for j in range(pieces):
                part = slice(j * LANES, (j + 1) * LANES)
                other = slice(pr + j * LANES, pr + (j + 1) * LANES)
                diff_real = fields[w][cut, part] - exits[w][0, cut, part]
                diff_imag = -fields[w][cut, other] - exits[w][1, cut, part]
                real, imag = patches[w][0, cut, part], patches[w][1, cut, part]
                weight = real * real + imag * imag
                if live is not None:
                    diff_real, diff_imag = diff_real * live, diff_imag * live
                    weight = weight * live
                probe_real, probe_imag = probe[0, cut, part], probe[1, cut, part]
                turned[0].append(pltpu.roll(probe_real * diff_real + probe_imag * diff_imag, shift, 1))
                turned[1].append(pltpu.roll(probe_real * diff_imag - probe_imag * diff_real, shift, 1))
                probe_sums[j, 0, cut, :] += real * diff_real + imag * diff_imag
                probe_sums[j, 1, cut, :] += real * diff_imag - imag * diff_real
                probe_sums[j, 2, cut, :] += weight
            for ch in range(2):
                at = ch * blocks + block
                grad[at, here, :] += jnp.where(low, zero, turned[ch][0])
                for j in range(1, pieces):
                    grad[at + j, here, :] += jnp.where(low, turned[ch][j - 1], turned[ch][j])
                grad[at + pieces, here, :] += jnp.where(low, turned[ch][-1], zero)

    def visit(i, carry):
        first = i * WAYS
        slots = [jnp.minimum(first + w, live_slots - 1) for w in range(WAYS)]
        lives = [None] + [jnp.where(first + w < live_slots, 1.0, 0.0) for w in range(1, WAYS)]
        for w in range(WAYS):

            @pl.when(first + w < live_slots)
            def _():
                level_copy(slots[w]).wait()

        start_levels(first + WAYS)

        @pl.when(i == 0)
        def _():
            tables[0].wait()

        for w in range(WAYS):
            load(w, slots[w])
            times_left(w)

        @pl.when(i == 0)
        def _():
            tables[1].wait()

        for w in range(WAYS):
            times_right(w)
        for w in range(WAYS):
            project(w, slots[w])
            times_left(w)
        for w in range(WAYS):
            times_right(w)
        for w in range(WAYS):
            finish(w, slots[w], lives[w])
        return carry

    lax.fori_loop(0, (live_slots + WAYS - 1) // WAYS, visit, 0)
    core = place[0] % 2
    span = pieces // 2
    for j in range(span):
        for ch in range(3):
            at = pl.ds((j * 3 + ch) * pr, pr)
            kept[at, :] = probe_sums[core * span + j, ch]
            sent[at, :] = probe_sums[(1 - core) * span + j, ch]
    for ch in range(2):
        for b in range(own_blocks):
            at, cut = ch * blocks + 1 + b, slice(b * LANES, (b + 1) * LANES)
            middle[ch, :, cut] = grad[at, own, :]
            near_rim[ch, :, cut] = grad[at, near_rows, :]
            far_rim[ch, :, cut] = grad[at, far_rows, :]
        for s in range(sides):
            at = ch * blocks + side_blocks[s]
            side_out[s][ch] = grad[at, own, :]
            near_ends[s][ch] = grad[at, near_rows, :]
            far_ends[s][ch] = grad[at, far_rows, :]


def positions_call(place, tile, near, far_side, side_in, near_corners, far_corners, probe, measured):
    pr = probe.shape[1]
    sides = len(side_in)
    tile_rows, tile_cols = tile.shape[1:]
    ext_rows = tile_rows + 2 * H
    blocks = (tile_cols + 2 * H) // LANES
    left, right = (jnp.asarray(table) for table in dft_tables(pr))
    shape = lambda *dims: jax.ShapeDtypeStruct(dims, F32)
    slots = measured.shape[2]
    rim = shape(2, H, tile_cols)
    middle, near_rim, far_rim, info, *rest = pl.pallas_call(
        functools.partial(positions_kernel, sides),
        out_shape=(
            shape(2, tile_rows, tile_cols),
            rim,
            rim,
            shape(3 * sides + 2, INFO, LANES),
            *[shape(2, tile_rows, LANES)] * sides,
            *[shape(2, H, LANES)] * (2 * sides),
            shape(3 * pr * pr // LANES // 2, LANES),
            shape(3 * pr * pr // LANES // 2, LANES),
        ),
        in_specs=[SMEM, HBM] + [ANY] * (2 + 3 * sides) + [HBM] * 4,
        out_specs=(VMEM,) * (6 + 3 * sides),
        scratch_shapes=[
            pltpu.VMEM((pr // LANES, 3, pr, LANES), F32),
            *[pltpu.VMEM((2 * blocks, ext_rows, LANES), F32)] * 2,
            pltpu.VMEM(left.shape, BF),
            pltpu.VMEM(right.shape, BF),
            pltpu.VMEM((slots, pr, pr), F32),
            pltpu.VMEM(probe.shape, F32),
            pltpu.SemaphoreType.DMA((3,)),
            pltpu.SemaphoreType.DMA((slots,)),
            pltpu.SemaphoreType.DMA((6 * blocks + 3 * sides + 2,)),
            *[pltpu.VMEM((2, pr, pr), F32)] * (2 * WAYS),
            *[pltpu.VMEM((4 * pr, 2 * pr), BF)] * WAYS,
            *[pltpu.VMEM((pr, 4 * pr), BF)] * WAYS,
            *[pltpu.VMEM((pr, 2 * pr), F32)] * WAYS,
        ],
        compiler_params=pltpu.CompilerParams(vmem_limit_bytes=GRANT),
        cost_estimate=pl.CostEstimate(
            flops=slots * 96 * pr * pr * pr, bytes_accessed=16_000_000, transcendentals=slots * 2 * pr * pr
        ),
        name="positions",
    )(place, tile, *far_corners, far_side, *side_in, *near_corners, near, probe, measured, left, right)
    ends = [rest[i * sides : (i + 1) * sides] for i in range(3)]
    return middle, near_rim, far_rim, *ends, *rest[3 * sides :], info


def update_kernel(sides, *refs):
    place, tile, middle, cover, near, far_side = refs[:6]
    side_in, near_ends, far_ends = [refs[6 + i * sides : 6 + (i + 1) * sides] for i in range(3)]
    own_got, other_got, probe, out, new_probe, sums = refs[6 + 3 * sides :]
    tile_rows, tile_cols = tile.shape[1:]
    own_blocks = tile_cols // LANES
    even = place[0] % 2 == 0
    sums[...] = middle[...]
    near_row = pl.multiple_of(jnp.where(even, tile_rows - H, 0), 8)
    far_row = pl.multiple_of(jnp.where(even, 0, tile_rows - H), 8)
    sums[:, pl.ds(near_row, H), :] += near[...]
    sums[:, pl.ds(far_row, H), :] += far_side[...]
    for s in range(sides):
        if sides == 1:
            edge = jnp.where(place[1] == 0, tile_cols - LANES, 0)
        else:
            edge = 0 if s == 0 else tile_cols - LANES
        at = pl.ds(pl.multiple_of(edge, LANES), LANES)
        sums[:, :, at] += side_in[s][...]
        sums[:, pl.ds(near_row, H), at] += near_ends[s][...]
        sums[:, pl.ds(far_row, H), at] += far_ends[s][...]
    rows = own_got.shape[1] - 8
    peak = jnp.maximum(jnp.max(own_got[:, rows:, :], axis=0), jnp.max(other_got[:, rows:, :], axis=0))
    top = MIX_OBJECT * jnp.max(peak, keepdims=True)
    inverse = 1.0 / ((1.0 - MIX_OBJECT) * cover[...] + top)
    for ch in range(2):
        out[ch] = tile[ch] + sums[ch] * inverse

    pr = probe.shape[1]
    pieces = pr // LANES
    both = [ref[:, 0:rows, :].reshape(-1, LANES) for ref in (own_got, other_got)]

    def update(parts):
        flat = [parts[j * len(parts) // pieces] for j in range(pieces)]
        span = flat[0].shape[0] // (pieces // len(parts))
        term = lambda j, ch: flat[j][(j % (pieces // len(parts))) * span + ch * pr :][:pr]
        weights = [term(j, 2) for j in range(pieces)]
        best = functools.reduce(jnp.maximum, weights)
        best = jnp.max(jnp.max(best.reshape(-1, 8, LANES), axis=0), keepdims=True)
        for j in range(pieces):
            cut = slice(j * LANES, (j + 1) * LANES)
            scale = 1.0 / ((1.0 - MIX_PROBE) * weights[j] + MIX_PROBE * best)
            for ch in range(2):
                new_probe[ch, :, cut] = probe[ch, :, cut] + term(j, ch) * scale

    for first in (0, 1):

        @pl.when(place[0] % 2 == first)
        def _():
            update([both[first], both[1 - first]])


def update_call(place, tile, middle, cover, near, far_side, side_in, ends, own, other, probe):
    sides = len(side_in)
    return pl.pallas_call(
        functools.partial(update_kernel, sides),
        out_shape=(jax.ShapeDtypeStruct(tile.shape, F32), jax.ShapeDtypeStruct(probe.shape, F32)),
        in_specs=[SMEM] + [VMEM] * (8 + 3 * sides),
        out_specs=(VMEM, VMEM),
        scratch_shapes=[pltpu.VMEM(tile.shape, F32)],
        compiler_params=pltpu.CompilerParams(vmem_limit_bytes=51 << 20),
        name="update",
    )(place, tile, middle, cover, near, far_side, *side_in, *ends, own, other, probe)


WIDE = ("rest", "core")
CHIPS = ("rest", "narrow")


def swap(x, axis, first):
    size = lax.axis_size(axis)
    pairs = []
    for i in range(first, size - 1, 2):
        pairs += [(i, i + 1), (i + 1, i)]
    return lax.ppermute(x, axis, pairs)


def shifted(x, axis, by):
    size = lax.axis_size(axis)
    return lax.ppermute(x, axis, [(i, i + by) for i in range(size) if 0 <= i + by < size])


def to_sides(pieces):
    if len(pieces) == 1:
        return [swap(pieces[0], "narrow", 0)]
    return [shifted(pieces[1], "narrow", 1), shifted(pieces[0], "narrow", -1)]


def to_corners(bands, first):
    wide, narrow = lax.axis_size(WIDE), lax.axis_size("narrow")
    steps = [0] if len(bands) == 1 else [-1, 1]
    got = []
    for s, step in enumerate(steps):
        pairs = []
        for i in range(first, wide - 1, 2):
            for n in range(narrow):
                m = 1 - n if step == 0 else n - step
                if 0 <= m < narrow:
                    pairs += [(i * narrow + n, (i + 1) * narrow + m), ((i + 1) * narrow + n, i * narrow + m)]
        band = bands[0] if step == 0 else bands[1 - s]
        got.append(lax.ppermute(band, (*WIDE, "narrow"), pairs))
    return got


def chip_exchange(chunks):
    return lax.all_to_all(chunks.reshape(-1, LANES), CHIPS, 0, 0, tiled=True).reshape(chunks.shape)


def after(x, *others):
    return lax.optimization_barrier((x, *others))[0]


def body(tile, probe, measured, rows, cols, counts):
    wide, narrow = lax.axis_index(WIDE), lax.axis_index("narrow")
    sides = 1 if lax.axis_size("narrow") == 2 else 2
    tile_rows, tile_cols = tile.shape[1:]
    even = wide % 2 == 0
    place = jnp.concatenate(
        [jnp.stack([wide, narrow, counts[0, 0]]).astype(jnp.int32), rows.reshape(-1), cols.reshape(-1)]
    )

    far_band, near_band, edges, far_ends, near_ends = pack_call(place, tile, sides)
    far_side = swap(far_band, WIDE, 1)
    far_corners = to_corners(far_ends, 1)
    side_in = to_sides(edges)
    near_corners = to_corners(near_ends, 0)
    near = swap(near_band, "core", 0)

    middle, near_rim, far_rim, side_rims, near_rim_ends, far_rim_ends, kept, sent, got_info = positions_call(
        place, tile, near, far_side, side_in, near_corners, far_corners, probe, measured
    )
    own_info = edges[0][:1, tile_rows:]

    terms = kept + swap(sent, "core", 0)
    near_got = swap(near_rim, "core", 0)
    far_got = swap(far_rim, WIDE, 1)
    side_got = to_sides(side_rims)
    info = jnp.concatenate([own_info, got_info], axis=0)[:, 0, :32].astype(jnp.int32)
    cover, peak = cover_call(place, after(info, terms), probe, tile_rows, tile_cols, sides)
    chips = lax.axis_size(CHIPS)
    got = chip_exchange(terms.reshape(chips, -1, LANES))
    chunk = jnp.sum(got, axis=0)
    rows_each = chunk.shape[0]
    chunk = after(jnp.concatenate([chunk, peak], axis=0), far_got, near_got, *side_got)
    got = chip_exchange(jnp.broadcast_to(chunk, (chips, *chunk.shape)))
    if rows_each % 8:
        peak = jnp.max(got[:, rows_each:], axis=0)
        got = jnp.concatenate([got[:, :rows_each].reshape(-1, LANES), peak], axis=0)[None]

    near_ends_got = to_corners(near_rim_ends, 0)
    far_ends_got = to_corners(far_rim_ends, 1)
    ends_got = near_ends_got + far_ends_got
    other = swap(after(got, *ends_got), "core", 0)
    return update_call(place, tile, middle, cover, near_got, far_got, side_got, ends_got, got, other, probe)


def solution(mesh):
    wide, narrow = mesh.devices.shape
    fine = Mesh(mesh.devices.reshape(wide // 2, 2, narrow), ("rest", "core", "narrow"))
    placed = (
        P(None, WIDE, "narrow"),
        P(),
        P(WIDE, "narrow", None, None, None),
        P(WIDE, "narrow", None),
        P(WIDE, "narrow", None),
        P(WIDE, "narrow"),
    )
    return jax.shard_map(
        body,
        mesh=fine,
        in_specs=placed,
        out_specs=(P(None, WIDE, "narrow"), P()),
        check_vma=False,
    )
```

```python
import functools
import math

import jax
import jax.numpy as jnp
import ml_dtypes
import numpy as np
from jax import lax
from jax.experimental import pallas as pl
from jax.experimental.pallas import tpu as pltpu
from jax.sharding import Mesh, PartitionSpec as P

H = 128
LANES = 128
CHUNK = 16
WAYS = 2
INFO = 8
GRANT = 50176 << 10
BF = jnp.bfloat16
F32 = jnp.float32
MIX_OBJECT = 0.5
MIX_PROBE = 0.5
VMEM = pl.BlockSpec(memory_space=pltpu.VMEM)
SMEM = pl.BlockSpec(memory_space=pltpu.SMEM)
ANY = pl.BlockSpec(memory_space=pl.ANY)
HBM = pl.BlockSpec(memory_space=pltpu.HBM)
COUNT, ROWS, COLS = 2, 3, 11


def rounded_pair(table):
    table = table.astype(np.float32)
    high = table.astype(ml_dtypes.bfloat16)
    low = (table - high.astype(np.float32)).astype(ml_dtypes.bfloat16)
    return high, low


def dft_tables(length):
    index = np.arange(length)
    angle = 2.0 * np.pi * ((index[:, None] * index[None, :]) % length) / length
    cos_high, cos_low = rounded_pair(np.cos(angle) / math.sqrt(length))
    sin_high, sin_low = rounded_pair(-np.sin(angle) / math.sqrt(length))
    left = np.concatenate([cos_high, sin_high, cos_high, sin_high, cos_low, sin_low], axis=1)
    right_high = np.block([[cos_high, sin_high], [-sin_high, cos_high]])
    right_low = np.block([[cos_low, sin_low], [-sin_low, cos_low]])
    right = np.concatenate([right_high, right_high, right_low], axis=0)
    return left, right


def split(x):
    high = x.astype(BF)
    return high, (x - high.astype(F32)).astype(BF)


def side_block(place, side, sides, blocks):
    if sides == 1:
        return jnp.where(place[1] == 0, blocks - 1, 0)
    return 0 if side == 0 else blocks - 1


def side_step(place, side, sides):
    if sides == 1:
        return jnp.where(place[1] == 0, 1, -1)
    return -1 if side == 0 else 1


def cover_kernel(tile_rows, tile_cols, sides, place, info, probe, cover, peak, total, power):
    pr = probe.shape[1]
    pieces = pr // LANES
    for j in range(pieces):
        cut = slice(j * LANES, (j + 1) * LANES)
        power[j] = probe[0, :, cut] * probe[0, :, cut] + probe[1, :, cut] * probe[1, :, cut]
    total[...] = jnp.zeros_like(total)
    lanes = lax.broadcasted_iota(jnp.int32, (CHUNK, LANES), 1)
    even = place[0] % 2 == 0
    steps_down = (0, jnp.where(even, 1, -1), jnp.where(even, -1, 1))
    steps_right = (0,) + tuple(side_step(place, s, sides) for s in range(sides))
    for v in range(3):
        for h in range(1 + sides):
            source = v * (1 + sides) + h
            down, right = steps_down[v], steps_right[h]

            def visit(k, carry):
                row = info[source, k] + pr - H + down * tile_rows
                col = info[source, 8 + k] + pr - H + right * tile_cols
                inside = (row > 0) & (row < pr + tile_rows) & (col > 0) & (col < pr + tile_cols)

                @pl.when(inside)
                def _():
                    shift = col & (LANES - 1)
                    block = col >> 7
                    low = lanes < shift
                    for q in range(pr // CHUNK):
                        turned = [
                            pltpu.roll(power[j, q * CHUNK : (q + 1) * CHUNK, :], shift, 1)
                            for j in range(pieces)
                        ]
                        here = pl.ds(row + q * CHUNK, CHUNK)
                        zero = jnp.zeros((CHUNK, LANES), F32)
                        total[block, here, :] += jnp.where(low, zero, turned[0])
                        for j in range(1, pieces):
                            total[block + j, here, :] += jnp.where(low, turned[j - 1], turned[j])
                        total[block + pieces, here, :] += jnp.where(low, turned[-1], zero)

                return carry

            lax.fori_loop(0, info[source, 16], visit, 0)
    first = pr // LANES
    best = jnp.zeros((8, LANES), F32)
    for b in range(tile_cols // LANES):
        own = total[first + b, pr : pr + tile_rows, :]
        cover[:, b * LANES : (b + 1) * LANES] = own
        best = jnp.maximum(best, jnp.max(own.reshape(tile_rows // 8, 8, LANES), axis=0))
    peak[...] = jnp.full((8, LANES), jnp.max(best), F32)


def cover_call(place, info, probe, tile_rows, tile_cols, sides):
    pr = probe.shape[1]
    blocks = (tile_cols + 2 * pr) // LANES + 1
    return pl.pallas_call(
        functools.partial(cover_kernel, tile_rows, tile_cols, sides),
        out_shape=(
            jax.ShapeDtypeStruct((tile_rows, tile_cols), F32),
            jax.ShapeDtypeStruct((8, LANES), F32),
        ),
        in_specs=[SMEM, SMEM, VMEM],
        out_specs=(VMEM, VMEM),
        scratch_shapes=[
            pltpu.VMEM((blocks, tile_rows + 2 * pr, LANES), F32),
            pltpu.VMEM((pr // LANES, pr, LANES), F32),
        ],
        compiler_params=pltpu.CompilerParams(vmem_limit_bytes=16 << 20),
        cost_estimate=pl.CostEstimate(flops=4_000_000, bytes_accessed=8_000_000, transcendentals=0),
        name="cover",
    )(place, info, probe)


def pack_kernel(sides, place, tile, *refs):
    far_band, near_band = refs[:2]
    edges, far_ends, near_ends = [refs[2 + i * sides : 2 + (i + 1) * sides] for i in range(3)]
    sems = refs[2 + 3 * sides]
    tile_rows, tile_cols = tile.shape[1:]
    even = place[0] % 2 == 0
    near_start = pl.multiple_of(jnp.where(even, tile_rows - H, 0), 8)
    far_start = pl.multiple_of(jnp.where(even, 0, tile_rows - H), 8)
    if sides == 1:
        starts = [pl.multiple_of(jnp.where(place[1] == 0, tile_cols - H, 0), LANES)]
    else:
        starts = [0, tile_cols - H]
    bands = [(far_band, far_start, H, 0), (near_band, near_start, H, 0)]
    for s, start in enumerate(starts):
        bands += [(edges[s], 0, tile_rows, start), (far_ends[s], far_start, H, start)]
        bands += [(near_ends[s], near_start, H, start)]
    copies = []
    for i, (band, row, height, col) in enumerate(bands):
        copies.append(
            pltpu.make_async_copy(
                tile.at[:, pl.ds(row, height), pl.ds(col, band.shape[2])], band.at[:, pl.ds(0, height), :], sems.at[i]
            )
        )
        copies[-1].start()
    lanes = lax.broadcasted_iota(jnp.int32, (INFO, LANES), 1)
    notes = jnp.where(lanes == 16, place[COUNT], 0)
    for k in range(8):
        notes = jnp.where(lanes == k, place[ROWS + k], jnp.where(lanes == 8 + k, place[COLS + k], notes))
    notes = notes.astype(F32)
    for band, row, height, col in bands:
        for ch in range(2):
            band[ch, height : height + INFO, 0:LANES] = notes
            if band.shape[2] > LANES:
                band[ch, height : height + INFO, LANES:] = jnp.zeros((INFO, band.shape[2] - LANES), F32)
    for copy in copies:
        copy.wait()


def pack_call(place, tile, sides):
    tile_rows, tile_cols = tile.shape[1:]
    shape = lambda height, width: jax.ShapeDtypeStruct((2, height + INFO, width), F32)
    shapes = [shape(H, tile_cols)] * 2 + [shape(tile_rows, LANES)] * sides + [shape(H, LANES)] * (2 * sides)
    out = pl.pallas_call(
        functools.partial(pack_kernel, sides),
        out_shape=shapes,
        in_specs=[SMEM, HBM],
        out_specs=[VMEM] * len(shapes),
        scratch_shapes=[pltpu.SemaphoreType.DMA((len(shapes),))],
        compiler_params=pltpu.CompilerParams(vmem_limit_bytes=8 << 20),
        name="pack",
    )(place, tile)
    return out[0], out[1], *[list(out[2 + i * sides : 2 + (i + 1) * sides]) for i in range(3)]


def positions_kernel(sides, *refs):
    place, tile, far_side, near = refs[0], refs[1], refs[2 + sides], refs[3 + 3 * sides]
    far_corners, side_in, near_corners = [
        refs[at : at + sides] for at in (2, 3 + sides, 3 + 2 * sides)
    ]
    probe_in, measured, left_in, right_in = refs[4 + 3 * sides : 8 + 3 * sides]
    middle, near_rim, far_rim, info = refs[8 + 3 * sides : 12 + 3 * sides]
    side_out, near_ends, far_ends = [refs[12 + i * sides : 12 + (i + 1) * sides] for i in range(3, 6)]
    kept, sent, probe_sums, ext, grad = refs[12 + 6 * sides : 17 + 6 * sides]
    scratch = refs[17 + 6 * sides :]
    left, right, levels, probe = scratch[:4]
    table_sems, level_sems, ext_sems = scratch[4:7]
    scratch = scratch[7:]
    patches, exits, stacks, wides, fields = [scratch[i * WAYS : (i + 1) * WAYS] for i in range(5)]

    pr = probe_in.shape[1]
    pieces = pr // LANES
    ext_rows = ext.shape[1]
    blocks = ext.shape[0] // 2
    own_blocks = blocks - 2
    tile_rows, tile_cols = ext_rows - 2 * H, own_blocks * LANES
    even = place[0] % 2 == 0
    near_row = pl.multiple_of(jnp.where(even, tile_rows + H, 0), 8)
    far_row = pl.multiple_of(jnp.where(even, 0, tile_rows + H), 8)
    side_blocks = [side_block(place, s, sides, blocks) for s in range(sides)]
    own, near_rows, far_rows = pl.ds(H, tile_rows), pl.ds(near_row, H), pl.ds(far_row, H)

    copies = []

    def fetch(source, target):
        copies.append(pltpu.make_async_copy(source, target, ext_sems.at[len(copies)]))
        copies[-1].start()

    for ch in range(2):
        for b in range(own_blocks):
            at, cut = ch * blocks + 1 + b, pl.ds(b * LANES, LANES)
            fetch(tile.at[ch, :, cut], ext.at[at, own, :])
            fetch(near.at[ch, pl.ds(0, H), cut], ext.at[at, near_rows, :])
            fetch(far_side.at[ch, pl.ds(0, H), cut], ext.at[at, far_rows, :])
        for s in range(sides):
            at = ch * blocks + side_blocks[s]
            fetch(side_in[s].at[ch, pl.ds(0, tile_rows), :], ext.at[at, own, :])
            fetch(near_corners[s].at[ch, pl.ds(0, H), :], ext.at[at, near_rows, :])
            fetch(far_corners[s].at[ch, pl.ds(0, H), :], ext.at[at, far_rows, :])
    for s in range(sides):
        fetch(side_in[s].at[0, pl.ds(tile_rows, INFO), :], info.at[s])
        fetch(near_corners[s].at[0, pl.ds(H, INFO), :], info.at[sides + 1 + s])
        fetch(far_corners[s].at[0, pl.ds(H, INFO), :], info.at[2 * sides + 2 + s])
    fetch(near.at[0, pl.ds(H, INFO), pl.ds(0, LANES)], info.at[sides])
    fetch(far_side.at[0, pl.ds(H, INFO), pl.ds(0, LANES)], info.at[2 * sides + 1])
    tables = [
        pltpu.make_async_copy(left_in, left, table_sems.at[0]),
        pltpu.make_async_copy(right_in, right, table_sems.at[1]),
        pltpu.make_async_copy(probe_in, probe, table_sems.at[2]),
    ]
    for copy in tables:
        copy.start()

    live_slots = place[COUNT]

    def level_copy(i):
        return pltpu.make_async_copy(measured.at[0, 0, i], levels.at[i], level_sems.at[i])

    def start_levels(first):
        for w in range(WAYS):

            @pl.when(first + w < live_slots)
            def _():
                level_copy(first + w).start()

    start_levels(0)
    if sides == 1:
        for ch in range(2):
            ext[ch * blocks + blocks - 1 - side_blocks[0]] = jnp.zeros((ext_rows, LANES), F32)
    grad[...] = jnp.zeros_like(grad)
    probe_sums[...] = jnp.zeros_like(probe_sums)
    for copy in copies:
        copy.wait()
    tables[2].wait()
    lanes = lax.broadcasted_iota(jnp.int32, (CHUNK, LANES), 1)

    def put(stack, value, part, q, first):
        width = value.shape[1]
        high, low = split(value)
        rows_at = lambda block: slice(block * pr + q * CHUNK, block * pr + (q + 1) * CHUNK)
        here, there = slice(first, first + width), slice(pr + first, pr + first + width)
        if part == 0:
            stack[rows_at(0), here], stack[rows_at(1), there] = high, high
            stack[rows_at(2), here], stack[rows_at(3), there] = low, low
        else:
            stack[rows_at(0), there], stack[rows_at(1), here] = high, -high
            stack[rows_at(2), there], stack[rows_at(3), here] = low, -low

    def times_left(w):
        stack = jnp.concatenate([stacks[w][...], stacks[w][0 : 2 * pr]], axis=0)
        fields[w][...] = jnp.dot(left[...], stack, preferred_element_type=F32)

    def times_right(w):
        for q in range(pr // CHUNK):
            cut = slice(q * CHUNK, (q + 1) * CHUNK)
            high, low = split(fields[w][cut, :])
            wides[w][cut, 0 : 2 * pr] = high
            wides[w][cut, 2 * pr : 4 * pr] = low
        stack = jnp.concatenate([wides[w][...], wides[w][:, 0 : 2 * pr]], axis=1)
        fields[w][...] = jnp.dot(stack, right[...], preferred_element_type=F32)

    def load(w, k):
        row, col = place[ROWS + k], place[COLS + k]
        shift, block = col & (LANES - 1), col >> 7
        back = (LANES - shift) & (LANES - 1)
        keep = lanes < LANES - shift
        for q in range(pr // CHUNK):
            cut = slice(q * CHUNK, (q + 1) * CHUNK)
            here = pl.ds(row + q * CHUNK, CHUNK)
            seen = []
            for ch in range(2):
                turned = [
                    pltpu.roll(ext[ch * blocks + block + j, here, :], back, 1)
                    for j in range(pieces + 1)
                ]
                seen.append([jnp.where(keep, turned[j], turned[j + 1]) for j in range(pieces)])
            for j in range(pieces):
                part = slice(j * LANES, (j + 1) * LANES)
                probe_real, probe_imag = probe[0, cut, part], probe[1, cut, part]
                real, imag = seen[0][j], seen[1][j]
                patches[w][0, cut, part], patches[w][1, cut, part] = real, imag
                exit_real = probe_real * real - probe_imag * imag
                exit_imag = probe_real * imag + probe_imag * real
                exits[w][0, cut, part], exits[w][1, cut, part] = exit_real, exit_imag
                put(stacks[w], exit_real, 0, q, j * LANES)
                put(stacks[w], exit_imag, 1, q, j * LANES)

    def project(w, k):
        for q in range(pr // CHUNK):
            cut = slice(q * CHUNK, (q + 1) * CHUNK)
            real, imag = fields[w][cut, 0:pr], fields[w][cut, pr : 2 * pr]
            factor = jnp.sqrt(levels[k, cut, :]) * lax.rsqrt(real * real + imag * imag + 1.0)
            put(stacks[w], real * factor, 0, q, 0)
            put(stacks[w], -(imag * factor), 1, q, 0)

    def finish(w, k, live):
        row, col = place[ROWS + k], place[COLS + k]
        shift, block = col & (LANES - 1), col >> 7
        low = lanes < shift
        zero = jnp.zeros((CHUNK, LANES), F32)
        for q in range(pr // CHUNK):
            cut = slice(q * CHUNK, (q + 1) * CHUNK)
            here = pl.ds(row + q * CHUNK, CHUNK)
            turned = [[], []]
            for j in range(pieces):
                part = slice(j * LANES, (j + 1) * LANES)
                other = slice(pr + j * LANES, pr + (j + 1) * LANES)
                diff_real = fields[w][cut, part] - exits[w][0, cut, part]
                diff_imag = -fields[w][cut, other] - exits[w][1, cut, part]
                real, imag = patches[w][0, cut, part], patches[w][1, cut, part]
                weight = real * real + imag * imag
                if live is not None:
                    diff_real, diff_imag = diff_real * live, diff_imag * live
                    weight = weight * live
                probe_real, probe_imag = probe[0, cut, part], probe[1, cut, part]
                turned[0].append(pltpu.roll(probe_real * diff_real + probe_imag * diff_imag, shift, 1))
                turned[1].append(pltpu.roll(probe_real * diff_imag - probe_imag * diff_real, shift, 1))
                probe_sums[j, 0, cut, :] += real * diff_real + imag * diff_imag
                probe_sums[j, 1, cut, :] += real * diff_imag - imag * diff_real
                probe_sums[j, 2, cut, :] += weight
            for ch in range(2):
                at = ch * blocks + block
                grad[at, here, :] += jnp.where(low, zero, turned[ch][0])
                for j in range(1, pieces):
                    grad[at + j, here, :] += jnp.where(low, turned[ch][j - 1], turned[ch][j])
                grad[at + pieces, here, :] += jnp.where(low, turned[ch][-1], zero)

    def visit(i, carry):
        first = i * WAYS
        slots = [jnp.minimum(first + w, live_slots - 1) for w in range(WAYS)]
        lives = [None] + [jnp.where(first + w < live_slots, 1.0, 0.0) for w in range(1, WAYS)]
        for w in range(WAYS):

            @pl.when(first + w < live_slots)
            def _():
                level_copy(slots[w]).wait()

        start_levels(first + WAYS)

        @pl.when(i == 0)
        def _():
            tables[0].wait()
            tables[1].wait()

        for w in range(WAYS):
            load(w, slots[w])
            times_left(w)
        for w in range(WAYS):
            times_right(w)
        for w in range(WAYS):
            project(w, slots[w])
            times_left(w)
        for w in range(WAYS):
            times_right(w)
        for w in range(WAYS):
            finish(w, slots[w], lives[w])
        return carry

    lax.fori_loop(0, (live_slots + WAYS - 1) // WAYS, visit, 0)
    core = place[0] % 2
    span = pieces // 2
    for j in range(span):
        for ch in range(3):
            at = pl.ds((j * 3 + ch) * pr, pr)
            kept[at, :] = probe_sums[core * span + j, ch]
            sent[at, :] = probe_sums[(1 - core) * span + j, ch]
    for ch in range(2):
        for b in range(own_blocks):
            at, cut = ch * blocks + 1 + b, slice(b * LANES, (b + 1) * LANES)
            middle[ch, :, cut] = grad[at, own, :]
            near_rim[ch, :, cut] = grad[at, near_rows, :]
            far_rim[ch, :, cut] = grad[at, far_rows, :]
        for s in range(sides):
            at = ch * blocks + side_blocks[s]
            side_out[s][ch] = grad[at, own, :]
            near_ends[s][ch] = grad[at, near_rows, :]
            far_ends[s][ch] = grad[at, far_rows, :]


def positions_call(place, tile, near, far_side, side_in, near_corners, far_corners, probe, measured):
    pr = probe.shape[1]
    sides = len(side_in)
    tile_rows, tile_cols = tile.shape[1:]
    ext_rows = tile_rows + 2 * H
    blocks = (tile_cols + 2 * H) // LANES
    left, right = (jnp.asarray(table) for table in dft_tables(pr))
    shape = lambda *dims: jax.ShapeDtypeStruct(dims, F32)
    slots = measured.shape[2]
    rim = shape(2, H, tile_cols)
    middle, near_rim, far_rim, info, *rest = pl.pallas_call(
        functools.partial(positions_kernel, sides),
        out_shape=(
            shape(2, tile_rows, tile_cols),
            rim,
            rim,
            shape(3 * sides + 2, INFO, LANES),
            *[shape(2, tile_rows, LANES)] * sides,
            *[shape(2, H, LANES)] * (2 * sides),
            shape(3 * pr * pr // LANES // 2, LANES),
            shape(3 * pr * pr // LANES // 2, LANES),
        ),
        in_specs=[SMEM, HBM] + [ANY] * (2 + 3 * sides) + [HBM] * 4,
        out_specs=(VMEM,) * (6 + 3 * sides),
        scratch_shapes=[
            pltpu.VMEM((pr // LANES, 3, pr, LANES), F32),
            *[pltpu.VMEM((2 * blocks, ext_rows, LANES), F32)] * 2,
            pltpu.VMEM(left.shape, BF),
            pltpu.VMEM(right.shape, BF),
            pltpu.VMEM((slots, pr, pr), F32),
            pltpu.VMEM(probe.shape, F32),
            pltpu.SemaphoreType.DMA((3,)),
            pltpu.SemaphoreType.DMA((slots,)),
            pltpu.SemaphoreType.DMA((6 * blocks + 3 * sides + 2,)),
            *[pltpu.VMEM((2, pr, pr), F32)] * (2 * WAYS),
            *[pltpu.VMEM((4 * pr, 2 * pr), BF)] * WAYS,
            *[pltpu.VMEM((pr, 4 * pr), BF)] * WAYS,
            *[pltpu.VMEM((pr, 2 * pr), F32)] * WAYS,
        ],
        compiler_params=pltpu.CompilerParams(vmem_limit_bytes=GRANT),
        cost_estimate=pl.CostEstimate(
            flops=slots * 96 * pr * pr * pr, bytes_accessed=16_000_000, transcendentals=slots * 2 * pr * pr
        ),
        name="positions",
    )(place, tile, *far_corners, far_side, *side_in, *near_corners, near, probe, measured, left, right)
    ends = [rest[i * sides : (i + 1) * sides] for i in range(3)]
    return middle, near_rim, far_rim, *ends, *rest[3 * sides :], info


def update_kernel(sides, *refs):
    place, tile, middle, cover, near, far_side = refs[:6]
    side_in, near_ends, far_ends = [refs[6 + i * sides : 6 + (i + 1) * sides] for i in range(3)]
    own_got, other_got, probe, out, new_probe, sums = refs[6 + 3 * sides :]
    tile_rows, tile_cols = tile.shape[1:]
    own_blocks = tile_cols // LANES
    even = place[0] % 2 == 0
    sums[...] = middle[...]
    near_row = pl.multiple_of(jnp.where(even, tile_rows - H, 0), 8)
    far_row = pl.multiple_of(jnp.where(even, 0, tile_rows - H), 8)
    sums[:, pl.ds(near_row, H), :] += near[...]
    sums[:, pl.ds(far_row, H), :] += far_side[...]
    for s in range(sides):
        if sides == 1:
            edge = jnp.where(place[1] == 0, tile_cols - LANES, 0)
        else:
            edge = 0 if s == 0 else tile_cols - LANES
        at = pl.ds(pl.multiple_of(edge, LANES), LANES)
        sums[:, :, at] += side_in[s][...]
        sums[:, pl.ds(near_row, H), at] += near_ends[s][...]
        sums[:, pl.ds(far_row, H), at] += far_ends[s][...]
    rows = own_got.shape[1] - 8
    peak = jnp.maximum(jnp.max(own_got[:, rows:, :], axis=0), jnp.max(other_got[:, rows:, :], axis=0))
    top = MIX_OBJECT * jnp.max(peak, keepdims=True)
    inverse = 1.0 / ((1.0 - MIX_OBJECT) * cover[...] + top)
    for ch in range(2):
        out[ch] = tile[ch] + sums[ch] * inverse

    pr = probe.shape[1]
    pieces = pr // LANES
    both = [ref[:, 0:rows, :].reshape(-1, LANES) for ref in (own_got, other_got)]

    def update(parts):
        flat = [parts[j * len(parts) // pieces] for j in range(pieces)]
        span = flat[0].shape[0] // (pieces // len(parts))
        term = lambda j, ch: flat[j][(j % (pieces // len(parts))) * span + ch * pr :][:pr]
        weights = [term(j, 2) for j in range(pieces)]
        best = functools.reduce(jnp.maximum, weights)
        best = jnp.max(jnp.max(best.reshape(-1, 8, LANES), axis=0), keepdims=True)
        for j in range(pieces):
            cut = slice(j * LANES, (j + 1) * LANES)
            scale = 1.0 / ((1.0 - MIX_PROBE) * weights[j] + MIX_PROBE * best)
            for ch in range(2):
                new_probe[ch, :, cut] = probe[ch, :, cut] + term(j, ch) * scale

    for first in (0, 1):

        @pl.when(place[0] % 2 == first)
        def _():
            update([both[first], both[1 - first]])


def update_call(place, tile, middle, cover, near, far_side, side_in, ends, own, other, probe):
    sides = len(side_in)
    return pl.pallas_call(
        functools.partial(update_kernel, sides),
        out_shape=(jax.ShapeDtypeStruct(tile.shape, F32), jax.ShapeDtypeStruct(probe.shape, F32)),
        in_specs=[SMEM] + [VMEM] * (8 + 3 * sides),
        out_specs=(VMEM, VMEM),
        scratch_shapes=[pltpu.VMEM(tile.shape, F32)],
        compiler_params=pltpu.CompilerParams(vmem_limit_bytes=51 << 20),
        name="update",
    )(place, tile, middle, cover, near, far_side, *side_in, *ends, own, other, probe)


WIDE = ("rest", "core")
CHIPS = ("rest", "narrow")


def swap(x, axis, first):
    size = lax.axis_size(axis)
    pairs = []
    for i in range(first, size - 1, 2):
        pairs += [(i, i + 1), (i + 1, i)]
    return lax.ppermute(x, axis, pairs)


def shifted(x, axis, by):
    size = lax.axis_size(axis)
    return lax.ppermute(x, axis, [(i, i + by) for i in range(size) if 0 <= i + by < size])


def to_sides(pieces):
    if len(pieces) == 1:
        return [swap(pieces[0], "narrow", 0)]
    return [shifted(pieces[1], "narrow", 1), shifted(pieces[0], "narrow", -1)]


def to_corners(bands, first):
    wide, narrow = lax.axis_size(WIDE), lax.axis_size("narrow")
    steps = [0] if len(bands) == 1 else [-1, 1]
    got = []
    for s, step in enumerate(steps):
        pairs = []
        for i in range(first, wide - 1, 2):
            for n in range(narrow):
                m = 1 - n if step == 0 else n - step
                if 0 <= m < narrow:
                    pairs += [(i * narrow + n, (i + 1) * narrow + m), ((i + 1) * narrow + n, i * narrow + m)]
        band = bands[0] if step == 0 else bands[1 - s]
        got.append(lax.ppermute(band, (*WIDE, "narrow"), pairs))
    return got


def chip_exchange(chunks):
    return lax.all_to_all(chunks.reshape(-1, LANES), CHIPS, 0, 0, tiled=True).reshape(chunks.shape)


def after(x, *others):
    return lax.optimization_barrier((x, *others))[0]


def body(tile, probe, measured, rows, cols, counts):
    wide, narrow = lax.axis_index(WIDE), lax.axis_index("narrow")
    sides = 1 if lax.axis_size("narrow") == 2 else 2
    tile_rows, tile_cols = tile.shape[1:]
    even = wide % 2 == 0
    place = jnp.concatenate(
        [jnp.stack([wide, narrow, counts[0, 0]]).astype(jnp.int32), rows.reshape(-1), cols.reshape(-1)]
    )

    far_band, near_band, edges, far_ends, near_ends = pack_call(place, tile, sides)
    far_side = swap(far_band, WIDE, 1)
    far_corners = to_corners(far_ends, 1)
    side_in = to_sides(edges)
    near_corners = to_corners(near_ends, 0)
    near = swap(near_band, "core", 0)

    middle, near_rim, far_rim, side_rims, near_rim_ends, far_rim_ends, kept, sent, got_info = positions_call(
        place, tile, near, far_side, side_in, near_corners, far_corners, probe, measured
    )
    own_info = edges[0][:1, tile_rows:]

    terms = kept + swap(sent, "core", 0)
    near_got = swap(near_rim, "core", 0)
    far_got = swap(far_rim, WIDE, 1)
    side_got = to_sides(side_rims)
    info = jnp.concatenate([own_info, got_info], axis=0)[:, 0, :32].astype(jnp.int32)
    cover, peak = cover_call(place, after(info, terms), probe, tile_rows, tile_cols, sides)
    chips = lax.axis_size(CHIPS)
    got = chip_exchange(terms.reshape(chips, -1, LANES))
    chunk = jnp.sum(got, axis=0)
    rows_each = chunk.shape[0]
    chunk = after(jnp.concatenate([chunk, peak], axis=0), far_got, near_got, *side_got)
    got = chip_exchange(jnp.broadcast_to(chunk, (chips, *chunk.shape)))
    if rows_each % 8:
        peak = jnp.max(got[:, rows_each:], axis=0)
        got = jnp.concatenate([got[:, :rows_each].reshape(-1, LANES), peak], axis=0)[None]

    near_ends_got = to_corners(near_rim_ends, 0)
    far_ends_got = to_corners(far_rim_ends, 1)
    ends_got = near_ends_got + far_ends_got
    other = swap(after(got, *ends_got), "core", 0)
    return update_call(place, tile, middle, cover, near_got, far_got, side_got, ends_got, got, other, probe)


def solution(mesh):
    wide, narrow = mesh.devices.shape
    fine = Mesh(mesh.devices.reshape(wide // 2, 2, narrow), ("rest", "core", "narrow"))
    placed = (
        P(None, WIDE, "narrow"),
        P(),
        P(WIDE, "narrow", None, None, None),
        P(WIDE, "narrow", None),
        P(WIDE, "narrow", None),
        P(WIDE, "narrow"),
    )
    return jax.shard_map(
        body,
        mesh=fine,
        in_specs=placed,
        out_specs=(P(None, WIDE, "narrow"), P()),
        check_vma=False,
    )
```
